32 devices in a mesh: tok: 16 (over z, x, core), ch: 2 (over y).
Axes of the slice: x: 2, y: 2, z: 4, core: 2. Of those that a mesh axis runs over, the one named last changes fastest.
Arguments:
- tokens: bfloat16 [2, 36864, 320], P(None, ('tok', 'ch')), may hold values from -6 to 6
- grad_output: bfloat16 [2, 36864, 320], P(None, ('tok', 'ch')), may hold values from -6 to 6
- valid_tiles: int32 [2, 64, 9], P(None, ('tok', 'ch')), may hold values 0 or 1
- master_a: float32 [320, 2560], replicated
- master_b: float32 [1280, 640], replicated
- vector_params: float32 [55, 320], replicated
- matrix_first: float32 [32, 51200], P(('tok', 'ch')), may hold values from -29.182657 to 29.182657
- matrix_second: float32 [32, 51200], P(('tok', 'ch')), may hold values from 1.92 to 7.68
- vector_first: float32 [55, 320], replicated, may hold values from -73.826935 to 73.826935
- vector_second: float32 [55, 320], replicated, may hold values from 12.288 to 49.152
- left_a: int32 [4, 320], replicated, may hold values from 0 to 639, as said below
- right_a: int32 [2560], replicated, may hold values from 0 to 5119, as said below
- left_b: int32 [2, 1280], replicated, may hold values from 0 to 2559, as said below
- right_b: int32 [640], replicated, may hold values from 0 to 1279, as said below
- owner_list: int32 [32], replicated, may hold values from 0 to 31, each once
- step_count: int32 [1], replicated, may hold values from 2 to 20
Outputs:
- block_output: bfloat16 [2, 36864, 320], P(None, ('tok', 'ch'))
- input_grad: float32 [2, 36864, 320], P(None, ('tok', 'ch'))
- matrix_grad: float32 [32, 51200], P(('tok', 'ch'))
- matrix_first_new: float32 [32, 51200], P(('tok', 'ch'))
- matrix_second_new: float32 [32, 51200], P(('tok', 'ch'))
- new_master_a: float32 [320, 2560], replicated
- new_master_b: float32 [1280, 640], replicated
- new_copy_a: bfloat16 [320, 2560], replicated
- new_copy_b: bfloat16 [1280, 640], replicated
- vector_grad: float32 [55, 320], replicated
- vector_first_new: float32 [55, 320], replicated
- vector_second_new: float32 [55, 320], replicated
- new_vectors: float32 [55, 320], replicated
The draws below stay inside these ranges and needn't reach their ends.
Inputs may be any that keep to these rules, and one draw needn't show every extreme that they name: `left_a`: each row holds codes 2 p + s, with p running over a permutation of 0 .. 319 and s in 0, 1. `right_a`: codes 2 p + s, s in 0, 1, where the indices p of each matrix's columns form a permutation of that matrix's own columns. `left_b`: each row holds codes 2 p + s, with p running over a permutation of 0 .. 1279 and s in 0, 1. `right_b`: codes 2 p + s, s in 0, 1, where the indices p of each matrix's columns form a permutation of that matrix's own columns.
All inputs are finite; a program needn't handle non-finite values. No bound on the sum of `valid_tiles` on one device may be relied on, other than what follows from the above.
Results may differ from the reference program's by a relative error of at most 0.014.
Values may be sent and summed in bfloat16 or wider, within the bound.
A program may use at most 192 MiB of HBM per device.

```python
import math
import jax
import jax.numpy as jnp
from jax import lax

D = 320
HEADS = 5
HEAD_DIM = 64
HIDDEN_SIZE = 1280
SIDE = 24
TILE = 8
MB = 2
TILES = 9
GRIDS = 64
TOKENS = 36864
BLOCK = 51200
VROWS = 55
DEVICES = 32


def signed_rows(key, row_count, span_size):
    subkeys = jax.random.split(key, row_count + 1)
    orders = jnp.stack([jax.random.permutation(subkeys[number], span_size) for number in range(row_count)])
    sign_bits = jax.random.randint(subkeys[row_count], (row_count, span_size), 0, 2)
    sign_bits = jnp.where(orders == span_size - 1, 1, jnp.where(orders == 0, 0, sign_bits))
    return (orders * 2 + sign_bits).astype(jnp.int32)


def signed_blocks(key, span_sizes):
    subkeys = jax.random.split(key, len(span_sizes) + 1)
    pieces = []
    offset_start = 0
    for number, span_size in enumerate(span_sizes):
        pieces.append(jax.random.permutation(subkeys[number], span_size) + offset_start)
        offset_start = offset_start + span_size
    orders = jnp.concatenate(pieces)
    sign_bits = jax.random.randint(subkeys[len(span_sizes)], orders.shape, 0, 2)
    sign_bits = jnp.where(orders == offset_start - 1, 1, jnp.where(orders == 0, 0, sign_bits))
    return (orders * 2 + sign_bits).astype(jnp.int32)


def draw_left_a(key, part):
    return signed_rows(jax.random.fold_in(key, 11), 4, D)


def draw_right_a(key, part):
    return signed_blocks(jax.random.fold_in(key, 12), (D, 2 * D, D, HIDDEN_SIZE))


def draw_left_b(key, part):
    return signed_rows(jax.random.fold_in(key, 13), 2, HIDDEN_SIZE)


def draw_right_b(key, part):
    return signed_blocks(jax.random.fold_in(key, 14), (D, D))


def draw_master_a(key, part):
    normal_values = jax.random.normal(jax.random.fold_in(key, 21), (D, 4 * D + HIDDEN_SIZE), jnp.float32)
    column = jnp.arange(4 * D + HIDDEN_SIZE)
    scales = jnp.where((column >= 3 * D) & (column < 4 * D), 3.0, 1.0) * D ** (-0.5)
    return normal_values * scales


def draw_master_b(key, part):
    normal_values = jax.random.normal(jax.random.fold_in(key, 22), (HIDDEN_SIZE, 2 * D), jnp.float32)
    column = jnp.arange(2 * D)
    scales = jnp.where(column >= D, 1.5, 1.0) * HIDDEN_SIZE ** (-0.5)
    return normal_values * scales


def draw_vector_params(key, part):
    row_total = 11 + 11 * (HIDDEN_SIZE // D)
    normal_values = jax.random.normal(jax.random.fold_in(key, 23), (row_total, D), jnp.float32)
    row_number = jnp.arange(row_total)[:, None]
    is_gain = (row_number == 0) | (row_number == 5) | (row_number == 8)
    is_tap = row_number >= 11 + 2 * (HIDDEN_SIZE // D)
    return jnp.where(is_gain, 1.0 + 0.15 * normal_values, jnp.where(is_tap, normal_values / 3.0, 0.3 * normal_values))


def place_ends(array, key, smallest, top_value):
    spot = [jax.random.randint(jax.random.fold_in(key, axis), (), 0, length) for axis, length in enumerate(array.shape)]
    main_axis = array.shape.index(max(array.shape))
    next_to = spot[:main_axis] + [(spot[main_axis] + 1) % array.shape[main_axis]] + spot[main_axis + 1:]
    return array.at[tuple(spot)].set(smallest).at[tuple(next_to)].set(top_value)


def steps_of(own_key, shape, cuts, least, top_value):
    def one(axis_at, shards_of):
        steps = jax.random.uniform(jax.random.fold_in(jax.random.fold_in(own_key, 6), axis_at), (shards_of,), jnp.float32, least / len(cuts), top_value / len(cuts))
        return jnp.repeat(jnp.exp(steps), shape[axis_at] // shards_of).reshape((-1,) + (1,) * (len(shape) - axis_at - 1))

    loudness = one(*cuts[0])
    for cut in cuts[1:]:
        loudness = loudness * one(*cut)
    return loudness


def gaussian(own_key, extent, scale, reach, shards=(), held_as=jnp.bfloat16):
    result = scale * jax.random.normal(own_key, extent, jnp.float32)
    if shards:
        result = result * steps_of(own_key, extent, shards, -0.22, 0.18)
    return jnp.clip(result, -reach, reach).astype(held_as)


def setup_inputs(seed: int = 0) -> dict:
    arg_keys = jax.random.split(jax.random.key(seed), 17)
    tokens = gaussian(arg_keys[0], (MB, TOKENS, D), 1.0, 6.0, ((1, 32),))
    grad_output = gaussian(arg_keys[1], (MB, TOKENS, D), 1.0, 6.0, ((1, 32),))
    valid_tiles = place_ends((jax.random.randint(arg_keys[2], (MB, GRIDS, TILES), 0, 8) < 7).astype(jnp.int32), jax.random.fold_in(arg_keys[2], 1), 0, 1)
    master_a = draw_master_a(jax.random.fold_in(arg_keys[16], 71), 0)
    master_b = draw_master_b(jax.random.fold_in(arg_keys[16], 71), 0)
    vector_params = draw_vector_params(jax.random.fold_in(arg_keys[16], 71), 0)
    matrix_first = gaussian(arg_keys[6], (DEVICES, BLOCK), (0.111 * (15 * MB * GRIDS) ** 0.5), 29.182657, ((0, 32),), jnp.float32)
    matrix_second = jnp.clip(jnp.exp(math.log(7.68) - 1.3862944 * jax.random.uniform(arg_keys[7], (DEVICES, BLOCK), jnp.float32) ** steps_of(arg_keys[7], (DEVICES, BLOCK), ((0, 32),), -0.2, 0.2)), 1.92, 7.68)
    vector_first = gaussian(arg_keys[8], (VROWS, D), (0.111 * (96 * MB * GRIDS) ** 0.5), 73.826935, (), jnp.float32)
    vector_second = jnp.clip(jnp.exp(jax.random.uniform(arg_keys[9], (VROWS, D), jnp.float32, math.log(12.288), math.log(49.152))), 12.288, 49.152)
    left_a = draw_left_a(jax.random.fold_in(arg_keys[16], 71), 0)
    right_a = draw_right_a(jax.random.fold_in(arg_keys[16], 71), 0)
    left_b = draw_left_b(jax.random.fold_in(arg_keys[16], 71), 0)
    right_b = draw_right_b(jax.random.fold_in(arg_keys[16], 71), 0)
    owner_list = jax.random.permutation(arg_keys[14], DEVICES).astype(jnp.int32)
    step_count = jax.random.randint(arg_keys[15], (1,), 2, 21).astype(jnp.int32)
    return dict(tokens=tokens, grad_output=grad_output, valid_tiles=valid_tiles, master_a=master_a, master_b=master_b, vector_params=vector_params, matrix_first=matrix_first, matrix_second=matrix_second, vector_first=vector_first, vector_second=vector_second, left_a=left_a, right_a=right_a, left_b=left_b, right_b=right_b, owner_list=owner_list, step_count=step_count)


@jax.custom_vjp
def low(v):
    return lax.optimization_barrier(v.astype(jnp.bfloat16)).astype(jnp.float32)

@jax.custom_vjp
def low_back(v):
    return v

def low_keep(v):
    return (low(v), None)

def low_pass(kept, grad):
    return (grad,)

def back_keep(v):
    return (v, None)

def back_low(kept, grad):
    return (low(grad),)
low.defvjp(low_keep, low_pass)
low_back.defvjp(back_keep, back_low)
beta_one = 0.9
beta_two = 0.999
adam_epsilon = 1e-08
norm_epsilon = 1e-05
matrix_rate = 0.05
vector_rate = 0.2
weight_decay = 0.01

def norm_rows(values, gain_row, shift_row):
    center = values - lax.optimization_barrier(jnp.mean(values, axis=-1, keepdims=True))
    return center * lax.rsqrt(lax.optimization_barrier(jnp.mean(center * center, axis=-1, keepdims=True)) + norm_epsilon) * gain_row + shift_row

def both_round(values):
    return low(low_back(values))

def product(left_side, right_side):
    return jnp.dot(left_side, right_side, precision=lax.Precision.HIGHEST, preferred_element_type=jnp.float32)

def tile_numbers():
    position = jnp.arange(SIDE * SIDE)
    grid_row = position // SIDE
    grid_col = position % SIDE
    per_side = SIDE // TILE
    return (grid_row, grid_col, grid_row // TILE * per_side + grid_col // TILE)

def slot_valid(tile_flags):
    grid_row, grid_col, owner_tile = tile_numbers()
    inside = (grid_row % TILE < TILE - 1) & (grid_col % TILE < TILE - 1)
    per_side = SIDE // TILE
    matches = owner_tile[None, :, None] == jnp.arange(per_side * per_side)[None, None, :]
    covered = lax.optimization_barrier(jnp.sum(jnp.where(matches, tile_flags[:, None, :], 0), axis=-1))
    return jnp.where(inside[None, :], covered, 0).astype(jnp.float32)

def attend_mask():
    grid_row, grid_col, owner_tile = tile_numbers()
    reduced_side = SIDE // 2
    reduced_pos = jnp.arange(reduced_side * reduced_side)
    reduced_tile = reduced_pos // reduced_side // (TILE // 2) * (SIDE // TILE) + reduced_pos % reduced_side // (TILE // 2)
    return owner_tile[:, None] == reduced_tile[None, :]

def invert_order(order_codes):
    return jnp.zeros(order_codes.shape, jnp.int32).at[order_codes].set(jnp.arange(order_codes.shape[0], dtype=jnp.int32))

def rotate_group(matrix, left_codes, right_codes, span_sizes):
    right_sign = (1 - 2 * (right_codes % 2)).astype(jnp.float32)
    columns_moved = jnp.take(matrix, right_codes // 2, axis=1) * right_sign
    pieces = []
    offset_start = 0
    for number, span_size in enumerate(span_sizes):
        left_sign = (1 - 2 * (left_codes[number] % 2)).astype(jnp.float32)
        block_part = jnp.take(columns_moved[:, offset_start:offset_start + span_size], left_codes[number] // 2, axis=0)
        pieces.append(block_part * left_sign[:, None])
        offset_start = offset_start + span_size
    return jnp.concatenate(pieces, axis=1)

def restore_group(rotated, left_codes, right_codes, span_sizes):
    pieces = []
    offset_start = 0
    for number, span_size in enumerate(span_sizes):
        left_sign = (1 - 2 * (left_codes[number] % 2)).astype(jnp.float32)
        block_part = rotated[:, offset_start:offset_start + span_size] * left_sign[:, None]
        pieces.append(jnp.take(block_part, invert_order(left_codes[number] // 2), axis=0))
        offset_start = offset_start + span_size
    right_sign = (1 - 2 * (right_codes % 2)).astype(jnp.float32)
    joined = jnp.concatenate(pieces, axis=1) * right_sign
    return jnp.take(joined, invert_order(right_codes // 2), axis=1)

def forward_grid(group_a, group_b, vectors, grid_tokens, valid_column, attend):
    model_width = grid_tokens.shape[1]
    hidden_width = group_b.shape[0]
    ratio_rows = hidden_width // model_width
    half_side = SIDE // 2
    w_query = group_a[:, :model_width]
    w_keyval = group_a[:, model_width:3 * model_width]
    w_output = group_a[:, 3 * model_width:4 * model_width]
    w_upward = group_a[:, 4 * model_width:]
    w_reduce = group_b[:, :model_width]
    w_downward = group_b[:, model_width:]
    bias_up = vectors[11:11 + ratio_rows].reshape(hidden_width)
    bias_depth = vectors[11 + ratio_rows:11 + 2 * ratio_rows].reshape(hidden_width)
    taps_depth = vectors[11 + 2 * ratio_rows:].reshape(9, hidden_width)
    normed = low(norm_rows(grid_tokens, vectors[0], vectors[1]))
    query = both_round(product(normed, w_query) + vectors[2])
    patches = (normed * valid_column).reshape(half_side, 2, half_side, 2, model_width)
    patches = patches.transpose(0, 2, 1, 3, 4).reshape(half_side * half_side, 4 * model_width)
    reduced = low_back(product(patches, w_reduce) + vectors[4])
    kv_input = low(norm_rows(reduced, vectors[5], vectors[6]))
    keyval = product(kv_input, w_keyval)
    keys_all = both_round(keyval[:, :model_width]).reshape(-1, HEADS, HEAD_DIM)
    values_all = both_round(keyval[:, model_width:] + vectors[3]).reshape(-1, HEADS, HEAD_DIM)
    scores = jnp.einsum('qhd,khd->hqk', query.reshape(-1, HEADS, HEAD_DIM), keys_all, precision=lax.Precision.HIGHEST) * HEAD_DIM ** (-0.5)
    scores = low_back(jnp.where(attend[None], scores, -1000000000.0))
    weights = low(jax.nn.softmax(scores, axis=-1))
    context = jnp.einsum('hqk,khd->qhd', weights, values_all, precision=lax.Precision.HIGHEST)
    context = both_round(context.reshape(-1, model_width))
    attn_out = low_back(product(context, w_output) + vectors[7])
    middle = grid_tokens + valid_column * attn_out
    normed_two = low(norm_rows(middle, vectors[8], vectors[9]))
    upward = low_back(product(normed_two, w_upward) + bias_up)
    padded = jnp.pad((upward * valid_column).reshape(SIDE, SIDE, hidden_width), ((1, 1), (1, 1), (0, 0)))
    mixed_conv = bias_depth
    for offset_row in range(3):
        for offset_col in range(3):
            mixed_conv = mixed_conv + padded[offset_row:offset_row + SIDE, offset_col:offset_col + SIDE] * taps_depth[offset_row * 3 + offset_col]
    hidden_low = low(jax.nn.gelu(mixed_conv, approximate=False)).reshape(SIDE * SIDE, hidden_width)
    branch = low_back(product(hidden_low, w_downward) + vectors[10])
    return middle + valid_column * branch

def reference(tokens, grad_output, valid_tiles, master_a, master_b, vector_params, matrix_first, matrix_second, vector_first, vector_second, left_a, right_a, left_b, right_b, owner_list, step_count):
    group_a = master_a.astype(jnp.bfloat16).astype(jnp.float32)
    group_b = master_b.astype(jnp.bfloat16).astype(jnp.float32)
    attend = attend_mask()
    grid_total = MB * GRIDS
    grid_tokens = tokens.astype(jnp.float32).reshape(grid_total, SIDE * SIDE, D)
    grid_grads = grad_output.astype(jnp.float32).reshape(grid_total, SIDE * SIDE, D)
    grid_valid = slot_valid(valid_tiles.reshape(grid_total, TILES))

    def one_grid(running, items):
        tokens_one, grads_one, valid_one = items

        def forward(first_group, second_group, vectors, inputs_one):
            return forward_grid(first_group, second_group, vectors, inputs_one, valid_one[:, None], attend)
        outputs_one, pullback = jax.vjp(forward, group_a, group_b, vector_params, tokens_one)
        grad_first, grad_second, grad_vec, grad_tokens = pullback(grads_one)
        summed = (running[0] + grad_first, running[1] + grad_second, running[2] + grad_vec)
        return (summed, (outputs_one.astype(jnp.bfloat16), grad_tokens))
    start_sums = (jnp.zeros(group_a.shape, jnp.float32), jnp.zeros(group_b.shape, jnp.float32), jnp.zeros(vector_params.shape, jnp.float32))
    sums_done, rows_done = lax.scan(one_grid, start_sums, (grid_tokens, grid_grads, grid_valid))
    sum_a, sum_b, vector_grad = sums_done
    block_output = rows_done[0].reshape(MB, TOKENS, D)
    input_grad = rows_done[1].reshape(MB, TOKENS, D)
    spans_a = (D, 2 * D, D, HIDDEN_SIZE)
    spans_b = (D, D)
    rotated_a = rotate_group(sum_a, left_a, right_a, spans_a)
    rotated_b = rotate_group(sum_b, left_b, right_b, spans_b)
    flat_values = jnp.concatenate([rotated_a.reshape(-1), rotated_b.reshape(-1)]).reshape(DEVICES, BLOCK)
    matrix_grad = jnp.take(flat_values, owner_list, axis=0)
    steps_done = step_count[0].astype(jnp.float32)
    first_new = beta_one * matrix_first + (1.0 - beta_one) * matrix_grad
    second_new = beta_two * matrix_second + (1.0 - beta_two) * matrix_grad * matrix_grad
    direction = first_new / (1.0 - beta_one ** steps_done) / (jnp.sqrt(second_new / (1.0 - beta_two ** steps_done)) + adam_epsilon)
    ordered = jnp.take(direction, invert_order(owner_list), axis=0).reshape(-1)
    split_point = D * (4 * D + HIDDEN_SIZE)
    step_a = restore_group(ordered[:split_point].reshape(D, 4 * D + HIDDEN_SIZE), left_a, right_a, spans_a)
    step_b = restore_group(ordered[split_point:].reshape(HIDDEN_SIZE, 2 * D), left_b, right_b, spans_b)
    new_master_a = master_a - matrix_rate * (step_a + weight_decay * master_a)
    new_master_b = master_b - matrix_rate * (step_b + weight_decay * master_b)
    vec_first_new = beta_one * vector_first + (1.0 - beta_one) * vector_grad
    vec_second_new = beta_two * vector_second + (1.0 - beta_two) * vector_grad * vector_grad
    vec_direction = vec_first_new / (1.0 - beta_one ** steps_done) / (jnp.sqrt(vec_second_new / (1.0 - beta_two ** steps_done)) + adam_epsilon)
    new_vectors = vector_params - vector_rate * (vec_direction + weight_decay * vector_params)
    return (block_output, input_grad, matrix_grad, first_new, second_new, new_master_a, new_master_b, new_master_a.astype(jnp.bfloat16), new_master_b.astype(jnp.bfloat16), vector_grad, vec_first_new, vec_second_new, new_vectors)
```

```python
import functools

import jax
import jax.numpy as jnp
from jax import lax
from jax.experimental import pallas as pl
from jax.experimental.pallas import tpu as pltpu
from jax.sharding import PartitionSpec as P

HEADS = 5
HEAD_DIM = 64
SIDE = 24
TILE = 8
TILES = 9
SLOTS = 576
KEYS = 144
LANES = 128
KEYS_TILE = 16

beta_one = 0.9
beta_two = 0.999
adam_epsilon = 1e-08
norm_epsilon = 1e-05
matrix_rate = 0.05
vector_rate = 0.2
weight_decay = 0.01

F32 = jnp.float32
BF16 = jnp.bfloat16


def contract(left, right, left_dim, right_dim):
    return lax.dot_general(
        left, right, (((left_dim,), (right_dim,)), ((), ())), preferred_element_type=F32
    )


def normalize(values):
    scale = 1.0 / values.shape[-1]
    center = values - jnp.sum(values, axis=-1, keepdims=True) * scale
    inverse = lax.rsqrt(jnp.sum(center * center, axis=-1, keepdims=True) * scale + norm_epsilon)
    return center * inverse, inverse


def norm_back(upstream, normal, inverse, gain):
    scale = 1.0 / upstream.shape[-1]
    scaled = upstream * gain
    inner = jnp.sum(scaled * normal, axis=-1, keepdims=True) * scale
    mean = jnp.sum(scaled, axis=-1, keepdims=True) * scale
    return inverse * (scaled - mean - normal * inner)


def row_sums(values):
    rows, cols = values.shape
    return jnp.sum(values.reshape(rows // 8, 8, cols), axis=0)


def group_all(values, op):
    lane = lax.broadcasted_iota(jnp.int32, values.shape, 1)
    for step in (1, 2, 4, 8):
        low = pltpu.roll(values, step, 1)
        high = pltpu.roll(values, LANES - step, 1)
        values = op(values, jnp.where((lane & step) != 0, low, high))
    return values


def split_tiles(rows):
    shaped = rows.reshape(TILE, 3, TILE, rows.shape[1])
    return [shaped[:, c].reshape(TILE * TILE, rows.shape[1]) for c in range(3)]


def join_tiles(tiles):
    return jnp.concatenate(
        [tiles[c][i * TILE : (i + 1) * TILE] for i in range(TILE) for c in range(3)], axis=0
    )


def gelu_parts(e):
    gauss = jnp.exp(-0.5 * e * e)
    size = jnp.abs(e)
    t = 1.0 / (1.0 + (0.3275911 * 0.7071067811865476) * size)
    poly = t * (
        0.5 * 0.254829592
        + t
        * (
            0.5 * -0.284496736
            + t * (0.5 * 1.421413741 + t * (0.5 * -1.453152027 + t * (0.5 * 1.061405429)))
        )
    )
    tail = poly * gauss
    phi = jnp.where(e >= 0.0, 1.0 - tail, tail)
    return phi, gauss * 0.3989422804014327


def block_kernel(
    flags,
    x_ref,
    dy_ref,
    wq,
    wk,
    wv,
    wo,
    wup,
    wr,
    wdn,
    vec,
    wide,
    pick,
    hmask,
    out_ref,
    gin_ref,
    gq,
    gk,
    gv,
    go,
    gup,
    gr,
    gdn,
    gsm,
    gwd,
    msk,
    xs,
    n1s,
    r1s,
    h1s,
    hms,
    qs,
    pats,
    kin,
    nks,
    rks,
    ks,
    vs,
    ps,
    ctxs,
    tmp,
    m1s,
    n2s,
    r2s,
    h2s,
    us,
    dhs,
    hids,
    dus,
    dms,
    das,
    dcs,
    dqs,
    dks,
    dvs,
    dps,
):
    g = pl.program_id(0)
    width = x_ref.shape[2]
    hidden = wup.shape[1]

    @pl.when(g == 0)
    def _():
        for ref in (gq, gk, gv, go, gup, gr, gdn, gsm, gwd):
            ref[...] = jnp.zeros(ref.shape, F32)

    row = lax.broadcasted_iota(jnp.int32, (TILE * TILE, width), 0)
    inside = jnp.where((row % TILE < TILE - 1) & (row < TILE * (TILE - 1)), 1.0, 0.0)
    for t in range(TILES):
        msk[t * 64 : (t + 1) * 64, :] = inside * flags[g, t].astype(F32)

    def vrow(number):
        return vec[number : number + 1, :]

    def add_small(number, sums):
        gsm[number : number + 1, :] += jnp.sum(sums, axis=0, keepdims=True)

    zero_rows = jnp.zeros((8, width), F32)

    def first_norm(big, carry):
        base = pl.multiple_of(big * 192, 64)
        tiles = split_tiles(x_ref[0, pl.ds(base, 192), :].astype(F32))
        grads = split_tiles(dy_ref[0, pl.ds(base, 192), :].astype(F32))
        for c in range(3):
            rows = pl.ds(base + c * 64, 64)
            normal, inverse = normalize(tiles[c])
            xs[rows, :] = tiles[c]
            n1s[rows, :] = normal
            r1s[rows, :] = inverse
            low = (normal * vrow(0) + vrow(1)).astype(BF16)
            h1s[rows, :] = low
            mask = msk[rows, :]
            hms[rows, :] = (low.astype(F32) * mask).astype(BF16)
            dms[rows, :] = (grads[c] * mask).astype(BF16)
        return carry

    lax.fori_loop(0, 3, first_norm, 0)
    qs[...] = (jnp.dot(h1s[...], wq[...], preferred_element_type=F32) + vrow(2)).astype(BF16)
    pats[...] = jnp.dot(pick[...], hms[...], preferred_element_type=F32).astype(BF16)
    reduced = vrow(4)
    for d in range(4):
        reduced = reduced + jnp.dot(
            pats[d * KEYS : (d + 1) * KEYS, :],
            wr[d * width : (d + 1) * width, :],
            preferred_element_type=F32,
        )
    normal, inverse = normalize(reduced)
    nks[...] = normal
    rks[...] = inverse
    kin[...] = (normal * vrow(5) + vrow(6)).astype(BF16)
    ks[...] = jnp.dot(kin[...], wk[...], preferred_element_type=F32).astype(BF16)
    vs[...] = (jnp.dot(kin[...], wv[...], preferred_element_type=F32) + vrow(3)).astype(BF16)
    score_scale = HEAD_DIM ** (-0.5)

    def spread(ref, t):
        part = ref[pl.ds(pl.multiple_of(t * KEYS_TILE, KEYS_TILE), KEYS_TILE), :]
        return jnp.concatenate([part] * 8, axis=0) * hmask[...]

    def gather_heads(big):
        big = big * hmask[...].astype(F32)
        total = big[0:KEYS_TILE]
        for h in range(1, HEADS):
            total = total + big[h * KEYS_TILE : (h + 1) * KEYS_TILE]
        return total

    def attend_tile(t, carry):
        rows = pl.ds(pl.multiple_of(t * 64, 64), 64)
        scores = contract(qs[rows, :], spread(ks, t), 1, 1) * score_scale
        exped = jnp.exp(scores - group_all(scores, jnp.maximum))
        probs = exped / group_all(exped, jnp.add)
        ps[rows, :] = probs
        ctxs[rows, :] = jnp.dot(
            probs.astype(BF16), spread(vs, t), preferred_element_type=F32
        ).astype(BF16)
        return carry

    lax.fori_loop(0, TILES, attend_tile, 0)
    tmp[...] = jnp.dot(ctxs[...], wo[...], preferred_element_type=F32)

    def second_norm(t, carry):
        rows = pl.ds(pl.multiple_of(t * 64, 64), 64)
        middle = xs[rows, :] + msk[rows, :] * (tmp[rows, :] + vrow(7))
        m1s[rows, :] = middle
        normal, inverse = normalize(middle)
        n2s[rows, :] = normal
        r2s[rows, :] = inverse
        h2s[rows, :] = (normal * vrow(8) + vrow(9)).astype(BF16)
        return carry

    lax.fori_loop(0, TILES, second_norm, 0)
    for c in range(hidden // 256):
        cols = slice(c * 256, (c + 1) * 256)
        us[:, cols] = jnp.dot(h2s[...], wup[:, cols], preferred_element_type=F32)
        dhs[:, cols] = contract(dms[...], wdn[cols, :], 1, 1)

    def mix_lanes(lane, carry):
        cols = pl.ds(pl.multiple_of(lane * LANES, LANES), LANES)
        bias_up = wide[0:1, cols]
        bias_dw = wide[1:2, cols]
        taps = [wide[2 + k : 3 + k, cols] for k in range(9)]

        def mix_tile(t, sums):
            sums = list(sums)
            rows = pl.ds(pl.multiple_of(t * 64, 64), 64)
            mask = msk[rows, 0:LANES]
            ups = (us[rows, cols] + bias_up) * mask
            mid = [ups[i * 8 : (i + 1) * 8] for i in range(7)]
            shifted = [
                [pltpu.roll(v, 1, 0) for v in mid],
                mid,
                [pltpu.roll(v, 7, 0) for v in mid],
            ]
            grads = dhs[rows, cols]
            hid_rows = []
            de_rows = []
            for i in range(7):
                e = bias_dw
                for a in range(3):
                    if 0 <= i + a - 1 < 7:
                        for b in range(3):
                            e = e + taps[3 * a + b] * shifted[b][i + a - 1]
                phi, gauss = gelu_parts(e)
                hid_rows.append(e * phi)
                de = grads[i * 8 : (i + 1) * 8] * (phi + e * gauss)
                de_rows.append(de)
                sums[1] = sums[1] + de
                for a in range(3):
                    if 0 <= i + a - 1 < 7:
                        for b in range(3):
                            k = 2 + 3 * a + b
                            sums[k] = sums[k] + de * shifted[b][i + a - 1]
            zero = jnp.zeros((8, LANES), F32)
            hids[rows, cols] = jnp.concatenate(hid_rows + [zero], axis=0).astype(BF16)
            back = [
                [pltpu.roll(v, 7, 0) for v in de_rows],
                de_rows,
                [pltpu.roll(v, 1, 0) for v in de_rows],
            ]
            du_rows = []
            for i in range(7):
                du = None
                for a in range(3):
                    if 0 <= i - a + 1 < 7:
                        for b in range(3):
                            term = taps[3 * a + b] * back[b][i - a + 1]
                            du = term if du is None else du + term
                du_rows.append(du * mask[i * 8 : (i + 1) * 8])
            du_low = jnp.concatenate(du_rows + [zero], axis=0).astype(BF16)
            dus[rows, cols] = du_low
            sums[0] = sums[0] + row_sums(du_low.astype(F32))
            return tuple(sums)

        zero = jnp.zeros((8, LANES), F32)
        sums = lax.fori_loop(0, TILES, mix_tile, (zero,) * 11)
        for k in range(11):
            gwd[k : k + 1, cols] += jnp.sum(sums[k], axis=0, keepdims=True)
        return carry

    lax.fori_loop(0, hidden // LANES, mix_lanes, 0)
    tmp[...] = jnp.dot(hids[...], wdn[...], preferred_element_type=F32)
    gdn[...] += contract(dms[...], hids[...], 0, 0)
    gup[...] += contract(h2s[...], dus[...], 0, 0)
    xs[...] = contract(dus[...], wup[...], 1, 1)

    def middle_rows(big, sums):
        sums = list(sums)
        base = pl.multiple_of(big * 192, 64)
        grads = split_tiles(dy_ref[0, pl.ds(base, 192), :].astype(F32))
        outs = []
        for c in range(3):
            rows = pl.ds(base + c * 64, 64)
            mask = msk[rows, :]
            outs.append(m1s[rows, :] + mask * (tmp[rows, :] + vrow(10)))
            dout = xs[rows, :]
            normal = n2s[rows, :]
            dmid = grads[c] + norm_back(dout, normal, r2s[rows, :], vrow(8))
            m1s[rows, :] = dmid
            low = (dmid * mask).astype(BF16)
            das[rows, :] = low
            sums[0] = sums[0] + row_sums(dout * normal)
            sums[1] = sums[1] + row_sums(dout)
            sums[2] = sums[2] + row_sums(low.astype(F32))
            sums[3] = sums[3] + row_sums(dms[rows, :].astype(F32))
        out_ref[0, pl.ds(base, 192), :] = join_tiles(outs).astype(BF16)
        return tuple(sums)

    sums = lax.fori_loop(0, 3, middle_rows, (zero_rows,) * 4)
    add_small(8, sums[0])
    add_small(9, sums[1])
    add_small(7, sums[2])
    add_small(10, sums[3])
    go[...] += contract(ctxs[...], das[...], 0, 0)
    dcs[...] = contract(das[...], wo[...], 1, 1).astype(BF16)

    def attend_back(t, sums):
        rows = pl.ds(pl.multiple_of(t * 64, 64), 64)
        keys = pl.ds(pl.multiple_of(t * KEYS_TILE, KEYS_TILE), KEYS_TILE)
        probs = ps[rows, :]
        upper = dcs[rows, :]
        dprobs = contract(upper, spread(vs, t), 1, 1)
        inner = group_all(dprobs * probs, jnp.add)
        dz = (probs * (dprobs - inner)).astype(BF16)
        dq = (
            jnp.dot(dz, spread(ks, t), preferred_element_type=F32) * score_scale
        ).astype(BF16)
        dqs[rows, :] = dq
        dk = gather_heads(contract(dz, qs[rows, :], 0, 0)) * score_scale
        dks[keys, :] = dk.astype(BF16)
        dv = gather_heads(contract(probs.astype(BF16), upper, 0, 0)).astype(BF16)
        dvs[keys, :] = dv
        return (sums[0] + row_sums(dq.astype(F32)), sums[1] + row_sums(dv.astype(F32)))

    sums = lax.fori_loop(0, TILES, attend_back, (zero_rows,) * 2)
    add_small(2, sums[0])
    add_small(3, sums[1])
    gq[...] += contract(h1s[...], dqs[...], 0, 0)
    gk[...] += contract(kin[...], dks[...], 0, 0)
    gv[...] += contract(kin[...], dvs[...], 0, 0)
    dout = contract(dks[...], wk[...], 1, 1) + contract(dvs[...], wv[...], 1, 1)
    normal = nks[...]
    ds = norm_back(dout, normal, rks[...], vrow(5)).astype(BF16)
    add_small(5, row_sums(dout * normal))
    add_small(6, row_sums(dout))
    add_small(4, row_sums(ds.astype(F32)))
    for d in range(4):
        rows = slice(d * KEYS, (d + 1) * KEYS)
        wide_rows = slice(d * width, (d + 1) * width)
        gr[wide_rows, :] += contract(pats[rows, :], ds, 0, 0)
        dps[rows, :] = contract(ds, wr[wide_rows, :], 1, 1).astype(BF16)
    tmp[...] = contract(pick[...], dps[...], 0, 0)
    xs[...] = contract(dqs[...], wq[...], 1, 1)

    def last_rows(big, sums):
        sums = list(sums)
        base = pl.multiple_of(big * 192, 64)
        outs = []
        for c in range(3):
            rows = pl.ds(base + c * 64, 64)
            dout = xs[rows, :] + msk[rows, :] * tmp[rows, :]
            normal = n1s[rows, :]
            outs.append(m1s[rows, :] + norm_back(dout, normal, r1s[rows, :], vrow(0)))
            sums[0] = sums[0] + row_sums(dout * normal)
            sums[1] = sums[1] + row_sums(dout)
        gin_ref[0, pl.ds(base, 192), :] = join_tiles(outs)
        return tuple(sums)

    sums = lax.fori_loop(0, 3, last_rows, (zero_rows,) * 2)
    add_small(0, sums[0])
    add_small(1, sums[1])


def pick_matrix():
    spot = jnp.arange(SLOTS)
    part = spot // KEYS
    key = spot % KEYS
    tile = key // KEYS_TILE
    inner = key % KEYS_TILE
    slot = tile * 64 + (2 * (inner // 4) + part // 2) * TILE + 2 * (inner % 4) + part % 2
    return (slot[:, None] == spot[None, :]).astype(BF16)


def head_mask(width):
    row = jnp.arange(8 * KEYS_TILE) // KEYS_TILE
    col = jnp.arange(width) // HEAD_DIM
    return (row[:, None] == col[None, :]).astype(BF16)


def run_block(tokens, grad_output, valid_tiles, master_a, master_b, vector_params):
    width = tokens.shape[2]
    hidden = master_b.shape[0]
    grids = tokens.shape[0] * tokens.shape[1] // SLOTS
    x = tokens.reshape(grids, SLOTS, width)
    dy = grad_output.reshape(grids, SLOTS, width)
    flags = valid_tiles.reshape(grids, TILES)
    low_a = master_a.astype(BF16)
    low_b = master_b.astype(BF16)
    weights = (
        low_a[:, :width],
        low_a[:, width : 2 * width],
        low_a[:, 2 * width : 3 * width],
        low_a[:, 3 * width : 4 * width],
        low_a[:, 4 * width :],
        low_b[:, :width],
        low_b[:, width:],
    )
    wide = vector_params[11:].reshape(11, hidden)
    consts = weights + (vector_params[:11], wide, pick_matrix(), head_mask(width))
    grid_spec = pl.BlockSpec((1, SLOTS, width), lambda g: (g, 0, 0))

    def whole(shape):
        return pl.BlockSpec(shape, lambda g: (0,) * len(shape), pipeline_mode=pl.Buffered(1))

    grad_shapes = [(width, width)] * 4 + [
        (width, hidden),
        (hidden, width),
        (width, hidden),
        (16, width),
        (16, hidden),
    ]
    tall = (SLOTS, width)
    keys = (KEYS, width)
    scratch = [
        (tall, F32),
        (tall, F32),
        (tall, F32),
        ((SLOTS, 1), F32),
        (tall, BF16),
        (tall, BF16),
        (tall, BF16),
        (tall, BF16),
        (keys, BF16),
        (keys, F32),
        ((KEYS, 1), F32),
        (keys, BF16),
        (keys, BF16),
        ((SLOTS, LANES), F32),
        (tall, BF16),
        (tall, F32),
        (tall, F32),
        (tall, F32),
        ((SLOTS, 1), F32),
        (tall, BF16),
        ((SLOTS, hidden), F32),
        ((SLOTS, hidden), F32),
        ((SLOTS, hidden), BF16),
        ((SLOTS, hidden), BF16),
        (tall, BF16),
        (tall, BF16),
        (tall, BF16),
        (tall, BF16),
        (keys, BF16),
        (keys, BF16),
        (tall, BF16),
    ]
    return pl.pallas_call(
        block_kernel,
        name="block_step",
        grid=(grids,),
        in_specs=[pl.BlockSpec(memory_space=pltpu.SMEM), grid_spec, grid_spec]
        + [whole(c.shape) for c in consts],
        out_specs=[grid_spec, grid_spec] + [whole(s) for s in grad_shapes],
        out_shape=[
            jax.ShapeDtypeStruct((grids, SLOTS, width), BF16),
            jax.ShapeDtypeStruct((grids, SLOTS, width), F32),
        ]
        + [jax.ShapeDtypeStruct(s, F32) for s in grad_shapes],
        scratch_shapes=[pltpu.VMEM(s, d) for s, d in scratch],
        compiler_params=pltpu.CompilerParams(vmem_limit_bytes=60 << 20),
    )(flags, x, dy, *consts)

SPANS_A = ((0, 1), (1, 2), (3, 1), (4, 4))
VECTOR_ROWS = 143
EXTRA = 16


def fill_codes(la, ra, lb, rb, codes, width):
    hidden = lb.shape[1]
    codes[...] = jnp.full(codes.shape, -2, jnp.int32)
    codes[0:4, 0:width] = la[...]
    codes[4:6, 0:hidden] = lb[...]
    for k, (first, count) in enumerate(SPANS_A):
        start = first * width
        span = count * width
        codes[6 + k : 7 + k, 0:span] = ra[:, start : start + span] - 2 * start
    for k in range(2):
        codes[10 + k : 11 + k, 0:width] = rb[:, k * width : (k + 1) * width] - 2 * k * width


def lane_matrix(codes, k, size):
    code = codes[k : k + 1, 0:size]
    sign = (1 - 2 * (code & 1)).astype(F32)
    spot = lax.broadcasted_iota(jnp.int32, (size, size), 0)
    return jnp.where(spot == (code >> 1), sign, 0.0).astype(BF16)


def row_matrix(codes, k, out, size):
    for start in range(0, size, LANES):
        code = codes[k : k + 1, start : start + LANES]
        spot = jnp.transpose(jnp.broadcast_to((code >> 1).astype(F32), (LANES, LANES)))
        sign = jnp.transpose(
            jnp.broadcast_to((1 - 2 * (code & 1)).astype(F32), (LANES, LANES))
        )
        for col in range(0, size, LANES):
            lane = lax.broadcasted_iota(jnp.int32, (LANES, LANES), 1).astype(F32) + col
            part = jnp.where(spot == lane, sign, 0.0).astype(BF16)
            out[start : start + LANES, col : col + LANES] = part


def vector_spots(width, hidden):
    spots = []
    for k in range(11):
        for col in range(0, width, LANES):
            spots.append((0, k, col, min(LANES, width - col)))
    for k in range(11):
        for col in range(0, hidden, LANES):
            spots.append((1, k, col, LANES))
    return spots


def rotate_kernel(
    gq, gk, gv, go, gup, gr, gdn, gsm, gwd, la, ra, lb, rb, flat_ref, vec_ref,
    codes, rows_m, ras, rbs, flat, per_block,
):
    width, hidden = gup.shape
    fill_codes(la, ra, lb, rb, codes, width)

    def dot(left, right):
        return jnp.dot(left, right, preferred_element_type=F32)

    for k, parts in enumerate(((gq,), (gk, gv), (go,), (gup,))):
        first, count = SPANS_A[k]
        right = lane_matrix(codes, 6 + k, count * width)
        total = None
        depth = right.shape[0] // len(parts)
        for p, part in enumerate(parts):
            piece = dot(part[...].astype(BF16), right[p * depth : (p + 1) * depth])
            total = piece if total is None else total + piece
        row_matrix(codes, k, rows_m, width)
        ras[:, first * width : (first + count) * width] = dot(rows_m[0:width, 0:width], total.astype(BF16))
    row_matrix(codes, 4, rows_m, hidden)
    part = dot(rows_m[...], gr[...].astype(BF16)).astype(BF16)
    rbs[:, 0:width] = dot(part, lane_matrix(codes, 10, width))
    row_matrix(codes, 5, rows_m, hidden)
    part = contract(rows_m[...], gdn[...].astype(BF16), 1, 1).astype(BF16)
    rbs[:, width : 2 * width] = dot(part, lane_matrix(codes, 11, width))
    per_row = ras.shape[1] // LANES
    for j in range(per_row):
        flat[pl.ds(j, width, stride=per_row), :] = ras[:, j * LANES : (j + 1) * LANES]
    base = width * per_row
    per_row = rbs.shape[1] // LANES
    for j in range(per_row):
        flat[pl.ds(base + j, hidden, stride=per_row), :] = rbs[:, j * LANES : (j + 1) * LANES]
    flat_ref[...] = flat[...].astype(BF16)
    vec_ref[...] = jnp.zeros(vec_ref.shape, BF16)
    for number, (kind, k, col, size) in enumerate(vector_spots(width, hidden)):
        block, row = number // per_block, number % per_block
        source = (gsm, gwd)[kind]
        vec_ref[block, row : row + 1, 0:size] = source[k : k + 1, col : col + size].astype(BF16)


def restore_kernel(
    blocks, vecs, order, la, ra, lb, rb, steps, ma, mb, vp, vf, vsec,
    na, nb, ca, cb, vg, vfn, vsn, nv,
    codes, rows_m, das, dbs, flat, wide_s, per_block,
):
    width = ma.shape[0]
    hidden = mb.shape[0]
    fill_codes(la, ra, lb, rb, codes, width)
    count, depth, _ = blocks.shape
    if depth % 8 == 0:
        for t in range(count):
            spot = pl.multiple_of(order[t] * depth, 8)
            flat[pl.ds(spot, depth), :] = blocks[t].astype(F32)
    else:
        for t in range(count):
            flat[t * depth : (t + 1) * depth, :] = blocks[t].astype(F32)
    per_row = ma.shape[1] // LANES
    for j in range(per_row):
        das[:, j * LANES : (j + 1) * LANES] = flat[pl.ds(j, width, stride=per_row), :]
    base = width * per_row
    per_row = mb.shape[1] // LANES
    for j in range(per_row):
        dbs[:, j * LANES : (j + 1) * LANES] = flat[pl.ds(base + j, hidden, stride=per_row), :]

    def dot(left, right):
        return jnp.dot(left, right, preferred_element_type=F32)

    def update(master, step, new, copy, cols):
        old = master[:, cols]
        value = old - matrix_rate * (step + weight_decay * old)
        new[:, cols] = value
        copy[:, cols] = value.astype(BF16)

    for k, (first, span) in enumerate(SPANS_A):
        size = span * width
        cols = slice(first * width, first * width + size)
        part = dot(lane_matrix(codes, k, width), das[:, cols].astype(BF16)).astype(BF16)
        row_matrix(codes, 6 + k, rows_m, size)
        update(ma, dot(part, rows_m[0:size, 0:size]), na, ca, cols)
    for k in range(2):
        cols = slice(k * width, (k + 1) * width)
        part = dot(lane_matrix(codes, 4 + k, hidden), dbs[:, cols].astype(BF16)).astype(BF16)
        row_matrix(codes, 10 + k, rows_m, width)
        update(mb, dot(part, rows_m[0:width, 0:width]), nb, cb, cols)
    for number, (kind, k, col, size) in enumerate(vector_spots(width, hidden)):
        block, row = number // per_block, number % per_block
        value = vecs[block, row : row + 1, 0:size].astype(F32)
        if kind == 0:
            vg[k : k + 1, col : col + size] = value
        else:
            wide_s[k : k + 1, col : col + size] = value
    ratio = hidden // width
    for k in range(11):
        for q in range(ratio):
            row = 11 + ratio * k + q
            vg[row : row + 1, :] = wide_s[k : k + 1, q * width : (q + 1) * width]
    grad = vg[...]
    first_new = beta_one * vf[...] + (1.0 - beta_one) * grad
    second_new = beta_two * vsec[...] + (1.0 - beta_two) * grad * grad
    vfn[...] = first_new
    vsn[...] = second_new
    move = direction_of(first_new, second_new, steps[0])
    old = vp[...]
    nv[...] = old - vector_rate * (move + weight_decay * old)


def direction_of(first_new, second_new, steps):
    count = jnp.full((1, LANES), steps, jnp.int32).astype(F32)
    log_one = -0.10536051565782628
    log_two = -0.0010005003335835335
    one = (1.0 / (1.0 - jnp.exp(count * log_one)))[:, 0:1]
    two = (1.0 / (1.0 - jnp.exp(count * log_two)))[:, 0:1]
    return first_new * one / (jnp.sqrt(second_new * two) + adam_epsilon)


def vmem_spec():
    return pl.BlockSpec(memory_space=pltpu.VMEM)


def rotate_blocks(grads, la, ra, lb, rb, blocks):
    width, hidden = grads[4].shape
    per_block = -(-VECTOR_ROWS // blocks)
    total = (width * 8 * width + hidden * 2 * width) // LANES
    return pl.pallas_call(
        functools.partial(rotate_kernel, per_block=per_block),
        name="rotate",
        in_specs=[vmem_spec()] * 13,
        out_specs=[vmem_spec()] * 2,
        out_shape=[
            jax.ShapeDtypeStruct((total, LANES), BF16),
            jax.ShapeDtypeStruct((blocks, EXTRA, LANES), BF16),
        ],
        scratch_shapes=[
            pltpu.VMEM((16, hidden), jnp.int32),
            pltpu.VMEM((hidden, hidden), BF16),
            pltpu.VMEM((width, 8 * width), F32),
            pltpu.VMEM((hidden, 2 * width), F32),
            pltpu.VMEM((total, LANES), F32),
        ],
        compiler_params=pltpu.CompilerParams(vmem_limit_bytes=60 << 20),
    )(*grads, la, ra.reshape(1, -1), lb, rb.reshape(1, -1))


def restore_blocks(blocks, vecs, order, la, ra, lb, rb, steps, ma, mb, vp, vf, vsec):
    width = ma.shape[0]
    hidden = mb.shape[0]
    per_block = -(-VECTOR_ROWS // blocks.shape[0])
    total = blocks.shape[0] * blocks.shape[1]
    smem = pl.BlockSpec(memory_space=pltpu.SMEM)
    return pl.pallas_call(
        functools.partial(restore_kernel, per_block=per_block),
        name="restore",
        in_specs=[vmem_spec()] * 2 + [smem] + [vmem_spec()] * 4 + [smem] + [vmem_spec()] * 5,
        out_specs=[vmem_spec()] * 8,
        out_shape=[
            jax.ShapeDtypeStruct(ma.shape, F32),
            jax.ShapeDtypeStruct(mb.shape, F32),
            jax.ShapeDtypeStruct(ma.shape, BF16),
            jax.ShapeDtypeStruct(mb.shape, BF16),
        ]
        + [jax.ShapeDtypeStruct(vp.shape, F32)] * 4,
        scratch_shapes=[
            pltpu.VMEM((16, hidden), jnp.int32),
            pltpu.VMEM((hidden, hidden), BF16),
            pltpu.VMEM((width, 8 * width), F32),
            pltpu.VMEM((hidden, 2 * width), F32),
            pltpu.VMEM((total, LANES), F32),
            pltpu.VMEM((16, hidden), F32),
        ],
        compiler_params=pltpu.CompilerParams(vmem_limit_bytes=60 << 20),
    )(blocks, vecs, order, la, ra.reshape(1, -1), lb, rb.reshape(1, -1), steps, ma, mb, vp, vf, vsec)


def on_device(
    tokens, grad_output, valid_tiles, master_a, master_b, vector_params, matrix_first,
    matrix_second, vector_first, vector_second, left_a, right_a, left_b, right_b,
    owner_list, step_count,
):
    out, grad_in, *grads = run_block(
        tokens, grad_output, valid_tiles, master_a, master_b, vector_params
    )
    count = owner_list.shape[0]
    flat, vecs = rotate_blocks(grads, left_a, right_a, left_b, right_b, count)
    depth = flat.shape[0] // count
    axes = ("tok", "ch")
    wire = jnp.concatenate(
        [jnp.take(flat.reshape(count, depth, LANES), owner_list, axis=0), vecs], axis=1
    )
    owned = lax.psum_scatter(wire, axes, scatter_dimension=0, tiled=True)
    matrix_grad = owned[:, :depth].astype(F32).reshape(matrix_first.shape)
    steps = step_count[0].astype(F32)
    first_new = beta_one * matrix_first + (1.0 - beta_one) * matrix_grad
    second_new = beta_two * matrix_second + (1.0 - beta_two) * matrix_grad * matrix_grad
    direction = (
        first_new
        / (1.0 - beta_one**steps)
        / (jnp.sqrt(second_new / (1.0 - beta_two**steps)) + adam_epsilon)
    )
    sent = jnp.concatenate(
        [direction.astype(BF16).reshape(1, depth, LANES), owned[:, depth:]], axis=1
    )
    every = lax.all_gather(sent, axes, axis=0, tiled=True)
    blocks = every[:, :depth]
    if depth % 8:
        order = jnp.zeros_like(owner_list).at[owner_list].set(jnp.arange(count, dtype=jnp.int32))
        blocks = jnp.take(blocks, order, axis=0)
    new_a, new_b, copy_a, copy_b, vec_grad, vec_first, vec_second, new_vec = restore_blocks(
        blocks, every[:, depth:], owner_list, left_a, right_a, left_b, right_b, step_count,
        master_a, master_b, vector_params, vector_first, vector_second,
    )
    return (
        out.reshape(tokens.shape),
        grad_in.reshape(tokens.shape),
        matrix_grad,
        first_new,
        second_new,
        new_a,
        new_b,
        copy_a,
        copy_b,
        vec_grad,
        vec_first,
        vec_second,
        new_vec,
    )


def solution(mesh):
    part = P(None, ("tok", "ch"), None)
    owned = P(("tok", "ch"), None)
    in_specs = (part,) * 3 + (P(),) * 3 + (owned,) * 2 + (P(),) * 8
    out_specs = (part,) * 2 + (owned,) * 3 + (P(),) * 8
    return jax.shard_map(
        on_device, mesh=mesh, in_specs=in_specs, out_specs=out_specs, check_vma=False
    )
```

```python
import functools

import jax
import jax.numpy as jnp
from jax import lax
from jax.experimental import pallas as pl
from jax.experimental.pallas import tpu as pltpu
from jax.sharding import PartitionSpec as P

HEADS = 5
HEAD_DIM = 64
SIDE = 24
TILE = 8
TILES = 9
SLOTS = 576
KEYS = 144
LANES = 128
KEYS_TILE = 16

beta_one = 0.9
beta_two = 0.999
adam_epsilon = 1e-08
norm_epsilon = 1e-05
matrix_rate = 0.05
vector_rate = 0.2
weight_decay = 0.01

F32 = jnp.float32
BF16 = jnp.bfloat16


def contract(left, right, left_dim, right_dim):
    return lax.dot_general(
        left, right, (((left_dim,), (right_dim,)), ((), ())), preferred_element_type=F32
    )


def normalize(values):
    scale = 1.0 / values.shape[-1]
    center = values - jnp.sum(values, axis=-1, keepdims=True) * scale
    inverse = lax.rsqrt(jnp.sum(center * center, axis=-1, keepdims=True) * scale + norm_epsilon)
    return center * inverse, inverse


def norm_back(upstream, normal, inverse, gain):
    scale = 1.0 / upstream.shape[-1]
    scaled = upstream * gain
    inner = jnp.sum(scaled * normal, axis=-1, keepdims=True) * scale
    mean = jnp.sum(scaled, axis=-1, keepdims=True) * scale
    return inverse * (scaled - mean - normal * inner)


def row_sums(values):
    rows, cols = values.shape
    return jnp.sum(values.reshape(rows // 8, 8, cols), axis=0)


def group_all(values, op):
    lane = lax.broadcasted_iota(jnp.int32, values.shape, 1)
    for step in (1, 2, 4, 8):
        low = pltpu.roll(values, step, 1)
        high = pltpu.roll(values, LANES - step, 1)
        values = op(values, jnp.where((lane & step) != 0, low, high))
    return values


def split_tiles(rows):
    shaped = rows.reshape(TILE, 3, TILE, rows.shape[1])
    return [shaped[:, c].reshape(TILE * TILE, rows.shape[1]) for c in range(3)]


def join_tiles(tiles):
    return jnp.concatenate(
        [tiles[c][i * TILE : (i + 1) * TILE] for i in range(TILE) for c in range(3)], axis=0
    )


def gelu_parts(e):
    gauss = jnp.exp(-0.5 * e * e)
    size = jnp.abs(e)
    t = 1.0 / (1.0 + (0.3275911 * 0.7071067811865476) * size)
    poly = t * (
        0.5 * 0.254829592
        + t
        * (
            0.5 * -0.284496736
            + t * (0.5 * 1.421413741 + t * (0.5 * -1.453152027 + t * (0.5 * 1.061405429)))
        )
    )
    tail = poly * gauss
    phi = jnp.where(e >= 0.0, 1.0 - tail, tail)
    return phi, gauss * 0.3989422804014327


def block_kernel(
    flags,
    x_ref,
    dy_ref,
    wq,
    wk,
    wv,
    wo,
    wup,
    wr,
    wdn,
    vec,
    wide,
    pick,
    hmask,
    out_ref,
    gin_ref,
    gq,
    gk,
    gv,
    go,
    gup,
    gr,
    gdn,
    gsm,
    gwd,
    msk,
    xs,
    n1s,
    r1s,
    h1s,
    hms,
    qs,
    pats,
    kin,
    nks,
    rks,
    ks,
    vs,
    ps,
    ctxs,
    tmp,
    m1s,
    n2s,
    r2s,
    h2s,
    us,
    dhs,
    hids,
    dus,
    dms,
    das,
    dcs,
    dqs,
    dks,
    dvs,
    dps,
):
    g = pl.program_id(0)
    width = x_ref.shape[2]
    hidden = wup.shape[1]

    @pl.when(g == 0)
    def _():
        for ref in (gq, gk, gv, go, gup, gr, gdn, gsm, gwd):
            ref[...] = jnp.zeros(ref.shape, F32)

    row = lax.broadcasted_iota(jnp.int32, (TILE * TILE, width), 0)
    inside = jnp.where((row % TILE < TILE - 1) & (row < TILE * (TILE - 1)), 1.0, 0.0)
    for t in range(TILES):
        msk[t * 64 : (t + 1) * 64, :] = inside * flags[g, t].astype(F32)

    def vrow(number):
        return vec[number : number + 1, :]

    def add_small(number, sums):
        gsm[number : number + 1, :] += jnp.sum(sums, axis=0, keepdims=True)

    zero_rows = jnp.zeros((8, width), F32)

    def first_norm(big, carry):
        base = pl.multiple_of(big * 192, 64)
        tiles = split_tiles(x_ref[0, pl.ds(base, 192), :].astype(F32))
        grads = split_tiles(dy_ref[0, pl.ds(base, 192), :].astype(F32))
        for c in range(3):
            rows = pl.ds(base + c * 64, 64)
            normal, inverse = normalize(tiles[c])
            xs[rows, :] = tiles[c]
            n1s[rows, :] = normal
            r1s[rows, :] = inverse
            low = (normal * vrow(0) + vrow(1)).astype(BF16)
            h1s[rows, :] = low
            mask = msk[rows, :]
            hms[rows, :] = (low.astype(F32) * mask).astype(BF16)
            dms[rows, :] = (grads[c] * mask).astype(BF16)
        return carry

    lax.fori_loop(0, 3, first_norm, 0)
    qs[...] = (jnp.dot(h1s[...], wq[...], preferred_element_type=F32) + vrow(2)).astype(BF16)
    pats[...] = jnp.dot(pick[...], hms[...], preferred_element_type=F32).astype(BF16)
    reduced = vrow(4)
    for d in range(4):
        reduced = reduced + jnp.dot(
            pats[d * KEYS : (d + 1) * KEYS, :],
            wr[d * width : (d + 1) * width, :],
            preferred_element_type=F32,
        )
    normal, inverse = normalize(reduced)
    nks[...] = normal
    rks[...] = inverse
    kin[...] = (normal * vrow(5) + vrow(6)).astype(BF16)
    ks[...] = jnp.dot(kin[...], wk[...], preferred_element_type=F32).astype(BF16)
    vs[...] = (jnp.dot(kin[...], wv[...], preferred_element_type=F32) + vrow(3)).astype(BF16)
    score_scale = HEAD_DIM ** (-0.5)

    def spread(ref, t):
        part = ref[pl.ds(pl.multiple_of(t * KEYS_TILE, KEYS_TILE), KEYS_TILE), :]
        return jnp.concatenate([part] * 8, axis=0) * hmask[...]

    def gather_heads(big):
        big = big * hmask[...].astype(F32)
        total = big[0:KEYS_TILE]
        for h in range(1, HEADS):
            total = total + big[h * KEYS_TILE : (h + 1) * KEYS_TILE]
        return total

    def attend_tile(t, carry):
        rows = pl.ds(pl.multiple_of(t * 64, 64), 64)
        scores = contract(qs[rows, :], spread(ks, t), 1, 1) * score_scale
        exped = jnp.exp(scores - group_all(scores, jnp.maximum))
        probs = exped / group_all(exped, jnp.add)
        ps[rows, :] = probs
        ctxs[rows, :] = jnp.dot(
            probs.astype(BF16), spread(vs, t), preferred_element_type=F32
        ).astype(BF16)
        return carry

    lax.fori_loop(0, TILES, attend_tile, 0)
    tmp[...] = jnp.dot(ctxs[...], wo[...], preferred_element_type=F32)

    def second_norm(t, carry):
        rows = pl.ds(pl.multiple_of(t * 64, 64), 64)
        middle = xs[rows, :] + msk[rows, :] * (tmp[rows, :] + vrow(7))
        m1s[rows, :] = middle
        normal, inverse = normalize(middle)
        n2s[rows, :] = normal
        r2s[rows, :] = inverse
        h2s[rows, :] = (normal * vrow(8) + vrow(9)).astype(BF16)
        return carry

    lax.fori_loop(0, TILES, second_norm, 0)
    for c in range(hidden // 256):
        cols = slice(c * 256, (c + 1) * 256)
        us[:, cols] = jnp.dot(h2s[...], wup[:, cols], preferred_element_type=F32)
        dhs[:, cols] = contract(dms[...], wdn[cols, :], 1, 1)

    def mix_lanes(lane, carry):
        cols = pl.ds(pl.multiple_of(lane * LANES, LANES), LANES)
        bias_up = wide[0:1, cols]
        bias_dw = wide[1:2, cols]
        taps = [wide[2 + k : 3 + k, cols] for k in range(9)]

        def mix_tile(t, sums):
            sums = list(sums)
            rows = pl.ds(pl.multiple_of(t * 64, 64), 64)
            mask = msk[rows, 0:LANES]
            ups = (us[rows, cols] + bias_up) * mask
            mid = [ups[i * 8 : (i + 1) * 8] for i in range(7)]
            shifted = [
                [pltpu.roll(v, 1, 0) for v in mid],
                mid,
                [pltpu.roll(v, 7, 0) for v in mid],
            ]
            grads = dhs[rows, cols]
            hid_rows = []
            de_rows = []
            for i in range(7):
                e = bias_dw
                for a in range(3):
                    if 0 <= i + a - 1 < 7:
                        for b in range(3):
                            e = e + taps[3 * a + b] * shifted[b][i + a - 1]
                phi, gauss = gelu_parts(e)
                hid_rows.append(e * phi)
                de = grads[i * 8 : (i + 1) * 8] * (phi + e * gauss)
                de_rows.append(de)
                sums[1] = sums[1] + de
                for a in range(3):
                    if 0 <= i + a - 1 < 7:
                        for b in range(3):
                            k = 2 + 3 * a + b
                            sums[k] = sums[k] + de * shifted[b][i + a - 1]
            zero = jnp.zeros((8, LANES), F32)
            hids[rows, cols] = jnp.concatenate(hid_rows + [zero], axis=0).astype(BF16)
            back = [
                [pltpu.roll(v, 7, 0) for v in de_rows],
                de_rows,
                [pltpu.roll(v, 1, 0) for v in de_rows],
            ]
            du_rows = []
            for i in range(7):
                du = None
                for a in range(3):
                    if 0 <= i - a + 1 < 7:
                        for b in range(3):
                            term = taps[3 * a + b] * back[b][i - a + 1]
                            du = term if du is None else du + term
                du_rows.append(du * mask[i * 8 : (i + 1) * 8])
            du_low = jnp.concatenate(du_rows + [zero], axis=0).astype(BF16)
            dus[rows, cols] = du_low
            sums[0] = sums[0] + row_sums(du_low.astype(F32))
            return tuple(sums)

        zero = jnp.zeros((8, LANES), F32)
        sums = lax.fori_loop(0, TILES, mix_tile, (zero,) * 11)
        for k in range(11):
            gwd[k : k + 1, cols] += jnp.sum(sums[k], axis=0, keepdims=True)
        return carry

    lax.fori_loop(0, hidden // LANES, mix_lanes, 0)
    tmp[...] = jnp.dot(hids[...], wdn[...], preferred_element_type=F32)
    gdn[...] += contract(dms[...], hids[...], 0, 0)
    gup[...] += contract(h2s[...], dus[...], 0, 0)
    xs[...] = contract(dus[...], wup[...], 1, 1)

    def middle_rows(big, sums):
        sums = list(sums)
        base = pl.multiple_of(big * 192, 64)
        grads = split_tiles(dy_ref[0, pl.ds(base, 192), :].astype(F32))
        outs = []
        for c in range(3):
            rows = pl.ds(base + c * 64, 64)
            mask = msk[rows, :]
            outs.append(m1s[rows, :] + mask * (tmp[rows, :] + vrow(10)))
            dout = xs[rows, :]
            normal = n2s[rows, :]
            dmid = grads[c] + norm_back(dout, normal, r2s[rows, :], vrow(8))
            m1s[rows, :] = dmid
            low = (dmid * mask).astype(BF16)
            das[rows, :] = low
            sums[0] = sums[0] + row_sums(dout * normal)
            sums[1] = sums[1] + row_sums(dout)
            sums[2] = sums[2] + row_sums(low.astype(F32))
            sums[3] = sums[3] + row_sums(dms[rows, :].astype(F32))
        out_ref[0, pl.ds(base, 192), :] = join_tiles(outs).astype(BF16)
        return tuple(sums)

    sums = lax.fori_loop(0, 3, middle_rows, (zero_rows,) * 4)
    add_small(8, sums[0])
    add_small(9, sums[1])
    add_small(7, sums[2])
    add_small(10, sums[3])
    go[...] += contract(ctxs[...], das[...], 0, 0)
    dcs[...] = contract(das[...], wo[...], 1, 1).astype(BF16)

    def attend_back(t, sums):
        rows = pl.ds(pl.multiple_of(t * 64, 64), 64)
        keys = pl.ds(pl.multiple_of(t * KEYS_TILE, KEYS_TILE), KEYS_TILE)
        probs = ps[rows, :]
        upper = dcs[rows, :]
        dprobs = contract(upper, spread(vs, t), 1, 1)
        inner = group_all(dprobs * probs, jnp.add)
        dz = (probs * (dprobs - inner)).astype(BF16)
        dq = (
            jnp.dot(dz, spread(ks, t), preferred_element_type=F32) * score_scale
        ).astype(BF16)
        dqs[rows, :] = dq
        dk = gather_heads(contract(dz, qs[rows, :], 0, 0)) * score_scale
        dks[keys, :] = dk.astype(BF16)
        dv = gather_heads(contract(probs.astype(BF16), upper, 0, 0)).astype(BF16)
        dvs[keys, :] = dv
        return (sums[0] + row_sums(dq.astype(F32)), sums[1] + row_sums(dv.astype(F32)))

    sums = lax.fori_loop(0, TILES, attend_back, (zero_rows,) * 2)
    add_small(2, sums[0])
    add_small(3, sums[1])
    gq[...] += contract(h1s[...], dqs[...], 0, 0)
    gk[...] += contract(kin[...], dks[...], 0, 0)
    gv[...] += contract(kin[...], dvs[...], 0, 0)
    dout = contract(dks[...], wk[...], 1, 1) + contract(dvs[...], wv[...], 1, 1)
    normal = nks[...]
    ds = norm_back(dout, normal, rks[...], vrow(5)).astype(BF16)
    add_small(5, row_sums(dout * normal))
    add_small(6, row_sums(dout))
    add_small(4, row_sums(ds.astype(F32)))
    for d in range(4):
        rows = slice(d * KEYS, (d + 1) * KEYS)
        wide_rows = slice(d * width, (d + 1) * width)
        gr[wide_rows, :] += contract(pats[rows, :], ds, 0, 0)
        dps[rows, :] = contract(ds, wr[wide_rows, :], 1, 1).astype(BF16)
    tmp[...] = contract(pick[...], dps[...], 0, 0)
    xs[...] = contract(dqs[...], wq[...], 1, 1)

    def last_rows(big, sums):
        sums = list(sums)
        base = pl.multiple_of(big * 192, 64)
        outs = []
        for c in range(3):
            rows = pl.ds(base + c * 64, 64)
            dout = xs[rows, :] + msk[rows, :] * tmp[rows, :]
            normal = n1s[rows, :]
            outs.append(m1s[rows, :] + norm_back(dout, normal, r1s[rows, :], vrow(0)))
            sums[0] = sums[0] + row_sums(dout * normal)
            sums[1] = sums[1] + row_sums(dout)
        gin_ref[0, pl.ds(base, 192), :] = join_tiles(outs)
        return tuple(sums)

    sums = lax.fori_loop(0, 3, last_rows, (zero_rows,) * 2)
    add_small(0, sums[0])
    add_small(1, sums[1])


def pick_matrix():
    spot = jnp.arange(SLOTS)
    part = spot // KEYS
    key = spot % KEYS
    tile = key // KEYS_TILE
    inner = key % KEYS_TILE
    slot = tile * 64 + (2 * (inner // 4) + part // 2) * TILE + 2 * (inner % 4) + part % 2
    return (slot[:, None] == spot[None, :]).astype(BF16)


def head_mask(width):
    row = jnp.arange(8 * KEYS_TILE) // KEYS_TILE
    col = jnp.arange(width) // HEAD_DIM
    return (row[:, None] == col[None, :]).astype(BF16)


def run_block(tokens, grad_output, valid_tiles, master_a, master_b, vector_params):
    width = tokens.shape[2]
    hidden = master_b.shape[0]
    grids = tokens.shape[0] * tokens.shape[1] // SLOTS
    x = tokens.reshape(grids, SLOTS, width)
    dy = grad_output.reshape(grids, SLOTS, width)
    flags = valid_tiles.reshape(grids, TILES)
    low_a = master_a.astype(BF16)
    low_b = master_b.astype(BF16)
    weights = (
        low_a[:, :width],
        low_a[:, width : 2 * width],
        low_a[:, 2 * width : 3 * width],
        low_a[:, 3 * width : 4 * width],
        low_a[:, 4 * width :],
        low_b[:, :width],
        low_b[:, width:],
    )
    wide = vector_params[11:].reshape(11, hidden)
    consts = weights + (vector_params[:11], wide, pick_matrix(), head_mask(width))
    grid_spec = pl.BlockSpec((1, SLOTS, width), lambda g: (g, 0, 0))

    def whole(shape):
        return pl.BlockSpec(shape, lambda g: (0,) * len(shape), pipeline_mode=pl.Buffered(1))

    grad_shapes = [(width, width)] * 4 + [
        (width, hidden),
        (hidden, width),
        (width, hidden),
        (16, width),
        (16, hidden),
    ]
    tall = (SLOTS, width)
    keys = (KEYS, width)
    scratch = [
        (tall, F32),
        (tall, F32),
        (tall, F32),
        ((SLOTS, 1), F32),
        (tall, BF16),
        (tall, BF16),
        (tall, BF16),
        (tall, BF16),
        (keys, BF16),
        (keys, F32),
        ((KEYS, 1), F32),
        (keys, BF16),
        (keys, BF16),
        ((SLOTS, LANES), F32),
        (tall, BF16),
        (tall, F32),
        (tall, F32),
        (tall, F32),
        ((SLOTS, 1), F32),
        (tall, BF16),
        ((SLOTS, hidden), F32),
        ((SLOTS, hidden), F32),
        ((SLOTS, hidden), BF16),
        ((SLOTS, hidden), BF16),
        (tall, BF16),
        (tall, BF16),
        (tall, BF16),
        (tall, BF16),
        (keys, BF16),
        (keys, BF16),
        (tall, BF16),
    ]
    return pl.pallas_call(
        block_kernel,
        name="block_step",
        grid=(grids,),
        in_specs=[pl.BlockSpec(memory_space=pltpu.SMEM), grid_spec, grid_spec]
        + [whole(c.shape) for c in consts],
        out_specs=[grid_spec, grid_spec] + [whole(s) for s in grad_shapes],
        out_shape=[
            jax.ShapeDtypeStruct((grids, SLOTS, width), BF16),
            jax.ShapeDtypeStruct((grids, SLOTS, width), F32),
        ]
        + [jax.ShapeDtypeStruct(s, F32) for s in grad_shapes],
        scratch_shapes=[pltpu.VMEM(s, d) for s, d in scratch],
        compiler_params=pltpu.CompilerParams(vmem_limit_bytes=60 << 20),
    )(flags, x, dy, *consts)

SPANS_A = ((0, 1), (1, 2), (3, 1), (4, 4))
VECTOR_ROWS = 143


def fill_codes(la, ra, lb, rb, codes, width):
    hidden = lb.shape[1]
    codes[...] = jnp.full(codes.shape, -2, jnp.int32)
    codes[0:4, 0:width] = la[...]
    codes[4:6, 0:hidden] = lb[...]
    for k, (first, count) in enumerate(SPANS_A):
        start = first * width
        span = count * width
        codes[6 + k : 7 + k, 0:span] = ra[:, start : start + span] - 2 * start
    for k in range(2):
        codes[10 + k : 11 + k, 0:width] = rb[:, k * width : (k + 1) * width] - 2 * k * width


def lane_matrix(codes, k, size):
    code = codes[k : k + 1, 0:size]
    sign = (1 - 2 * (code & 1)).astype(F32)
    spot = lax.broadcasted_iota(jnp.int32, (size, size), 0)
    return jnp.where(spot == (code >> 1), sign, 0.0).astype(BF16)


def row_matrix(codes, k, out, size):
    for start in range(0, size, LANES):
        code = codes[k : k + 1, start : start + LANES]
        spot = jnp.transpose(jnp.broadcast_to((code >> 1).astype(F32), (LANES, LANES)))
        sign = jnp.transpose(
            jnp.broadcast_to((1 - 2 * (code & 1)).astype(F32), (LANES, LANES))
        )
        for col in range(0, size, LANES):
            lane = lax.broadcasted_iota(jnp.int32, (LANES, LANES), 1).astype(F32) + col
            part = jnp.where(spot == lane, sign, 0.0).astype(BF16)
            out[start : start + LANES, col : col + LANES] = part


def vector_spots(width, hidden):
    spots = []
    for k in range(11):
        for col in range(0, width, LANES):
            spots.append((0, k, col, min(LANES, width - col)))
    for k in range(11):
        for col in range(0, hidden, LANES):
            spots.append((1, k, col, LANES))
    return spots


def rotate_kernel(
    order, gq, gk, gv, go, gup, gr, gdn, gsm, gwd, la, ra, lb, rb, wire,
    codes, rows_m, ras, rbs, flat, per_block,
):
    width, hidden = gup.shape
    fill_codes(la, ra, lb, rb, codes, width)

    def dot(left, right):
        return jnp.dot(left, right, preferred_element_type=F32)

    for k, parts in enumerate(((gq,), (gk, gv), (go,), (gup,))):
        first, count = SPANS_A[k]
        right = lane_matrix(codes, 6 + k, count * width)
        total = None
        depth = right.shape[0] // len(parts)
        for p, part in enumerate(parts):
            piece = dot(part[...].astype(BF16), right[p * depth : (p + 1) * depth])
            total = piece if total is None else total + piece
        row_matrix(codes, k, rows_m, width)
        ras[:, first * width : (first + count) * width] = dot(rows_m[0:width, 0:width], total.astype(BF16))
    row_matrix(codes, 4, rows_m, hidden)
    part = dot(rows_m[...], gr[...].astype(BF16)).astype(BF16)
    rbs[:, 0:width] = dot(part, lane_matrix(codes, 10, width))
    row_matrix(codes, 5, rows_m, hidden)
    part = contract(rows_m[...], gdn[...].astype(BF16), 1, 1).astype(BF16)
    rbs[:, width : 2 * width] = dot(part, lane_matrix(codes, 11, width))
    per_row = ras.shape[1] // LANES
    for j in range(per_row):
        flat[pl.ds(j, width, stride=per_row), :] = ras[:, j * LANES : (j + 1) * LANES]
    base = width * per_row
    per_row = rbs.shape[1] // LANES
    for j in range(per_row):
        flat[pl.ds(base + j, hidden, stride=per_row), :] = rbs[:, j * LANES : (j + 1) * LANES]
    count, tall, _ = wire.shape
    depth = flat.shape[0] // count

    def place(t, carry):
        wire[t, 0:depth, :] = flat[pl.ds(order[t] * depth, depth), :].astype(BF16)
        wire[t, depth:tall, :] = jnp.zeros((tall - depth, LANES), BF16)
        return carry

    lax.fori_loop(0, count, place, 0)
    for number, (kind, k, col, size) in enumerate(vector_spots(width, hidden)):
        block, row = number // per_block, depth + number % per_block
        source = (gsm, gwd)[kind]
        wire[block, row : row + 1, 0:size] = source[k : k + 1, col : col + size].astype(BF16)


def restore_kernel(
    blocks, order, la, ra, lb, rb, steps, ma, mb, vp, vf, vsec,
    na, nb, ca, cb, vg, vfn, vsn, nv,
    codes, rows_m, das, dbs, flat, wide_s, per_block,
):
    width = ma.shape[0]
    hidden = mb.shape[0]
    fill_codes(la, ra, lb, rb, codes, width)
    count = blocks.shape[0]
    depth = flat.shape[0] // count

    def place(t, carry):
        flat[pl.ds(order[t] * depth, depth), :] = blocks[t, 0:depth, :].astype(F32)
        return carry

    lax.fori_loop(0, count, place, 0)
    per_row = ma.shape[1] // LANES
    for j in range(per_row):
        das[:, j * LANES : (j + 1) * LANES] = flat[pl.ds(j, width, stride=per_row), :]
    base = width * per_row
    per_row = mb.shape[1] // LANES
    for j in range(per_row):
        dbs[:, j * LANES : (j + 1) * LANES] = flat[pl.ds(base + j, hidden, stride=per_row), :]

    def dot(left, right):
        return jnp.dot(left, right, preferred_element_type=F32)

    def update(master, step, new, copy, cols):
        old = master[:, cols]
        value = old - matrix_rate * (step + weight_decay * old)
        new[:, cols] = value
        copy[:, cols] = value.astype(BF16)

    for k, (first, span) in enumerate(SPANS_A):
        size = span * width
        cols = slice(first * width, first * width + size)
        part = dot(lane_matrix(codes, k, width), das[:, cols].astype(BF16)).astype(BF16)
        row_matrix(codes, 6 + k, rows_m, size)
        update(ma, dot(part, rows_m[0:size, 0:size]), na, ca, cols)
    for k in range(2):
        cols = slice(k * width, (k + 1) * width)
        part = dot(lane_matrix(codes, 4 + k, hidden), dbs[:, cols].astype(BF16)).astype(BF16)
        row_matrix(codes, 10 + k, rows_m, width)
        update(mb, dot(part, rows_m[0:width, 0:width]), nb, cb, cols)
    for number, (kind, k, col, size) in enumerate(vector_spots(width, hidden)):
        block, row = number // per_block, depth + number % per_block
        value = blocks[block, row : row + 1, 0:size].astype(F32)
        if kind == 0:
            vg[k : k + 1, col : col + size] = value
        else:
            wide_s[k : k + 1, col : col + size] = value
    ratio = hidden // width
    for k in range(11):
        for q in range(ratio):
            row = 11 + ratio * k + q
            vg[row : row + 1, :] = wide_s[k : k + 1, q * width : (q + 1) * width]
    grad = vg[...]
    first_new = beta_one * vf[...] + (1.0 - beta_one) * grad
    second_new = beta_two * vsec[...] + (1.0 - beta_two) * grad * grad
    vfn[...] = first_new
    vsn[...] = second_new
    move = direction_of(first_new, second_new, steps[0])
    old = vp[...]
    nv[...] = old - vector_rate * (move + weight_decay * old)


def direction_of(first_new, second_new, steps):
    count = jnp.full((1, LANES), steps, jnp.int32).astype(F32)
    log_one = -0.10536051565782628
    log_two = -0.0010005003335835335
    one = (1.0 / (1.0 - jnp.exp(count * log_one)))[:, 0:1]
    two = (1.0 / (1.0 - jnp.exp(count * log_two)))[:, 0:1]
    return first_new * one / (jnp.sqrt(second_new * two) + adam_epsilon)


def vmem_spec():
    return pl.BlockSpec(memory_space=pltpu.VMEM)


def rotate_blocks(order, grads, la, ra, lb, rb):
    width, hidden = grads[4].shape
    blocks = order.shape[0]
    per_block = -(-VECTOR_ROWS // blocks)
    total = (width * 8 * width + hidden * 2 * width) // LANES
    tall = -(-(total // blocks + per_block) // 32) * 32
    smem = pl.BlockSpec(memory_space=pltpu.SMEM)
    return pl.pallas_call(
        functools.partial(rotate_kernel, per_block=per_block),
        name="rotate",
        in_specs=[smem] + [vmem_spec()] * 13,
        out_specs=vmem_spec(),
        out_shape=jax.ShapeDtypeStruct((blocks, tall, LANES), BF16),
        scratch_shapes=[
            pltpu.VMEM((16, hidden), jnp.int32),
            pltpu.VMEM((hidden, hidden), BF16),
            pltpu.VMEM((width, 8 * width), F32),
            pltpu.VMEM((hidden, 2 * width), F32),
            pltpu.VMEM((total, LANES), F32),
        ],
        compiler_params=pltpu.CompilerParams(vmem_limit_bytes=60 << 20),
    )(order, *grads, la, ra.reshape(1, -1), lb, rb.reshape(1, -1))


def restore_blocks(blocks, order, la, ra, lb, rb, steps, ma, mb, vp, vf, vsec):
    width = ma.shape[0]
    hidden = mb.shape[0]
    per_block = -(-VECTOR_ROWS // blocks.shape[0])
    total = (ma.size + mb.size) // LANES
    smem = pl.BlockSpec(memory_space=pltpu.SMEM)
    return pl.pallas_call(
        functools.partial(restore_kernel, per_block=per_block),
        name="restore",
        in_specs=[vmem_spec(), smem] + [vmem_spec()] * 4 + [smem] + [vmem_spec()] * 5,
        out_specs=[vmem_spec()] * 8,
        out_shape=[
            jax.ShapeDtypeStruct(ma.shape, F32),
            jax.ShapeDtypeStruct(mb.shape, F32),
            jax.ShapeDtypeStruct(ma.shape, BF16),
            jax.ShapeDtypeStruct(mb.shape, BF16),
        ]
        + [jax.ShapeDtypeStruct(vp.shape, F32)] * 4,
        scratch_shapes=[
            pltpu.VMEM((16, hidden), jnp.int32),
            pltpu.VMEM((hidden, hidden), BF16),
            pltpu.VMEM((width, 8 * width), F32),
            pltpu.VMEM((hidden, 2 * width), F32),
            pltpu.VMEM((total, LANES), F32),
            pltpu.VMEM((16, hidden), F32),
        ],
        compiler_params=pltpu.CompilerParams(vmem_limit_bytes=60 << 20),
    )(blocks, order, la, ra.reshape(1, -1), lb, rb.reshape(1, -1), steps, ma, mb, vp, vf, vsec)


def exchange_kernel(wire, first, second, steps, grad, first_new, second_new, every, *scratch,
                    plan, bits, depth):
    buffers = []
    spot = 0
    for _, _, order in plan:
        buffers.append(scratch[spot : spot + len(order)])
        spot += len(order)
    rs_send, rs_recv, ag_send, ag_recv = scratch[spot:]
    tok = lax.axis_index("tok")
    side = lax.axis_index("ch")

    def mine(axis):
        return side if axis == "ch" else lax.rem(lax.div(tok, 2**axis), 2)

    def peer(axis):
        if axis == "ch":
            return {"ch": 1 - side}
        return {"tok": tok + 2**axis - 2 ** (axis + 1) * mine(axis)}

    axes = [*reversed(range(bits)), "ch"]
    barrier = pltpu.get_barrier_semaphore()
    for axis in axes:
        pl.semaphore_signal(barrier, inc=1, device_id=peer(axis), device_id_type=pl.DeviceIdType.MESH)
    pl.semaphore_wait(barrier, len(axes))

    chunks = range(len(plan))
    left = [list(axes) for _ in chunks]
    held = [wire for _ in chunks]
    pending = []

    def region(c, choice):
        index = tuple(choice(axis) for axis in left[c])
        start, size, _ = plan[c]
        rows = pl.ds(start, size) if held[c] is wire else slice(None)
        return index + (rows, slice(None))

    def scatter_start(c, s):
        axis = plan[c][2][s]
        index = region(c, lambda a: 1 - mine(a) if a == axis else slice(None))
        copy = pltpu.make_async_remote_copy(
            held[c].at[index], buffers[c][s], rs_send.at[c, s], rs_recv.at[c, s],
            device_id=peer(axis), device_id_type=pl.DeviceIdType.MESH,
        )
        copy.start()
        pending.append(copy)
        return copy

    def scatter_keep(c, s):
        axis = plan[c][2][s]
        return held[c][region(c, lambda a: mine(a) if a == axis else slice(None))]

    def gather_start(c, s):
        start, size, order = plan[c]
        axis = order[len(order) - 1 - s]
        done = order[len(order) - s :]
        index = tuple(slice(None) if a in done else mine(a) for a in axes)
        piece = every.at[index + (pl.ds(start, size), slice(None))]
        copy = pltpu.make_async_remote_copy(
            piece, piece, ag_send.at[c, s], ag_recv.at[c, s],
            device_id=peer(axis), device_id_type=pl.DeviceIdType.MESH,
        )
        copy.start()
        pending.append(copy)
        return copy

    stages = len(axes)
    flying = [scatter_start(c, 0) for c in chunks]
    for s in range(stages):
        for c in chunks:
            start, size, order = plan[c]
            flying[c].wait_recv()
            kept = scatter_keep(c, s)
            buffer = buffers[c][s]
            if s < stages - 1:
                buffer[...] = buffer[...] + kept
                left[c].remove(order[s])
                held[c] = buffer
                flying[c] = scatter_start(c, s + 1)
                continue
            total = buffer[...].astype(F32) + kept.astype(F32)
            count = max(0, min(depth - start, size))
            parts = []
            if count:
                rows = slice(start, start + count)
                owned = total[:count]
                grad[rows, :] = owned
                one = beta_one * first[rows, :] + (1.0 - beta_one) * owned
                two = beta_two * second[rows, :] + (1.0 - beta_two) * owned * owned
                first_new[rows, :] = one
                second_new[rows, :] = two
                parts.append(direction_of(one, two, steps[0]))
            if count < size:
                parts.append(total[count:])
            ready = parts[0] if len(parts) == 1 else jnp.concatenate(parts, axis=0)
            own = tuple(mine(a) for a in axes)
            every[own + (slice(start, start + size), slice(None))] = ready.astype(BF16)
            flying[c] = gather_start(c, 0)
    for s in range(stages):
        for c in chunks:
            flying[c].wait_recv()
            if s < stages - 1:
                flying[c] = gather_start(c, s + 1)
    for copy in pending:
        copy.wait_send()


def exchange_blocks(wire, first, second, steps, bits):
    count, tall, _ = wire.shape
    depth = first.shape[0]
    units = tall // 16
    small = max(1, units * 6 // 26)
    large = (units - small + 1) // 2
    rest = list(range(2, bits))
    sizes = (small, large, units - small - large)
    orders = ([0] + rest + ["ch", 1], [0, "ch", 1] + rest, [0, 1, "ch"] + rest)
    plan = []
    start = 0
    for size, order in zip(sizes, orders):
        plan.append((start, size * 16, order))
        start += size * 16
    scratch = []
    for _, size, order in plan:
        for s in range(len(order)):
            scratch.append(pltpu.VMEM((2,) * (len(order) - 1 - s) + (size, LANES), BF16))
    for _ in range(4):
        scratch.append(pltpu.SemaphoreType.DMA((len(plan), bits + 1)))
    shape = (2,) * (bits + 1) + (tall, LANES)
    block = jax.ShapeDtypeStruct((depth, LANES), F32)
    grad, first_new, second_new, every = pl.pallas_call(
        functools.partial(exchange_kernel, plan=plan, bits=bits, depth=depth),
        name="exchange",
        in_specs=[vmem_spec()] * 3 + [pl.BlockSpec(memory_space=pltpu.SMEM)],
        out_specs=[vmem_spec()] * 4,
        out_shape=[block, block, block, jax.ShapeDtypeStruct(shape, BF16)],
        scratch_shapes=scratch,
        compiler_params=pltpu.CompilerParams(
            vmem_limit_bytes=60 << 20, collective_id=0, has_side_effects=True
        ),
    )(wire.reshape(shape), first, second, steps)
    return grad, first_new, second_new, every.reshape(wire.shape)


def on_device(
    tokens, grad_output, valid_tiles, master_a, master_b, vector_params, matrix_first,
    matrix_second, vector_first, vector_second, left_a, right_a, left_b, right_b,
    owner_list, step_count, bits,
):
    out, grad_in, *grads = run_block(
        tokens, grad_output, valid_tiles, master_a, master_b, vector_params
    )
    wire = rotate_blocks(owner_list, grads, left_a, right_a, left_b, right_b)
    shape = matrix_first.shape
    grad, first_new, second_new, every = exchange_blocks(
        wire, matrix_first.reshape(-1, LANES), matrix_second.reshape(-1, LANES), step_count, bits
    )
    restored = restore_blocks(
        every, owner_list, left_a, right_a, left_b, right_b, step_count,
        master_a, master_b, vector_params, vector_first, vector_second,
    )
    return (
        out.reshape(tokens.shape),
        grad_in.reshape(tokens.shape),
        grad.reshape(shape),
        first_new.reshape(shape),
        second_new.reshape(shape),
        *restored,
    )


def solution(mesh):
    bits = mesh.shape["tok"].bit_length() - 1
    part = P(None, ("tok", "ch"), None)
    owned = P(("tok", "ch"), None)
    in_specs = (part,) * 3 + (P(),) * 3 + (owned,) * 2 + (P(),) * 8
    out_specs = (part,) * 2 + (owned,) * 3 + (P(),) * 8
    return jax.shard_map(
        functools.partial(on_device, bits=bits), mesh=mesh, in_specs=in_specs, out_specs=out_specs, check_vma=False
    )
```

```python
import functools

import jax
import jax.numpy as jnp
from jax import lax
from jax.experimental import pallas as pl
from jax.experimental.pallas import tpu as pltpu
from jax.sharding import PartitionSpec as P

HEADS = 5
HEAD_DIM = 64
SIDE = 24
TILE = 8
TILES = 9
SLOTS = 576
KEYS = 144
LANES = 128
KEYS_TILE = 16

beta_one = 0.9
beta_two = 0.999
adam_epsilon = 1e-08
norm_epsilon = 1e-05
matrix_rate = 0.05
vector_rate = 0.2
weight_decay = 0.01

F32 = jnp.float32
BF16 = jnp.bfloat16


def contract(left, right, left_dim, right_dim):
    return lax.dot_general(
        left, right, (((left_dim,), (right_dim,)), ((), ())), preferred_element_type=F32
    )


def normalize(values):
    scale = 1.0 / values.shape[-1]
    center = values - jnp.sum(values, axis=-1, keepdims=True) * scale
    inverse = lax.rsqrt(jnp.sum(center * center, axis=-1, keepdims=True) * scale + norm_epsilon)
    return center * inverse, inverse


def norm_back(upstream, normal, inverse, gain):
    scale = 1.0 / upstream.shape[-1]
    scaled = upstream * gain
    inner = jnp.sum(scaled * normal, axis=-1, keepdims=True) * scale
    mean = jnp.sum(scaled, axis=-1, keepdims=True) * scale
    return inverse * (scaled - mean - normal * inner)


def row_sums(values):
    rows, cols = values.shape
    return jnp.sum(values.reshape(rows // 8, 8, cols), axis=0)


def group_all(values, op):
    lane = lax.broadcasted_iota(jnp.int32, values.shape, 1)
    for step in (1, 2, 4, 8):
        low = pltpu.roll(values, step, 1)
        high = pltpu.roll(values, LANES - step, 1)
        values = op(values, jnp.where((lane & step) != 0, low, high))
    return values


def split_tiles(rows):
    shaped = rows.reshape(TILE, 3, TILE, rows.shape[1])
    return [shaped[:, c].reshape(TILE * TILE, rows.shape[1]) for c in range(3)]


def join_tiles(tiles):
    return jnp.concatenate(
        [tiles[c][i * TILE : (i + 1) * TILE] for i in range(TILE) for c in range(3)], axis=0
    )


def gelu_parts(e):
    gauss = jnp.exp2((-0.5 * 1.4426950408889634) * (e * e))
    size = jnp.abs(e)
    t = 1.0 / (1.0 + (0.3275911 * 0.7071067811865476) * size)
    poly = t * (
        0.5 * 0.254829592
        + t
        * (
            0.5 * -0.284496736
            + t * (0.5 * 1.421413741 + t * (0.5 * -1.453152027 + t * (0.5 * 1.061405429)))
        )
    )
    tail = poly * gauss
    phi = jnp.where(e >= 0.0, 1.0 - tail, tail)
    return phi, gauss * 0.3989422804014327


def block_kernel(
    flags,
    order,
    x_ref,
    dy_ref,
    ma,
    mb,
    vec,
    la,
    ra,
    lb,
    rb,
    out_ref,
    gin_ref,
    wire,
    wq,
    wk,
    wv,
    wo,
    wup,
    wr,
    wdn,
    wide,
    pick,
    hmask,
    gq,
    gk,
    gv,
    go,
    gup,
    gr,
    gdn,
    gsm,
    gwd,
    mas,
    mbs,
    sems,
    xrow,
    dyrow,
    orow,
    grow,
    codes,
    rows_m,
    flat,
    msk,
    xs,
    n1s,
    r1s,
    h1s,
    hms,
    qs,
    pats,
    kin,
    nks,
    rks,
    ks,
    vs,
    ps,
    ctxs,
    tmp,
    m1s,
    n2s,
    r2s,
    h2s,
    us,
    dhs,
    hids,
    dus,
    dms,
    das,
    dcs,
    dqs,
    dks,
    dvs,
    dps,
    *,
    per,
    per_block,
):
    g = pl.program_id(0)
    part = lax.rem(g, per)
    width = x_ref.shape[1]
    hidden = wup.shape[1]
    spans = x_ref.shape[2] // LANES
    base_row = part * SLOTS
    load_a = pltpu.make_async_copy(ma, mas, sems.at[0])
    load_b = pltpu.make_async_copy(mb, mbs, sems.at[1])

    @pl.when(g == 0)
    def _():
        load_a.start()
        load_b.start()
        pick[...] = pick_matrix()
        hmask[...] = head_mask(width)
        ratio = hidden // width
        for k in range(11):
            for q in range(ratio):
                row = 11 + ratio * k + q
                wide[k : k + 1, q * width : (q + 1) * width] = vec[row : row + 1, :]
        for ref in (gq, gk, gv, go, gup, gr, gdn, gsm, gwd):
            ref[...] = jnp.zeros(ref.shape, F32)

    @pl.when(part == 0)
    def _():
        for c in range(spans):
            cols = slice(c * LANES, (c + 1) * LANES)
            xrow[cols, :] = jnp.transpose(x_ref[0, :, cols].astype(F32)).astype(BF16)
            dyrow[cols, :] = jnp.transpose(dy_ref[0, :, cols].astype(F32)).astype(BF16)

    row = lax.broadcasted_iota(jnp.int32, (TILE * TILE, width), 0)
    inside = jnp.where((row % TILE < TILE - 1) & (row < TILE * (TILE - 1)), 1.0, 0.0)
    for t in range(TILES):
        msk[t * 64 : (t + 1) * 64, :] = inside * flags[g, t].astype(F32)

    def vrow(number):
        return vec[number : number + 1, :]

    def add_small(number, sums):
        gsm[number : number + 1, :] += jnp.sum(sums, axis=0, keepdims=True)

    zero_rows = jnp.zeros((8, width), F32)

    def first_norm(big, carry):
        base = pl.multiple_of(big * 192, 64)
        tiles = split_tiles(xrow[pl.ds(base_row + base, 192), :].astype(F32))
        grads = split_tiles(dyrow[pl.ds(base_row + base, 192), :].astype(F32))
        for c in range(3):
            rows = pl.ds(base + c * 64, 64)
            normal, inverse = normalize(tiles[c])
            xs[rows, :] = tiles[c]
            n1s[rows, :] = normal
            r1s[rows, :] = inverse
            low = (normal * vrow(0) + vrow(1)).astype(BF16)
            h1s[rows, :] = low
            mask = msk[rows, :]
            hms[rows, :] = (low.astype(F32) * mask).astype(BF16)
            dms[rows, :] = (grads[c] * mask).astype(BF16)
        return carry

    lax.fori_loop(0, 3, first_norm, 0)

    @pl.when(g == 0)
    def _():
        load_a.wait()
        for k, ref in enumerate((wq, wk, wv, wo)):
            ref[...] = mas[:, k * width : (k + 1) * width].astype(BF16)
        wup[...] = mas[:, 4 * width :].astype(BF16)
        load_b.wait()
        wr[...] = mbs[:, :width].astype(BF16)
        wdn[...] = mbs[:, width:].astype(BF16)

    qs[...] = (jnp.dot(h1s[...], wq[...], preferred_element_type=F32) + vrow(2)).astype(BF16)
    pats[...] = jnp.dot(pick[...], hms[...], preferred_element_type=F32).astype(BF16)
    reduced = vrow(4)
    for d in range(4):
        reduced = reduced + jnp.dot(
            pats[d * KEYS : (d + 1) * KEYS, :],
            wr[d * width : (d + 1) * width, :],
            preferred_element_type=F32,
        )
    normal, inverse = normalize(reduced)
    nks[...] = normal
    rks[...] = inverse
    kin[...] = (normal * vrow(5) + vrow(6)).astype(BF16)
    ks[...] = jnp.dot(kin[...], wk[...], preferred_element_type=F32).astype(BF16)
    vs[...] = (jnp.dot(kin[...], wv[...], preferred_element_type=F32) + vrow(3)).astype(BF16)
    score_scale = HEAD_DIM ** (-0.5)

    def spread(ref, t):
        part = ref[pl.ds(pl.multiple_of(t * KEYS_TILE, KEYS_TILE), KEYS_TILE), :]
        return jnp.concatenate([part] * 8, axis=0) * hmask[...]

    def gather_heads(big):
        big = big * hmask[...].astype(F32)
        total = big[0:KEYS_TILE]
        for h in range(1, HEADS):
            total = total + big[h * KEYS_TILE : (h + 1) * KEYS_TILE]
        return total

    def attend_tile(t, carry):
        rows = pl.ds(pl.multiple_of(t * 64, 64), 64)
        scores = contract(qs[rows, :], spread(ks, t), 1, 1) * score_scale
        exped = jnp.exp(scores - group_all(scores, jnp.maximum))
        probs = exped / group_all(exped, jnp.add)
        ps[rows, :] = probs
        ctxs[rows, :] = jnp.dot(
            probs.astype(BF16), spread(vs, t), preferred_element_type=F32
        ).astype(BF16)
        return carry

    lax.fori_loop(0, TILES, attend_tile, 0, unroll=3)
    tmp[...] = jnp.dot(ctxs[...], wo[...], preferred_element_type=F32)

    def second_norm(t, carry):
        rows = pl.ds(pl.multiple_of(t * 64, 64), 64)
        middle = xs[rows, :] + msk[rows, :] * (tmp[rows, :] + vrow(7))
        m1s[rows, :] = middle
        normal, inverse = normalize(middle)
        n2s[rows, :] = normal
        r2s[rows, :] = inverse
        h2s[rows, :] = (normal * vrow(8) + vrow(9)).astype(BF16)
        return carry

    lax.fori_loop(0, TILES, second_norm, 0, unroll=3)
    for c in range(hidden // 256):
        cols = slice(c * 256, (c + 1) * 256)
        us[:, cols] = jnp.dot(h2s[...], wup[:, cols], preferred_element_type=F32)
        dhs[:, cols] = contract(dms[...], wdn[cols, :], 1, 1)

    def mix_lanes(lane, carry):
        cols = pl.ds(pl.multiple_of(lane * LANES, LANES), LANES)
        bias_up = wide[0:1, cols]
        bias_dw = wide[1:2, cols]
        taps = [wide[2 + k : 3 + k, cols] for k in range(9)]

        def mix_tile(t, sums):
            sums = list(sums)
            rows = pl.ds(pl.multiple_of(t * 64, 64), 64)
            mask = msk[rows, 0:LANES]
            ups = (us[rows, cols] + bias_up) * mask
            mid = [ups[i * 8 : (i + 1) * 8] for i in range(7)]
            shifted = [
                [pltpu.roll(v, 1, 0) for v in mid],
                mid,
                [pltpu.roll(v, 7, 0) for v in mid],
            ]
            grads = dhs[rows, cols]
            hid_rows = []
            de_rows = []
            for i in range(7):
                e = bias_dw
                for a in range(3):
                    if 0 <= i + a - 1 < 7:
                        for b in range(3):
                            e = e + taps[3 * a + b] * shifted[b][i + a - 1]
                phi, gauss = gelu_parts(e)
                hid_rows.append(e * phi)
                de = grads[i * 8 : (i + 1) * 8] * (phi + e * gauss)
                de_rows.append(de)
                sums[1] = sums[1] + de
                for a in range(3):
                    if 0 <= i + a - 1 < 7:
                        for b in range(3):
                            k = 2 + 3 * a + b
                            sums[k] = sums[k] + de * shifted[b][i + a - 1]
            zero = jnp.zeros((8, LANES), F32)
            hids[rows, cols] = jnp.concatenate(hid_rows + [zero], axis=0).astype(BF16)
            back = [
                [pltpu.roll(v, 7, 0) for v in de_rows],
                de_rows,
                [pltpu.roll(v, 1, 0) for v in de_rows],
            ]
            du_rows = []
            for i in range(7):
                du = None
                for a in range(3):
                    if 0 <= i - a + 1 < 7:
                        for b in range(3):
                            term = taps[3 * a + b] * back[b][i - a + 1]
                            du = term if du is None else du + term
                du_rows.append(du * mask[i * 8 : (i + 1) * 8])
            du_low = jnp.concatenate(du_rows + [zero], axis=0).astype(BF16)
            dus[rows, cols] = du_low
            sums[0] = sums[0] + row_sums(du_low.astype(F32))
            return tuple(sums)

        zero = jnp.zeros((8, LANES), F32)
        sums = lax.fori_loop(0, TILES, mix_tile, (zero,) * 11)
        for k in range(11):
            gwd[k : k + 1, cols] += jnp.sum(sums[k], axis=0, keepdims=True)
        return carry

    lax.fori_loop(0, hidden // LANES, mix_lanes, 0)
    tmp[...] = jnp.dot(hids[...], wdn[...], preferred_element_type=F32)
    gdn[...] += contract(dms[...], hids[...], 0, 0)
    gup[...] += contract(h2s[...], dus[...], 0, 0)
    xs[...] = contract(dus[...], wup[...], 1, 1)

    def middle_rows(big, sums):
        sums = list(sums)
        base = pl.multiple_of(big * 192, 64)
        grads = split_tiles(dyrow[pl.ds(base_row + base, 192), :].astype(F32))
        outs = []
        for c in range(3):
            rows = pl.ds(base + c * 64, 64)
            mask = msk[rows, :]
            outs.append(m1s[rows, :] + mask * (tmp[rows, :] + vrow(10)))
            dout = xs[rows, :]
            normal = n2s[rows, :]
            dmid = grads[c] + norm_back(dout, normal, r2s[rows, :], vrow(8))
            m1s[rows, :] = dmid
            low = (dmid * mask).astype(BF16)
            das[rows, :] = low
            sums[0] = sums[0] + row_sums(dout * normal)
            sums[1] = sums[1] + row_sums(dout)
            sums[2] = sums[2] + row_sums(low.astype(F32))
            sums[3] = sums[3] + row_sums(dms[rows, :].astype(F32))
        orow[pl.ds(base_row + base, 192), :] = join_tiles(outs).astype(BF16)
        return tuple(sums)

    sums = lax.fori_loop(0, 3, middle_rows, (zero_rows,) * 4)
    add_small(8, sums[0])
    add_small(9, sums[1])
    add_small(7, sums[2])
    add_small(10, sums[3])
    go[...] += contract(ctxs[...], das[...], 0, 0)
    dcs[...] = contract(das[...], wo[...], 1, 1).astype(BF16)

    def attend_back(t, sums):
        rows = pl.ds(pl.multiple_of(t * 64, 64), 64)
        keys = pl.ds(pl.multiple_of(t * KEYS_TILE, KEYS_TILE), KEYS_TILE)
        probs = ps[rows, :]
        upper = dcs[rows, :]
        dprobs = contract(upper, spread(vs, t), 1, 1)
        inner = group_all(dprobs * probs, jnp.add)
        dz = (probs * (dprobs - inner)).astype(BF16)
        dq = (
            jnp.dot(dz, spread(ks, t), preferred_element_type=F32) * score_scale
        ).astype(BF16)
        dqs[rows, :] = dq
        dk = gather_heads(contract(dz, qs[rows, :], 0, 0)) * score_scale
        dks[keys, :] = dk.astype(BF16)
        dv = gather_heads(contract(probs.astype(BF16), upper, 0, 0)).astype(BF16)
        dvs[keys, :] = dv
        return (sums[0] + row_sums(dq.astype(F32)), sums[1] + row_sums(dv.astype(F32)))

    sums = lax.fori_loop(0, TILES, attend_back, (zero_rows,) * 2, unroll=3)
    add_small(2, sums[0])
    add_small(3, sums[1])
    gq[...] += contract(h1s[...], dqs[...], 0, 0)
    gk[...] += contract(kin[...], dks[...], 0, 0)
    gv[...] += contract(kin[...], dvs[...], 0, 0)
    dout = contract(dks[...], wk[...], 1, 1) + contract(dvs[...], wv[...], 1, 1)
    normal = nks[...]
    ds = norm_back(dout, normal, rks[...], vrow(5)).astype(BF16)
    add_small(5, row_sums(dout * normal))
    add_small(6, row_sums(dout))
    add_small(4, row_sums(ds.astype(F32)))
    for d in range(4):
        rows = slice(d * KEYS, (d + 1) * KEYS)
        wide_rows = slice(d * width, (d + 1) * width)
        gr[wide_rows, :] += contract(pats[rows, :], ds, 0, 0)
        dps[rows, :] = contract(ds, wr[wide_rows, :], 1, 1).astype(BF16)
    tmp[...] = contract(pick[...], dps[...], 0, 0)
    xs[...] = contract(dqs[...], wq[...], 1, 1)

    def last_rows(big, sums):
        sums = list(sums)
        base = pl.multiple_of(big * 192, 64)
        outs = []
        for c in range(3):
            rows = pl.ds(base + c * 64, 64)
            dout = xs[rows, :] + msk[rows, :] * tmp[rows, :]
            normal = n1s[rows, :]
            outs.append(m1s[rows, :] + norm_back(dout, normal, r1s[rows, :], vrow(0)))
            sums[0] = sums[0] + row_sums(dout * normal)
            sums[1] = sums[1] + row_sums(dout)
        grow[pl.ds(base_row + base, 192), :] = join_tiles(outs)
        return tuple(sums)

    sums = lax.fori_loop(0, 3, last_rows, (zero_rows,) * 2)
    add_small(0, sums[0])
    add_small(1, sums[1])

    @pl.when(part == per - 1)
    def _():
        for c in range(spans):
            cols = slice(c * LANES, (c + 1) * LANES)
            out_ref[0, :, cols] = jnp.transpose(orow[cols, :].astype(F32)).astype(BF16)
            gin_ref[0, :, cols] = jnp.transpose(grow[cols, :])

    @pl.when(g == pl.num_programs(0) - 1)
    def _():
        rotate(
            order, gq, gk, gv, go, gup, gr, gdn, gsm, gwd, la, ra, lb, rb, wire,
            codes, rows_m, mas, mbs, flat, per_block,
        )


def rotate(
    order, gq, gk, gv, go, gup, gr, gdn, gsm, gwd, la, ra, lb, rb, wire,
    codes, rows_m, ras, rbs, flat, per_block,
):
    width, hidden = gup.shape
    fill_codes(la, ra, lb, rb, codes, width)

    def dot(left, right):
        return jnp.dot(left, right, preferred_element_type=F32)

    for k, parts in enumerate(((gq,), (gk, gv), (go,), (gup,))):
        first, count = SPANS_A[k]
        right = lane_matrix(codes, 6 + k, count * width)
        total = None
        depth = right.shape[0] // len(parts)
        for p, part in enumerate(parts):
            piece = dot(part[...].astype(BF16), right[p * depth : (p + 1) * depth])
            total = piece if total is None else total + piece
        row_matrix(codes, k, rows_m, width)
        ras[:, first * width : (first + count) * width] = dot(rows_m[0:width, 0:width], total.astype(BF16))
    row_matrix(codes, 4, rows_m, hidden)
    part = dot(rows_m[...], gr[...].astype(BF16)).astype(BF16)
    rbs[:, 0:width] = dot(part, lane_matrix(codes, 10, width))
    row_matrix(codes, 5, rows_m, hidden)
    part = contract(rows_m[...], gdn[...].astype(BF16), 1, 1).astype(BF16)
    rbs[:, width : 2 * width] = dot(part, lane_matrix(codes, 11, width))
    count, tall, _ = wire.shape
    half = count // 2
    depth = 2 * flat.shape[0] // count
    for first, (source, rows) in enumerate(((ras, width), (rbs, hidden))):
        per_row = source.shape[1] // LANES
        for j in range(per_row):
            cols = slice(j * LANES, (j + 1) * LANES)
            flat[pl.ds(j, rows, stride=per_row), :] = source[:, cols]

        def place(t, carry, first=first):
            spot = order[t] - first * half

            @pl.when((spot >= 0) & (spot < half))
            def _():
                wire[t, 0:depth, :] = flat[pl.ds(spot * depth, depth), :].astype(BF16)
                wire[t, depth:tall, :] = jnp.zeros((tall - depth, LANES), BF16)

            return carry

        lax.fori_loop(0, count, place, 0)
    for number, (kind, k, col, size) in enumerate(vector_spots(width, hidden)):
        block, row = number // per_block, depth + number % per_block
        source = (gsm, gwd)[kind]
        wire[block, row : row + 1, 0:size] = source[k : k + 1, col : col + size].astype(BF16)


def pick_matrix():
    spot = lax.broadcasted_iota(jnp.int32, (SLOTS, SLOTS), 0)
    lane = lax.broadcasted_iota(jnp.int32, (SLOTS, SLOTS), 1)
    part = spot // KEYS
    key = spot - part * KEYS
    tile = key >> 4
    inner = key & 15
    row = 2 * (inner >> 2) + (part >> 1)
    col = 2 * (inner & 3) + (part & 1)
    return jnp.where(tile * 64 + row * TILE + col == lane, 1.0, 0.0).astype(BF16)


def head_mask(width):
    row = lax.broadcasted_iota(jnp.int32, (8 * KEYS_TILE, width), 0) >> 4
    col = lax.broadcasted_iota(jnp.int32, (8 * KEYS_TILE, width), 1) >> 6
    return jnp.where(row == col, 1.0, 0.0).astype(BF16)


def run_block(
    tokens, grad_output, valid_tiles, master_a, master_b, vector_params, order, la, ra, lb, rb
):
    width = tokens.shape[2]
    hidden = master_b.shape[0]
    rows = tokens.shape[1]
    per = rows // SLOTS
    grids = tokens.shape[0] * per
    flags = valid_tiles.reshape(grids, TILES)
    blocks = order.shape[0]
    per_block = -(-VECTOR_ROWS // blocks)
    total = (master_a.size + master_b.size) // LANES
    tall_block = -(-(total // blocks + per_block) // 32) * 32
    flip = pl.BlockSpec((1, width, rows), lambda g: (g // per, 0, 0))
    tall = (SLOTS, width)
    keys = (KEYS, width)
    scratch = [((width, width), BF16)] * 4 + [
        ((width, hidden), BF16),
        ((hidden, width), BF16),
        ((hidden, width), BF16),
        ((16, hidden), F32),
        ((SLOTS, SLOTS), BF16),
        ((8 * KEYS_TILE, width), BF16),
    ]
    scratch += [((width, width), F32)] * 4 + [
        ((width, hidden), F32),
        ((hidden, width), F32),
        ((width, hidden), F32),
        ((16, width), F32),
        ((16, hidden), F32),
        (master_a.shape, F32),
        (master_b.shape, F32),
        None,
        ((rows, width), BF16),
        ((rows, width), BF16),
        ((rows, width), BF16),
        ((rows, width), F32),
        ((16, hidden), jnp.int32),
        ((hidden, hidden), BF16),
        ((total // 2, LANES), F32),
    ]
    scratch += [
        (tall, F32),
        (tall, F32),
        (tall, F32),
        ((SLOTS, 1), F32),
        (tall, BF16),
        (tall, BF16),
        (tall, BF16),
        (tall, BF16),
        (keys, BF16),
        (keys, F32),
        ((KEYS, 1), F32),
        (keys, BF16),
        (keys, BF16),
        ((SLOTS, LANES), F32),
        (tall, BF16),
        (tall, F32),
        (tall, F32),
        (tall, F32),
        ((SLOTS, 1), F32),
        (tall, BF16),
        ((SLOTS, hidden), F32),
        ((SLOTS, hidden), F32),
        ((SLOTS, hidden), BF16),
        ((SLOTS, hidden), BF16),
        (tall, BF16),
        (tall, BF16),
        (tall, BF16),
        (tall, BF16),
        (keys, BF16),
        (keys, BF16),
        (tall, BF16),
    ]
    smem = pl.BlockSpec(memory_space=pltpu.SMEM)
    anywhere = pl.BlockSpec(memory_space=pl.ANY)

    def whole(shape):
        return pl.BlockSpec(shape, lambda g: (0,) * len(shape), pipeline_mode=pl.Buffered(1))

    small = (vector_params, la, ra.reshape(1, -1), lb, rb.reshape(1, -1))
    out, gin, wire = pl.pallas_call(
        functools.partial(block_kernel, per=per, per_block=per_block),
        name="block_step",
        grid=(grids,),
        in_specs=[smem, smem, flip, flip, anywhere, anywhere] + [whole(c.shape) for c in small],
        out_specs=[flip, flip, whole((blocks, tall_block, LANES))],
        out_shape=[
            jax.ShapeDtypeStruct((tokens.shape[0], width, rows), BF16),
            jax.ShapeDtypeStruct((tokens.shape[0], width, rows), F32),
            jax.ShapeDtypeStruct((blocks, tall_block, LANES), BF16),
        ],
        scratch_shapes=[
            pltpu.SemaphoreType.DMA((2,)) if item is None else pltpu.VMEM(*item)
            for item in scratch
        ],
        compiler_params=pltpu.CompilerParams(vmem_limit_bytes=67_000_000),
    )(
        flags,
        order,
        jnp.transpose(tokens, (0, 2, 1)),
        jnp.transpose(grad_output, (0, 2, 1)),
        master_a,
        master_b,
        *small,
    )
    return jnp.transpose(out, (0, 2, 1)), jnp.transpose(gin, (0, 2, 1)), wire

SPANS_A = ((0, 1), (1, 2), (3, 1), (4, 4))
VECTOR_ROWS = 143


def fill_codes(la, ra, lb, rb, codes, width):
    hidden = lb.shape[1]
    codes[...] = jnp.full(codes.shape, -2, jnp.int32)
    codes[0:4, 0:width] = la[...]
    codes[4:6, 0:hidden] = lb[...]
    for k, (first, count) in enumerate(SPANS_A):
        start = first * width
        span = count * width
        codes[6 + k : 7 + k, 0:span] = ra[:, start : start + span] - 2 * start
    for k in range(2):
        codes[10 + k : 11 + k, 0:width] = rb[:, k * width : (k + 1) * width] - 2 * k * width


def lane_matrix(codes, k, size):
    code = codes[k : k + 1, 0:size]
    sign = (1 - 2 * (code & 1)).astype(F32)
    spot = lax.broadcasted_iota(jnp.int32, (size, size), 0)
    return jnp.where(spot == (code >> 1), sign, 0.0).astype(BF16)


def row_matrix(codes, k, out, size):
    for start in range(0, size, LANES):
        code = codes[k : k + 1, start : start + LANES]
        spot = jnp.transpose(jnp.broadcast_to((code >> 1).astype(F32), (LANES, LANES)))
        sign = jnp.transpose(
            jnp.broadcast_to((1 - 2 * (code & 1)).astype(F32), (LANES, LANES))
        )
        for col in range(0, size, LANES):
            lane = lax.broadcasted_iota(jnp.int32, (LANES, LANES), 1).astype(F32) + col
            part = jnp.where(spot == lane, sign, 0.0).astype(BF16)
            out[start : start + LANES, col : col + LANES] = part


def vector_spots(width, hidden):
    spots = []
    for k in range(11):
        for col in range(0, width, LANES):
            spots.append((0, k, col, min(LANES, width - col)))
    for k in range(11):
        for col in range(0, hidden, LANES):
            spots.append((1, k, col, LANES))
    return spots


def restore_kernel(
    blocks, order, la, ra, lb, rb, steps, ma, mb, vp, vf, vsec,
    na, nb, ca, cb, vg, vfn, vsn, nv,
    codes, rows_m, das, dbs, flat, wide_s, per_block,
):
    width = ma.shape[0]
    hidden = mb.shape[0]
    fill_codes(la, ra, lb, rb, codes, width)
    count = blocks.shape[0]
    depth = flat.shape[0] // count

    def place(t, carry):
        flat[pl.ds(order[t] * depth, depth), :] = blocks[t, 0:depth, :].astype(F32)
        return carry

    lax.fori_loop(0, count, place, 0)
    per_row = ma.shape[1] // LANES
    for j in range(per_row):
        das[:, j * LANES : (j + 1) * LANES] = flat[pl.ds(j, width, stride=per_row), :]
    base = width * per_row
    per_row = mb.shape[1] // LANES
    for j in range(per_row):
        dbs[:, j * LANES : (j + 1) * LANES] = flat[pl.ds(base + j, hidden, stride=per_row), :]

    def dot(left, right):
        return jnp.dot(left, right, preferred_element_type=F32)

    def update(master, step, new, copy, cols):
        old = master[:, cols]
        value = old - matrix_rate * (step + weight_decay * old)
        new[:, cols] = value
        copy[:, cols] = value.astype(BF16)

    for k, (first, span) in enumerate(SPANS_A):
        size = span * width
        cols = slice(first * width, first * width + size)
        part = dot(lane_matrix(codes, k, width), das[:, cols].astype(BF16)).astype(BF16)
        row_matrix(codes, 6 + k, rows_m, size)
        update(ma, dot(part, rows_m[0:size, 0:size]), na, ca, cols)
    for k in range(2):
        cols = slice(k * width, (k + 1) * width)
        part = dot(lane_matrix(codes, 4 + k, hidden), dbs[:, cols].astype(BF16)).astype(BF16)
        row_matrix(codes, 10 + k, rows_m, width)
        update(mb, dot(part, rows_m[0:width, 0:width]), nb, cb, cols)
    for number, (kind, k, col, size) in enumerate(vector_spots(width, hidden)):
        block, row = number // per_block, depth + number % per_block
        value = blocks[block, row : row + 1, 0:size].astype(F32)
        if kind == 0:
            vg[k : k + 1, col : col + size] = value
        else:
            wide_s[k : k + 1, col : col + size] = value
    ratio = hidden // width
    for k in range(11):
        for q in range(ratio):
            row = 11 + ratio * k + q
            vg[row : row + 1, :] = wide_s[k : k + 1, q * width : (q + 1) * width]
    grad = vg[...]
    first_new = beta_one * vf[...] + (1.0 - beta_one) * grad
    second_new = beta_two * vsec[...] + (1.0 - beta_two) * grad * grad
    vfn[...] = first_new
    vsn[...] = second_new
    move = direction_of(first_new, second_new, steps[0])
    old = vp[...]
    nv[...] = old - vector_rate * (move + weight_decay * old)


def direction_of(first_new, second_new, steps):
    count = jnp.full((1, LANES), steps, jnp.int32).astype(F32)
    log_one = -0.10536051565782628
    log_two = -0.0010005003335835335
    one = (1.0 / (1.0 - jnp.exp(count * log_one)))[:, 0:1]
    two = (1.0 / (1.0 - jnp.exp(count * log_two)))[:, 0:1]
    return first_new * one / (jnp.sqrt(second_new * two) + adam_epsilon)


def vmem_spec():
    return pl.BlockSpec(memory_space=pltpu.VMEM)


def restore_blocks(blocks, order, la, ra, lb, rb, steps, ma, mb, vp, vf, vsec):
    width = ma.shape[0]
    hidden = mb.shape[0]
    per_block = -(-VECTOR_ROWS // blocks.shape[0])
    total = (ma.size + mb.size) // LANES
    smem = pl.BlockSpec(memory_space=pltpu.SMEM)
    return pl.pallas_call(
        functools.partial(restore_kernel, per_block=per_block),
        name="restore",
        in_specs=[vmem_spec(), smem] + [vmem_spec()] * 4 + [smem] + [vmem_spec()] * 5,
        out_specs=[vmem_spec()] * 8,
        out_shape=[
            jax.ShapeDtypeStruct(ma.shape, F32),
            jax.ShapeDtypeStruct(mb.shape, F32),
            jax.ShapeDtypeStruct(ma.shape, BF16),
            jax.ShapeDtypeStruct(mb.shape, BF16),
        ]
        + [jax.ShapeDtypeStruct(vp.shape, F32)] * 4,
        scratch_shapes=[
            pltpu.VMEM((16, hidden), jnp.int32),
            pltpu.VMEM((hidden, hidden), BF16),
            pltpu.VMEM((width, 8 * width), F32),
            pltpu.VMEM((hidden, 2 * width), F32),
            pltpu.VMEM((total, LANES), F32),
            pltpu.VMEM((16, hidden), F32),
        ],
        compiler_params=pltpu.CompilerParams(vmem_limit_bytes=60 << 20),
    )(blocks, order, la, ra.reshape(1, -1), lb, rb.reshape(1, -1), steps, ma, mb, vp, vf, vsec)


def exchange_kernel(wire, first, second, steps, grad, first_new, second_new, every, *scratch,
                    plan, bits, depth):
    buffers = []
    spot = 0
    for _, _, order in plan:
        buffers.append(scratch[spot : spot + len(order)])
        spot += len(order)
    rs_send, rs_recv, ag_send, ag_recv = scratch[spot:]
    tok = lax.axis_index("tok")
    side = lax.axis_index("ch")

    def mine(axis):
        return side if axis == "ch" else lax.rem(lax.div(tok, 2**axis), 2)

    def peer(axis):
        if axis == "ch":
            return {"ch": 1 - side}
        return {"tok": tok + 2**axis - 2 ** (axis + 1) * mine(axis)}

    axes = [*reversed(range(bits)), "ch"]
    barrier = pltpu.get_barrier_semaphore()
    for axis in axes:
        pl.semaphore_signal(barrier, inc=1, device_id=peer(axis), device_id_type=pl.DeviceIdType.MESH)
    pl.semaphore_wait(barrier, len(axes))

    chunks = range(len(plan))
    left = [list(axes) for _ in chunks]
    held = [wire for _ in chunks]
    pending = []

    def region(c, choice):
        index = tuple(choice(axis) for axis in left[c])
        start, size, _ = plan[c]
        rows = pl.ds(start, size) if held[c] is wire else slice(None)
        return index + (rows, slice(None))

    def scatter_start(c, s):
        axis = plan[c][2][s]
        index = region(c, lambda a: 1 - mine(a) if a == axis else slice(None))
        copy = pltpu.make_async_remote_copy(
            held[c].at[index], buffers[c][s], rs_send.at[c, s], rs_recv.at[c, s],
            device_id=peer(axis), device_id_type=pl.DeviceIdType.MESH,
        )
        copy.start()
        pending.append(copy)
        return copy

    def scatter_keep(c, s):
        axis = plan[c][2][s]
        return held[c][region(c, lambda a: mine(a) if a == axis else slice(None))]

    def gather_start(c, s):
        start, size, order = plan[c]
        axis = order[len(order) - 1 - s]
        done = order[len(order) - s :]
        index = tuple(slice(None) if a in done else mine(a) for a in axes)
        piece = every.at[index + (pl.ds(start, size), slice(None))]
        copy = pltpu.make_async_remote_copy(
            piece, piece, ag_send.at[c, s], ag_recv.at[c, s],
            device_id=peer(axis), device_id_type=pl.DeviceIdType.MESH,
        )
        copy.start()
        pending.append(copy)
        return copy

    stages = len(axes)
    flying = [scatter_start(c, 0) for c in chunks]
    for s in range(stages):
        for c in chunks:
            start, size, order = plan[c]
            flying[c].wait_recv()
            kept = scatter_keep(c, s)
            buffer = buffers[c][s]
            if s < stages - 1:
                buffer[...] = buffer[...] + kept
                left[c].remove(order[s])
                held[c] = buffer
                flying[c] = scatter_start(c, s + 1)
                continue
            total = buffer[...].astype(F32) + kept.astype(F32)
            count = max(0, min(depth - start, size))
            parts = []
            if count:
                rows = slice(start, start + count)
                owned = total[:count]
                grad[rows, :] = owned
                one = beta_one * first[rows, :] + (1.0 - beta_one) * owned
                two = beta_two * second[rows, :] + (1.0 - beta_two) * owned * owned
                first_new[rows, :] = one
                second_new[rows, :] = two
                parts.append(direction_of(one, two, steps[0]))
            if count < size:
                parts.append(total[count:])
            ready = parts[0] if len(parts) == 1 else jnp.concatenate(parts, axis=0)
            own = tuple(mine(a) for a in axes)
            every[own + (slice(start, start + size), slice(None))] = ready.astype(BF16)
            flying[c] = gather_start(c, 0)
    for s in range(stages):
        for c in chunks:
            flying[c].wait_recv()
            if s < stages - 1:
                flying[c] = gather_start(c, s + 1)
    for copy in pending:
        copy.wait_send()


def exchange_blocks(wire, first, second, steps, bits):
    count, tall, _ = wire.shape
    depth = first.shape[0]
    units = tall // 16
    small = max(1, units * 6 // 26)
    large = (units - small + 1) // 2
    rest = list(range(2, bits))
    sizes = (small, large, units - small - large)
    orders = ([0] + rest + ["ch", 1], [0, "ch", 1] + rest, [0, 1, "ch"] + rest)
    plan = []
    start = 0
    for size, order in zip(sizes, orders):
        plan.append((start, size * 16, order))
        start += size * 16
    scratch = []
    for _, size, order in plan:
        for s in range(len(order)):
            scratch.append(pltpu.VMEM((2,) * (len(order) - 1 - s) + (size, LANES), BF16))
    for _ in range(4):
        scratch.append(pltpu.SemaphoreType.DMA((len(plan), bits + 1)))
    shape = (2,) * (bits + 1) + (tall, LANES)
    block = jax.ShapeDtypeStruct((depth, LANES), F32)
    grad, first_new, second_new, every = pl.pallas_call(
        functools.partial(exchange_kernel, plan=plan, bits=bits, depth=depth),
        name="exchange",
        in_specs=[vmem_spec()] * 3 + [pl.BlockSpec(memory_space=pltpu.SMEM)],
        out_specs=[vmem_spec()] * 4,
        out_shape=[block, block, block, jax.ShapeDtypeStruct(shape, BF16)],
        scratch_shapes=scratch,
        compiler_params=pltpu.CompilerParams(
            vmem_limit_bytes=60 << 20, collective_id=0, has_side_effects=True
        ),
    )(wire.reshape(shape), first, second, steps)
    return grad, first_new, second_new, every.reshape(wire.shape)


def on_device(
    tokens, grad_output, valid_tiles, master_a, master_b, vector_params, matrix_first,
    matrix_second, vector_first, vector_second, left_a, right_a, left_b, right_b,
    owner_list, step_count, bits,
):
    out, grad_in, wire = run_block(
        tokens, grad_output, valid_tiles, master_a, master_b, vector_params, owner_list,
        left_a, right_a, left_b, right_b,
    )
    shape = matrix_first.shape
    grad, first_new, second_new, every = exchange_blocks(
        wire, matrix_first.reshape(-1, LANES), matrix_second.reshape(-1, LANES), step_count, bits
    )
    restored = restore_blocks(
        every, owner_list, left_a, right_a, left_b, right_b, step_count,
        master_a, master_b, vector_params, vector_first, vector_second,
    )
    return (
        out,
        grad_in,
        grad.reshape(shape),
        first_new.reshape(shape),
        second_new.reshape(shape),
        *restored,
    )


def solution(mesh):
    bits = mesh.shape["tok"].bit_length() - 1
    part = P(None, ("tok", "ch"), None)
    owned = P(("tok", "ch"), None)
    in_specs = (part,) * 3 + (P(),) * 3 + (owned,) * 2 + (P(),) * 8
    out_specs = (part,) * 2 + (owned,) * 3 + (P(),) * 8
    return jax.shard_map(
        functools.partial(on_device, bits=bits), mesh=mesh, in_specs=in_specs, out_specs=out_specs, check_vma=False
    )
```

```python
import functools

import jax
import jax.numpy as jnp
from jax import lax
from jax.experimental import pallas as pl
from jax.experimental.pallas import tpu as pltpu
from jax.sharding import PartitionSpec as P

HEADS = 5
HEAD_DIM = 64
SIDE = 24
TILE = 8
TILES = 9
SLOTS = 576
KEYS = 144
LANES = 128
KEYS_TILE = 16

beta_one = 0.9
beta_two = 0.999
adam_epsilon = 1e-08
norm_epsilon = 1e-05
matrix_rate = 0.05
vector_rate = 0.2
weight_decay = 0.01

F32 = jnp.float32
BF16 = jnp.bfloat16


def contract(left, right, left_dim, right_dim):
    return lax.dot_general(
        left, right, (((left_dim,), (right_dim,)), ((), ())), preferred_element_type=F32
    )


def normalize(values):
    scale = 1.0 / values.shape[-1]
    center = values - jnp.sum(values, axis=-1, keepdims=True) * scale
    inverse = lax.rsqrt(jnp.sum(center * center, axis=-1, keepdims=True) * scale + norm_epsilon)
    return center * inverse, inverse


def norm_back(upstream, normal, inverse, gain):
    scale = 1.0 / upstream.shape[-1]
    scaled = upstream * gain
    inner = jnp.sum(scaled * normal, axis=-1, keepdims=True) * scale
    mean = jnp.sum(scaled, axis=-1, keepdims=True) * scale
    return inverse * (scaled - mean - normal * inner)


def row_sums(values):
    rows, cols = values.shape
    return jnp.sum(values.reshape(rows // 8, 8, cols), axis=0)


def by_head(values):
    return values.reshape(HEADS, KEYS_TILE, values.shape[1])


def split_tiles(rows):
    shaped = rows.reshape(TILE, 3, TILE, rows.shape[1])
    return [shaped[:, c].reshape(TILE * TILE, rows.shape[1]) for c in range(3)]


def join_tiles(tiles):
    return jnp.concatenate(
        [tiles[c][i * TILE : (i + 1) * TILE] for i in range(TILE) for c in range(3)], axis=0
    )


def gelu_parts(e):
    gauss = jnp.exp2((-0.5 * 1.4426950408889634) * (e * e))
    size = jnp.abs(e)
    t = 1.0 / (1.0 + (0.3275911 * 0.7071067811865476) * size)
    poly = t * (
        0.5 * 0.254829592
        + t
        * (
            0.5 * -0.284496736
            + t * (0.5 * 1.421413741 + t * (0.5 * -1.453152027 + t * (0.5 * 1.061405429)))
        )
    )
    tail = poly * gauss
    phi = jnp.where(e >= 0.0, 1.0 - tail, tail)
    return phi, gauss * 0.3989422804014327


def block_kernel(
    flags,
    order,
    x_ref,
    dy_ref,
    ma,
    mb,
    vec,
    la,
    ra,
    lb,
    rb,
    out_ref,
    gin_ref,
    wire,
    wq,
    wk,
    wv,
    wo,
    wup,
    wr,
    wdn,
    wide,
    pick,
    hmask,
    gq,
    gk,
    gv,
    go,
    gup,
    gr,
    gdn,
    gsm,
    gwd,
    mas,
    mbs,
    sems,
    xrow,
    dyrow,
    orow,
    grow,
    codes,
    rows_m,
    flat,
    msk,
    xs,
    n1s,
    r1s,
    h1s,
    hms,
    qs,
    pats,
    kin,
    nks,
    rks,
    ks,
    vs,
    ps,
    ctxs,
    tmp,
    m1s,
    n2s,
    r2s,
    h2s,
    dmt,
    h2t,
    acc,
    u_a,
    d_a,
    hid_a,
    du_a,
    u_b,
    d_b,
    hid_b,
    du_b,
    dms,
    das,
    dcs,
    dqs,
    dks,
    dvs,
    dps,
    *,
    per,
    per_block,
):
    g = pl.program_id(0)
    part = lax.rem(g, per)
    width = x_ref.shape[1]
    hidden = wup.shape[1]
    spans = x_ref.shape[2] // LANES
    base_row = part * SLOTS
    load_a = pltpu.make_async_copy(ma, mas, sems.at[0])
    load_b = pltpu.make_async_copy(mb, mbs, sems.at[1])

    @pl.when(g == 0)
    def _():
        load_a.start()
        load_b.start()
        pick[...] = pick_matrix()
        hmask[...] = head_mask(width)
        ratio = hidden // width
        for k in range(11):
            for q in range(ratio):
                row = 11 + ratio * k + q
                wide[k : k + 1, q * width : (q + 1) * width] = vec[row : row + 1, :]
        for ref in (gq, gk, gv, go, gup, gr, gdn, gsm, acc):
            ref[...] = jnp.zeros(ref.shape, F32)

    @pl.when(part == 0)
    def _():
        for c in range(spans):
            cols = slice(c * LANES, (c + 1) * LANES)
            xrow[cols, :] = jnp.transpose(x_ref[0, :, cols].astype(F32)).astype(BF16)
            dyrow[cols, :] = jnp.transpose(dy_ref[0, :, cols].astype(F32)).astype(BF16)

    row = lax.broadcasted_iota(jnp.int32, (TILE * TILE, width), 0)
    inside = jnp.where((row % TILE < TILE - 1) & (row < TILE * (TILE - 1)), 1.0, 0.0)
    for t in range(TILES):
        msk[t * 64 : (t + 1) * 64, :] = inside * flags[g, t].astype(F32)

    def vrow(number):
        return vec[number : number + 1, :]

    def add_small(number, sums):
        gsm[number : number + 1, :] += jnp.sum(sums, axis=0, keepdims=True)

    zero_rows = jnp.zeros((8, width), F32)

    def first_norm(big, carry):
        base = pl.multiple_of(big * 192, 64)
        tiles = split_tiles(xrow[pl.ds(base_row + base, 192), :].astype(F32))
        grads = split_tiles(dyrow[pl.ds(base_row + base, 192), :].astype(F32))
        for c in range(3):
            rows = pl.ds(base + c * 64, 64)
            normal, inverse = normalize(tiles[c])
            xs[rows, :] = tiles[c]
            n1s[rows, :] = normal
            r1s[rows, :] = inverse
            low = (normal * vrow(0) + vrow(1)).astype(BF16)
            h1s[rows, :] = low
            mask = msk[rows, :]
            hms[rows, :] = (low.astype(F32) * mask).astype(BF16)
            dms[rows, :] = (grads[c] * mask).astype(BF16)
        return carry

    lax.fori_loop(0, 3, first_norm, 0)

    @pl.when(g == 0)
    def _():
        load_a.wait()
        for k, ref in enumerate((wq, wk, wv, wo)):
            ref[...] = mas[:, k * width : (k + 1) * width].astype(BF16)
        wup[...] = mas[:, 4 * width :].astype(BF16)
        load_b.wait()
        wr[...] = mbs[:, :width].astype(BF16)
        wdn[...] = mbs[:, width:].astype(BF16)

    qs[...] = (jnp.dot(h1s[...], wq[...], preferred_element_type=F32) + vrow(2)).astype(BF16)
    pats[...] = jnp.dot(pick[...], hms[...], preferred_element_type=F32).astype(BF16)
    reduced = vrow(4)
    for d in range(4):
        reduced = reduced + jnp.dot(
            pats[d * KEYS : (d + 1) * KEYS, :],
            wr[d * width : (d + 1) * width, :],
            preferred_element_type=F32,
        )
    normal, inverse = normalize(reduced)
    nks[...] = normal
    rks[...] = inverse
    kin[...] = (normal * vrow(5) + vrow(6)).astype(BF16)
    ks[...] = jnp.dot(kin[...], wk[...], preferred_element_type=F32).astype(BF16)
    vs[...] = (jnp.dot(kin[...], wv[...], preferred_element_type=F32) + vrow(3)).astype(BF16)
    score_scale = HEAD_DIM ** (-0.5)

    def spread(ref, t):
        part = ref[pl.ds(pl.multiple_of(t * KEYS_TILE, KEYS_TILE), KEYS_TILE), :]
        return jnp.concatenate([part] * HEADS, axis=0) * hmask[...]

    def gather_heads(big):
        big = by_head(big * hmask[...].astype(F32))
        return jnp.sum(big, axis=0)

    def attend_tile(t, carry):
        rows = pl.ds(pl.multiple_of(t * 64, 64), 64)
        scores = by_head(contract(spread(ks, t), qs[rows, :], 1, 1) * score_scale)
        exped = jnp.exp(scores - jnp.max(scores, axis=1, keepdims=True))
        probs = exped * (1.0 / jnp.sum(exped, axis=1, keepdims=True))
        probs = probs.reshape(HEADS * KEYS_TILE, 64)
        ps[pl.ds(pl.multiple_of(t * 80, 16), 80), :] = probs
        ctxs[rows, :] = contract(probs.astype(BF16), spread(vs, t), 0, 0).astype(BF16)
        return carry

    lax.fori_loop(0, TILES, attend_tile, 0, unroll=3)
    tmp[...] = jnp.dot(ctxs[...], wo[...], preferred_element_type=F32)

    def second_norm(t, carry):
        rows = pl.ds(pl.multiple_of(t * 64, 64), 64)
        middle = xs[rows, :] + msk[rows, :] * (tmp[rows, :] + vrow(7))
        m1s[rows, :] = middle
        normal, inverse = normalize(middle)
        n2s[rows, :] = normal
        r2s[rows, :] = inverse
        h2s[rows, :] = (normal * vrow(8) + vrow(9)).astype(BF16)
        return carry

    lax.fori_loop(0, TILES, second_norm, 0, unroll=3)
    for r in range(3):
        rows = slice(r * 192, (r + 1) * 192)
        dmt[r] = jnp.transpose(dms[rows, :])
        h2t[r] = jnp.transpose(h2s[rows, :])
    for ref in (tmp, xs):
        ref[...] = jnp.zeros(ref.shape, F32)
    for ref in (hid_b, du_b):
        ref[...] = jnp.zeros(ref.shape, BF16)

    def spots(step):
        group = lax.div(step, 3)
        big = step - group * 3
        return big, pl.ds(pl.multiple_of(big * 192, 64), 192), pl.ds(
            pl.multiple_of(group * 256, 256), 256
        )

    def feed(step, u_ref, d_ref):
        big, rows, cols = spots(step)

        def up():
            u_ref[...] = jnp.dot(h2s[rows, :], wup[:, cols], preferred_element_type=F32)

        def down():
            d_ref[...] = contract(dms[rows, :], wdn[cols, :], 1, 1)

        return [up, down]

    def drain(step, hid_ref, du_ref):
        big, rows, cols = spots(step)

        def one():
            tmp[rows, :] += jnp.dot(hid_ref[...], wdn[cols, :], preferred_element_type=F32)

        def two():
            xs[rows, :] += contract(du_ref[...], wup[:, cols], 1, 1)

        def three():
            gdn[:, cols] += jnp.dot(dmt[big], hid_ref[...], preferred_element_type=F32)

        def four():
            gup[:, cols] += jnp.dot(h2t[big], du_ref[...], preferred_element_type=F32)

        return [one, two, three, four]

    def mix(step, u_ref, d_ref, hid_ref, du_ref, extras):
        big = lax.rem(step, 3)
        extras = list(extras)
        for lane in range(2):
            local = slice(lane * LANES, (lane + 1) * LANES)
            cols = pl.ds(
                pl.multiple_of(lax.div(step, 3) * 256 + lane * LANES, LANES), LANES
            )
            bias_up = wide[0:1, cols]
            bias_dw = wide[1:2, cols]
            taps = [wide[2 + k : 3 + k, cols] for k in range(9)]
            sums = [jnp.zeros((8, LANES), F32)] * 11
            for c in range(3):
                rows = slice(c * 64, (c + 1) * 64)
                mask = msk[pl.ds(pl.multiple_of(big * 192 + c * 64, 64), 64), 0:LANES]
                sums = mix_unit(
                    u_ref, d_ref, hid_ref, du_ref, rows, local, mask, bias_up, bias_dw, taps, sums
                )
                if extras:
                    extras.pop(0)()
            for k in range(11):
                acc[k * 8 : (k + 1) * 8, cols] += sums[k]
        for extra in extras:
            extra()

    def mix_unit(
        u_ref, d_ref, hid_ref, du_ref, rows, local, mask, bias_up, bias_dw, taps, sums
    ):
        sums = list(sums)
        ups = (u_ref[rows, local] + bias_up) * mask
        mid = [ups[i * 8 : (i + 1) * 8] for i in range(7)]
        shifted = [
            [pltpu.roll(v, 1, 0) for v in mid],
            mid,
            [pltpu.roll(v, 7, 0) for v in mid],
        ]
        grads = d_ref[rows, local]
        hid_rows = []
        de_rows = []
        for i in range(7):
            e = bias_dw
            for a in range(3):
                if 0 <= i + a - 1 < 7:
                    for b in range(3):
                        e = e + taps[3 * a + b] * shifted[b][i + a - 1]
            phi, gauss = gelu_parts(e)
            hid_rows.append(e * phi)
            de = grads[i * 8 : (i + 1) * 8] * (phi + e * gauss)
            de_rows.append(de)
            sums[1] = sums[1] + de
            for a in range(3):
                if 0 <= i + a - 1 < 7:
                    for b in range(3):
                        k = 2 + 3 * a + b
                        sums[k] = sums[k] + de * shifted[b][i + a - 1]
        zero = jnp.zeros((8, LANES), F32)
        hid_ref[rows, local] = jnp.concatenate(hid_rows + [zero], axis=0).astype(BF16)
        back = [
            [pltpu.roll(v, 7, 0) for v in de_rows],
            de_rows,
            [pltpu.roll(v, 1, 0) for v in de_rows],
        ]
        du_rows = []
        for i in range(7):
            du = None
            for a in range(3):
                if 0 <= i - a + 1 < 7:
                    for b in range(3):
                        term = taps[3 * a + b] * back[b][i - a + 1]
                        du = term if du is None else du + term
            du_rows.append(du * mask[i * 8 : (i + 1) * 8])
        du_low = jnp.concatenate(du_rows + [zero], axis=0).astype(BF16)
        du_ref[rows, local] = du_low
        sums[0] = sums[0] + row_sums(du_low.astype(F32))
        return sums

    steps = 3 * hidden // 256
    even = (u_a, d_a, hid_a, du_a)
    odd = (u_b, d_b, hid_b, du_b)
    for piece in feed(0, *even[:2]):
        piece()

    def slot(step, own, other, ahead):
        extras = feed(step + 1, *other[:2]) if ahead else []
        mix(step, *own, extras + drain(jnp.maximum(step - 1, 0), *other[2:]))

    def pair(number, carry):
        slot(2 * number, even, odd, True)
        slot(2 * number + 1, odd, even, True)
        return carry

    lax.fori_loop(0, (steps - 1) // 2, pair, 0)
    slot(steps - 1, even, odd, False)
    for piece in drain(steps - 1, *even[2:]):
        piece()

    def middle_rows(big, sums):
        sums = list(sums)
        base = pl.multiple_of(big * 192, 64)
        grads = split_tiles(dyrow[pl.ds(base_row + base, 192), :].astype(F32))
        outs = []
        for c in range(3):
            rows = pl.ds(base + c * 64, 64)
            mask = msk[rows, :]
            outs.append(m1s[rows, :] + mask * (tmp[rows, :] + vrow(10)))
            dout = xs[rows, :]
            normal = n2s[rows, :]
            dmid = grads[c] + norm_back(dout, normal, r2s[rows, :], vrow(8))
            m1s[rows, :] = dmid
            low = (dmid * mask).astype(BF16)
            das[rows, :] = low
            sums[0] = sums[0] + row_sums(dout * normal)
            sums[1] = sums[1] + row_sums(dout)
            sums[2] = sums[2] + row_sums(low.astype(F32))
            sums[3] = sums[3] + row_sums(dms[rows, :].astype(F32))
        orow[pl.ds(base_row + base, 192), :] = join_tiles(outs).astype(BF16)
        return tuple(sums)

    sums = lax.fori_loop(0, 3, middle_rows, (zero_rows,) * 4)
    add_small(8, sums[0])
    add_small(9, sums[1])
    add_small(7, sums[2])
    add_small(10, sums[3])
    go[...] += contract(ctxs[...], das[...], 0, 0)
    dcs[...] = contract(das[...], wo[...], 1, 1).astype(BF16)

    def attend_back(t, sums):
        rows = pl.ds(pl.multiple_of(t * 64, 64), 64)
        keys = pl.ds(pl.multiple_of(t * KEYS_TILE, KEYS_TILE), KEYS_TILE)
        probs = ps[pl.ds(pl.multiple_of(t * 80, 16), 80), :]
        upper = dcs[rows, :]
        dprobs = contract(spread(vs, t), upper, 1, 1)
        inner = jnp.sum(by_head(dprobs * probs), axis=1, keepdims=True)
        dz = (by_head(probs) * (by_head(dprobs) - inner)).reshape(probs.shape).astype(BF16)
        dq = (contract(dz, spread(ks, t), 0, 0) * score_scale).astype(BF16)
        dqs[rows, :] = dq
        dk = gather_heads(jnp.dot(dz, qs[rows, :], preferred_element_type=F32)) * score_scale
        dks[keys, :] = dk.astype(BF16)
        dv = gather_heads(
            jnp.dot(probs.astype(BF16), upper, preferred_element_type=F32)
        ).astype(BF16)
        dvs[keys, :] = dv
        return (sums[0] + row_sums(dq.astype(F32)), sums[1] + row_sums(dv.astype(F32)))

    sums = lax.fori_loop(0, TILES, attend_back, (zero_rows,) * 2, unroll=3)
    add_small(2, sums[0])
    add_small(3, sums[1])
    gq[...] += contract(h1s[...], dqs[...], 0, 0)
    gk[...] += contract(kin[...], dks[...], 0, 0)
    gv[...] += contract(kin[...], dvs[...], 0, 0)
    dout = contract(dks[...], wk[...], 1, 1) + contract(dvs[...], wv[...], 1, 1)
    normal = nks[...]
    ds = norm_back(dout, normal, rks[...], vrow(5)).astype(BF16)
    add_small(5, row_sums(dout * normal))
    add_small(6, row_sums(dout))
    add_small(4, row_sums(ds.astype(F32)))
    for d in range(4):
        rows = slice(d * KEYS, (d + 1) * KEYS)
        wide_rows = slice(d * width, (d + 1) * width)
        gr[wide_rows, :] += contract(pats[rows, :], ds, 0, 0)
        dps[rows, :] = contract(ds, wr[wide_rows, :], 1, 1).astype(BF16)
    tmp[...] = contract(pick[...], dps[...], 0, 0)
    xs[...] = contract(dqs[...], wq[...], 1, 1)

    def last_rows(big, sums):
        sums = list(sums)
        base = pl.multiple_of(big * 192, 64)
        outs = []
        for c in range(3):
            rows = pl.ds(base + c * 64, 64)
            dout = xs[rows, :] + msk[rows, :] * tmp[rows, :]
            normal = n1s[rows, :]
            outs.append(m1s[rows, :] + norm_back(dout, normal, r1s[rows, :], vrow(0)))
            sums[0] = sums[0] + row_sums(dout * normal)
            sums[1] = sums[1] + row_sums(dout)
        grow[pl.ds(base_row + base, 192), :] = join_tiles(outs)
        return tuple(sums)

    sums = lax.fori_loop(0, 3, last_rows, (zero_rows,) * 2)
    add_small(0, sums[0])
    add_small(1, sums[1])

    @pl.when(part == per - 1)
    def _():
        for c in range(spans):
            cols = slice(c * LANES, (c + 1) * LANES)
            out_ref[0, :, cols] = jnp.transpose(orow[cols, :].astype(F32)).astype(BF16)
            gin_ref[0, :, cols] = jnp.transpose(grow[cols, :])

    @pl.when(g == pl.num_programs(0) - 1)
    def _():
        for k in range(11):
            gwd[k : k + 1, :] = jnp.sum(acc[k * 8 : (k + 1) * 8, :], axis=0, keepdims=True)
        rotate(
            order, gq, gk, gv, go, gup, gr, gdn, gsm, gwd, la, ra, lb, rb, wire,
            codes, rows_m, mas, mbs, flat, per_block,
        )


def rotate(
    order, gq, gk, gv, go, gup, gr, gdn, gsm, gwd, la, ra, lb, rb, wire,
    codes, rows_m, ras, rbs, flat, per_block,
):
    width, hidden = gup.shape
    fill_codes(la, ra, lb, rb, codes, width)

    def dot(left, right):
        return jnp.dot(left, right, preferred_element_type=F32)

    for k, parts in enumerate(((gq,), (gk, gv), (go,), (gup,))):
        first, count = SPANS_A[k]
        right = lane_matrix(codes, 6 + k, count * width)
        total = None
        depth = right.shape[0] // len(parts)
        for p, part in enumerate(parts):
            piece = dot(part[...].astype(BF16), right[p * depth : (p + 1) * depth])
            total = piece if total is None else total + piece
        row_matrix(codes, k, rows_m, width)
        ras[:, first * width : (first + count) * width] = dot(rows_m[0:width, 0:width], total.astype(BF16))
    row_matrix(codes, 4, rows_m, hidden)
    part = dot(rows_m[...], gr[...].astype(BF16)).astype(BF16)
    rbs[:, 0:width] = dot(part, lane_matrix(codes, 10, width))
    row_matrix(codes, 5, rows_m, hidden)
    part = contract(rows_m[...], gdn[...].astype(BF16), 1, 1).astype(BF16)
    rbs[:, width : 2 * width] = dot(part, lane_matrix(codes, 11, width))
    count, tall, _ = wire.shape
    half = count // 2
    depth = 2 * flat.shape[0] // count
    for first, (source, rows) in enumerate(((ras, width), (rbs, hidden))):
        per_row = source.shape[1] // LANES
        for j in range(per_row):
            cols = slice(j * LANES, (j + 1) * LANES)
            flat[pl.ds(j, rows, stride=per_row), :] = source[:, cols]

        def place(t, carry, first=first):
            spot = order[t] - first * half

            @pl.when((spot >= 0) & (spot < half))
            def _():
                wire[t, 0:depth, :] = flat[pl.ds(spot * depth, depth), :].astype(BF16)
                wire[t, depth:tall, :] = jnp.zeros((tall - depth, LANES), BF16)

            return carry

        lax.fori_loop(0, count, place, 0)
    for number, (kind, k, col, size) in enumerate(vector_spots(width, hidden)):
        block, row = number // per_block, depth + number % per_block
        source = (gsm, gwd)[kind]
        wire[block, row : row + 1, 0:size] = source[k : k + 1, col : col + size].astype(BF16)


def pick_matrix():
    spot = lax.broadcasted_iota(jnp.int32, (SLOTS, SLOTS), 0)
    lane = lax.broadcasted_iota(jnp.int32, (SLOTS, SLOTS), 1)
    part = spot // KEYS
    key = spot - part * KEYS
    tile = key >> 4
    inner = key & 15
    row = 2 * (inner >> 2) + (part >> 1)
    col = 2 * (inner & 3) + (part & 1)
    return jnp.where(tile * 64 + row * TILE + col == lane, 1.0, 0.0).astype(BF16)


def head_mask(width):
    row = lax.broadcasted_iota(jnp.int32, (HEADS * KEYS_TILE, width), 0) >> 4
    col = lax.broadcasted_iota(jnp.int32, (HEADS * KEYS_TILE, width), 1) >> 6
    return jnp.where(row == col, 1.0, 0.0).astype(BF16)


def run_block(
    tokens, grad_output, valid_tiles, master_a, master_b, vector_params, order, la, ra, lb, rb
):
    width = tokens.shape[2]
    hidden = master_b.shape[0]
    rows = tokens.shape[1]
    per = rows // SLOTS
    grids = tokens.shape[0] * per
    flags = valid_tiles.reshape(grids, TILES)
    blocks = order.shape[0]
    per_block = -(-VECTOR_ROWS // blocks)
    total = (master_a.size + master_b.size) // LANES
    tall_block = -(-(total // blocks + per_block) // 32) * 32
    flip = pl.BlockSpec((1, width, rows), lambda g: (g // per, 0, 0))
    tall = (SLOTS, width)
    keys = (KEYS, width)
    scratch = [((width, width), BF16)] * 4 + [
        ((width, hidden), BF16),
        ((hidden, width), BF16),
        ((hidden, width), BF16),
        ((16, hidden), F32),
        ((SLOTS, SLOTS), BF16),
        ((HEADS * KEYS_TILE, width), BF16),
    ]
    scratch += [((width, width), F32)] * 4 + [
        ((width, hidden), F32),
        ((hidden, width), F32),
        ((width, hidden), F32),
        ((16, width), F32),
        ((16, hidden), F32),
        (master_a.shape, F32),
        (master_b.shape, F32),
        None,
        ((rows, width), BF16),
        ((rows, width), BF16),
        ((rows, width), BF16),
        ((rows, width), F32),
        ((16, hidden), jnp.int32),
        ((hidden, hidden), BF16),
        ((total // 2, LANES), F32),
    ]
    scratch += [
        (tall, F32),
        (tall, F32),
        (tall, F32),
        ((SLOTS, 1), F32),
        (tall, BF16),
        (tall, BF16),
        (tall, BF16),
        (tall, BF16),
        (keys, BF16),
        (keys, F32),
        ((KEYS, 1), F32),
        (keys, BF16),
        (keys, BF16),
        ((TILES * HEADS * KEYS_TILE, 64), F32),
        (tall, BF16),
        (tall, F32),
        (tall, F32),
        (tall, F32),
        ((SLOTS, 1), F32),
        (tall, BF16),
        ((3, width, 192), BF16),
        ((3, width, 192), BF16),
        ((88, hidden), F32),
        ((192, 256), F32),
        ((192, 256), F32),
        ((192, 256), BF16),
        ((192, 256), BF16),
        ((192, 256), F32),
        ((192, 256), F32),
        ((192, 256), BF16),
        ((192, 256), BF16),
        (tall, BF16),
        (tall, BF16),
        (tall, BF16),
        (tall, BF16),
        (keys, BF16),
        (keys, BF16),
        (tall, BF16),
    ]
    smem = pl.BlockSpec(memory_space=pltpu.SMEM)
    anywhere = pl.BlockSpec(memory_space=pl.ANY)

    def whole(shape):
        return pl.BlockSpec(shape, lambda g: (0,) * len(shape), pipeline_mode=pl.Buffered(1))

    small = (vector_params, la, ra.reshape(1, -1), lb, rb.reshape(1, -1))
    out, gin, wire = pl.pallas_call(
        functools.partial(block_kernel, per=per, per_block=per_block),
        name="block_step",
        grid=(grids,),
        in_specs=[smem, smem, flip, flip, anywhere, anywhere] + [whole(c.shape) for c in small],
        out_specs=[flip, flip, whole((blocks, tall_block, LANES))],
        out_shape=[
            jax.ShapeDtypeStruct((tokens.shape[0], width, rows), BF16),
            jax.ShapeDtypeStruct((tokens.shape[0], width, rows), F32),
            jax.ShapeDtypeStruct((blocks, tall_block, LANES), BF16),
        ],
        scratch_shapes=[
            pltpu.SemaphoreType.DMA((2,)) if item is None else pltpu.VMEM(*item)
            for item in scratch
        ],
        compiler_params=pltpu.CompilerParams(vmem_limit_bytes=67_000_000),
    )(
        flags,
        order,
        jnp.transpose(tokens, (0, 2, 1)),
        jnp.transpose(grad_output, (0, 2, 1)),
        master_a,
        master_b,
        *small,
    )
    return jnp.transpose(out, (0, 2, 1)), jnp.transpose(gin, (0, 2, 1)), wire

SPANS_A = ((0, 1), (1, 2), (3, 1), (4, 4))
VECTOR_ROWS = 143


def fill_codes(la, ra, lb, rb, codes, width):
    hidden = lb.shape[1]
    codes[...] = jnp.full(codes.shape, -2, jnp.int32)
    codes[0:4, 0:width] = la[...]
    codes[4:6, 0:hidden] = lb[...]
    for k, (first, count) in enumerate(SPANS_A):
        start = first * width
        span = count * width
        codes[6 + k : 7 + k, 0:span] = ra[:, start : start + span] - 2 * start
    for k in range(2):
        codes[10 + k : 11 + k, 0:width] = rb[:, k * width : (k + 1) * width] - 2 * k * width


def lane_matrix(codes, k, size):
    code = codes[k : k + 1, 0:size]
    sign = (1 - 2 * (code & 1)).astype(F32)
    spot = lax.broadcasted_iota(jnp.int32, (size, size), 0)
    return jnp.where(spot == (code >> 1), sign, 0.0).astype(BF16)


def row_matrix(codes, k, out, size):
    for start in range(0, size, LANES):
        code = codes[k : k + 1, start : start + LANES]
        spot = jnp.transpose(jnp.broadcast_to((code >> 1).astype(F32), (LANES, LANES)))
        sign = jnp.transpose(
            jnp.broadcast_to((1 - 2 * (code & 1)).astype(F32), (LANES, LANES))
        )
        for col in range(0, size, LANES):
            lane = lax.broadcasted_iota(jnp.int32, (LANES, LANES), 1).astype(F32) + col
            part = jnp.where(spot == lane, sign, 0.0).astype(BF16)
            out[start : start + LANES, col : col + LANES] = part


def vector_spots(width, hidden):
    spots = []
    for k in range(11):
        for col in range(0, width, LANES):
            spots.append((0, k, col, min(LANES, width - col)))
    for k in range(11):
        for col in range(0, hidden, LANES):
            spots.append((1, k, col, LANES))
    return spots


def restore_kernel(
    blocks, order, la, ra, lb, rb, steps, ma, mb, vp, vf, vsec,
    na, nb, ca, cb, vg, vfn, vsn, nv,
    codes, rows_m, das, dbs, flat, wide_s, per_block,
):
    width = ma.shape[0]
    hidden = mb.shape[0]
    fill_codes(la, ra, lb, rb, codes, width)
    count = blocks.shape[0]
    depth = flat.shape[0] // count

    def place(t, carry):
        flat[pl.ds(order[t] * depth, depth), :] = blocks[t, 0:depth, :].astype(F32)
        return carry

    lax.fori_loop(0, count, place, 0)
    per_row = ma.shape[1] // LANES
    for j in range(per_row):
        das[:, j * LANES : (j + 1) * LANES] = flat[pl.ds(j, width, stride=per_row), :]
    base = width * per_row
    per_row = mb.shape[1] // LANES
    for j in range(per_row):
        dbs[:, j * LANES : (j + 1) * LANES] = flat[pl.ds(base + j, hidden, stride=per_row), :]

    def dot(left, right):
        return jnp.dot(left, right, preferred_element_type=F32)

    def update(master, step, new, copy, cols):
        old = master[:, cols]
        value = old - matrix_rate * (step + weight_decay * old)
        new[:, cols] = value
        copy[:, cols] = value.astype(BF16)

    for k, (first, span) in enumerate(SPANS_A):
        size = span * width
        cols = slice(first * width, first * width + size)
        part = dot(lane_matrix(codes, k, width), das[:, cols].astype(BF16)).astype(BF16)
        row_matrix(codes, 6 + k, rows_m, size)
        update(ma, dot(part, rows_m[0:size, 0:size]), na, ca, cols)
    for k in range(2):
        cols = slice(k * width, (k + 1) * width)
        part = dot(lane_matrix(codes, 4 + k, hidden), dbs[:, cols].astype(BF16)).astype(BF16)
        row_matrix(codes, 10 + k, rows_m, width)
        update(mb, dot(part, rows_m[0:width, 0:width]), nb, cb, cols)
    for number, (kind, k, col, size) in enumerate(vector_spots(width, hidden)):
        block, row = number // per_block, depth + number % per_block
        value = blocks[block, row : row + 1, 0:size].astype(F32)
        if kind == 0:
            vg[k : k + 1, col : col + size] = value
        else:
            wide_s[k : k + 1, col : col + size] = value
    ratio = hidden // width
    for k in range(11):
        for q in range(ratio):
            row = 11 + ratio * k + q
            vg[row : row + 1, :] = wide_s[k : k + 1, q * width : (q + 1) * width]
    grad = vg[...]
    first_new = beta_one * vf[...] + (1.0 - beta_one) * grad
    second_new = beta_two * vsec[...] + (1.0 - beta_two) * grad * grad
    vfn[...] = first_new
    vsn[...] = second_new
    move = direction_of(first_new, second_new, steps[0])
    old = vp[...]
    nv[...] = old - vector_rate * (move + weight_decay * old)


def direction_of(first_new, second_new, steps):
    count = jnp.full((1, LANES), steps, jnp.int32).astype(F32)
    log_one = -0.10536051565782628
    log_two = -0.0010005003335835335
    one = (1.0 / (1.0 - jnp.exp(count * log_one)))[:, 0:1]
    two = (1.0 / (1.0 - jnp.exp(count * log_two)))[:, 0:1]
    return first_new * one / (jnp.sqrt(second_new * two) + adam_epsilon)


def vmem_spec():
    return pl.BlockSpec(memory_space=pltpu.VMEM)


def restore_blocks(blocks, order, la, ra, lb, rb, steps, ma, mb, vp, vf, vsec):
    width = ma.shape[0]
    hidden = mb.shape[0]
    per_block = -(-VECTOR_ROWS // blocks.shape[0])
    total = (ma.size + mb.size) // LANES
    smem = pl.BlockSpec(memory_space=pltpu.SMEM)
    return pl.pallas_call(
        functools.partial(restore_kernel, per_block=per_block),
        name="restore",
        in_specs=[vmem_spec(), smem] + [vmem_spec()] * 4 + [smem] + [vmem_spec()] * 5,
        out_specs=[vmem_spec()] * 8,
        out_shape=[
            jax.ShapeDtypeStruct(ma.shape, F32),
            jax.ShapeDtypeStruct(mb.shape, F32),
            jax.ShapeDtypeStruct(ma.shape, BF16),
            jax.ShapeDtypeStruct(mb.shape, BF16),
        ]
        + [jax.ShapeDtypeStruct(vp.shape, F32)] * 4,
        scratch_shapes=[
            pltpu.VMEM((16, hidden), jnp.int32),
            pltpu.VMEM((hidden, hidden), BF16),
            pltpu.VMEM((width, 8 * width), F32),
            pltpu.VMEM((hidden, 2 * width), F32),
            pltpu.VMEM((total, LANES), F32),
            pltpu.VMEM((16, hidden), F32),
        ],
        compiler_params=pltpu.CompilerParams(vmem_limit_bytes=60 << 20),
    )(blocks, order, la, ra.reshape(1, -1), lb, rb.reshape(1, -1), steps, ma, mb, vp, vf, vsec)


def exchange_kernel(wire, first, second, steps, grad, first_new, second_new, every, *scratch,
                    plan, bits, depth):
    buffers = []
    spot = 0
    for _, _, order in plan:
        buffers.append(scratch[spot : spot + len(order)])
        spot += len(order)
    rs_send, rs_recv, ag_send, ag_recv = scratch[spot:]
    tok = lax.axis_index("tok")
    side = lax.axis_index("ch")

    def mine(axis):
        return side if axis == "ch" else lax.rem(lax.div(tok, 2**axis), 2)

    def peer(axis):
        if axis == "ch":
            return {"ch": 1 - side}
        return {"tok": tok + 2**axis - 2 ** (axis + 1) * mine(axis)}

    axes = [*reversed(range(bits)), "ch"]
    barrier = pltpu.get_barrier_semaphore()
    for axis in axes:
        pl.semaphore_signal(barrier, inc=1, device_id=peer(axis), device_id_type=pl.DeviceIdType.MESH)
    pl.semaphore_wait(barrier, len(axes))

    chunks = range(len(plan))
    left = [list(axes) for _ in chunks]
    held = [wire for _ in chunks]
    pending = []

    def region(c, choice):
        index = tuple(choice(axis) for axis in left[c])
        start, size, _ = plan[c]
        rows = pl.ds(start, size) if held[c] is wire else slice(None)
        return index + (rows, slice(None))

    def scatter_start(c, s):
        axis = plan[c][2][s]
        index = region(c, lambda a: 1 - mine(a) if a == axis else slice(None))
        copy = pltpu.make_async_remote_copy(
            held[c].at[index], buffers[c][s], rs_send.at[c, s], rs_recv.at[c, s],
            device_id=peer(axis), device_id_type=pl.DeviceIdType.MESH,
        )
        copy.start()
        pending.append(copy)
        return copy

    def scatter_keep(c, s):
        axis = plan[c][2][s]
        return held[c][region(c, lambda a: mine(a) if a == axis else slice(None))]

    def gather_start(c, s):
        start, size, order = plan[c]
        axis = order[len(order) - 1 - s]
        done = order[len(order) - s :]
        index = tuple(slice(None) if a in done else mine(a) for a in axes)
        piece = every.at[index + (pl.ds(start, size), slice(None))]
        copy = pltpu.make_async_remote_copy(
            piece, piece, ag_send.at[c, s], ag_recv.at[c, s],
            device_id=peer(axis), device_id_type=pl.DeviceIdType.MESH,
        )
        copy.start()
        pending.append(copy)
        return copy

    stages = len(axes)
    flying = [scatter_start(c, 0) for c in chunks]
    for s in range(stages):
        for c in chunks:
            start, size, order = plan[c]
            flying[c].wait_recv()
            kept = scatter_keep(c, s)
            buffer = buffers[c][s]
            if s < stages - 1:
                buffer[...] = buffer[...] + kept
                left[c].remove(order[s])
                held[c] = buffer
                flying[c] = scatter_start(c, s + 1)
                continue
            total = buffer[...].astype(F32) + kept.astype(F32)
            count = max(0, min(depth - start, size))
            parts = []
            if count:
                rows = slice(start, start + count)
                owned = total[:count]
                grad[rows, :] = owned
                one = beta_one * first[rows, :] + (1.0 - beta_one) * owned
                two = beta_two * second[rows, :] + (1.0 - beta_two) * owned * owned
                first_new[rows, :] = one
                second_new[rows, :] = two
                parts.append(direction_of(one, two, steps[0]))
            if count < size:
                parts.append(total[count:])
            ready = parts[0] if len(parts) == 1 else jnp.concatenate(parts, axis=0)
            own = tuple(mine(a) for a in axes)
            every[own + (slice(start, start + size), slice(None))] = ready.astype(BF16)
            flying[c] = gather_start(c, 0)
    for s in range(stages):
        for c in chunks:
            flying[c].wait_recv()
            if s < stages - 1:
                flying[c] = gather_start(c, s + 1)
    for copy in pending:
        copy.wait_send()


def exchange_blocks(wire, first, second, steps, bits):
    units = wire.shape[1] // 16
    each = -(-units // 9)
    rest = list(range(2, bits))
    orders = ([0] + rest + ["ch", 1], [0, "ch", 1] + rest, [0, 1, "ch"] + rest)
    plan = []
    for number, start in enumerate(range(0, units, each)):
        size = min(each, units - start)
        plan.append((start * 16, size * 16, orders[number % 3]))
    return exchange_plan(wire, first, second, steps, bits, plan)


def exchange_plan(wire, first, second, steps, bits, plan):
    count, tall, _ = wire.shape
    depth = first.shape[0]
    scratch = []
    for _, size, order in plan:
        for s in range(len(order)):
            scratch.append(pltpu.VMEM((2,) * (len(order) - 1 - s) + (size, LANES), BF16))
    for _ in range(4):
        scratch.append(pltpu.SemaphoreType.DMA((len(plan), bits + 1)))
    shape = (2,) * (bits + 1) + (tall, LANES)
    block = jax.ShapeDtypeStruct((depth, LANES), F32)
    grad, first_new, second_new, every = pl.pallas_call(
        functools.partial(exchange_kernel, plan=plan, bits=bits, depth=depth),
        name="exchange",
        in_specs=[vmem_spec()] * 3 + [pl.BlockSpec(memory_space=pltpu.SMEM)],
        out_specs=[vmem_spec()] * 4,
        out_shape=[block, block, block, jax.ShapeDtypeStruct(shape, BF16)],
        scratch_shapes=scratch,
        compiler_params=pltpu.CompilerParams(
            vmem_limit_bytes=60 << 20, collective_id=0, has_side_effects=True
        ),
    )(wire.reshape(shape), first, second, steps)
    return grad, first_new, second_new, every.reshape(wire.shape)


def on_device(
    tokens, grad_output, valid_tiles, master_a, master_b, vector_params, matrix_first,
    matrix_second, vector_first, vector_second, left_a, right_a, left_b, right_b,
    owner_list, step_count, bits,
):
    out, grad_in, wire = run_block(
        tokens, grad_output, valid_tiles, master_a, master_b, vector_params, owner_list,
        left_a, right_a, left_b, right_b,
    )
    shape = matrix_first.shape
    grad, first_new, second_new, every = exchange_blocks(
        wire, matrix_first.reshape(-1, LANES), matrix_second.reshape(-1, LANES), step_count, bits
    )
    restored = restore_blocks(
        every, owner_list, left_a, right_a, left_b, right_b, step_count,
        master_a, master_b, vector_params, vector_first, vector_second,
    )
    return (
        out,
        grad_in,
        grad.reshape(shape),
        first_new.reshape(shape),
        second_new.reshape(shape),
        *restored,
    )


def solution(mesh):
    bits = mesh.shape["tok"].bit_length() - 1
    part = P(None, ("tok", "ch"), None)
    owned = P(("tok", "ch"), None)
    in_specs = (part,) * 3 + (P(),) * 3 + (owned,) * 2 + (P(),) * 8
    out_specs = (part,) * 2 + (owned,) * 3 + (P(),) * 8
    return jax.shard_map(
        functools.partial(on_device, bits=bits), mesh=mesh, in_specs=in_specs, out_specs=out_specs, check_vma=False
    )
```

```python
import functools

import jax
import jax.numpy as jnp
from jax import lax
from jax.experimental import pallas as pl
from jax.experimental.pallas import tpu as pltpu
from jax.sharding import PartitionSpec as P

HEADS = 5
HEAD_DIM = 64
SIDE = 24
TILE = 8
TILES = 9
SLOTS = 576
KEYS = 144
LANES = 128
KEYS_TILE = 16

beta_one = 0.9
beta_two = 0.999
adam_epsilon = 1e-08
norm_epsilon = 1e-05
matrix_rate = 0.05
vector_rate = 0.2
weight_decay = 0.01

F32 = jnp.float32
BF16 = jnp.bfloat16


def contract(left, right, left_dim, right_dim):
    return lax.dot_general(
        left, right, (((left_dim,), (right_dim,)), ((), ())), preferred_element_type=F32
    )


def normalize(values):
    scale = 1.0 / values.shape[-1]
    center = values - jnp.sum(values, axis=-1, keepdims=True) * scale
    inverse = lax.rsqrt(jnp.sum(center * center, axis=-1, keepdims=True) * scale + norm_epsilon)
    return center * inverse, inverse


def norm_back(upstream, normal, inverse, gain):
    scale = 1.0 / upstream.shape[-1]
    scaled = upstream * gain
    inner = jnp.sum(scaled * normal, axis=-1, keepdims=True) * scale
    mean = jnp.sum(scaled, axis=-1, keepdims=True) * scale
    return inverse * (scaled - mean - normal * inner)


def row_sums(values):
    rows, cols = values.shape
    return jnp.sum(values.reshape(rows // 8, 8, cols), axis=0)


def by_head(values):
    return values.reshape(HEADS, KEYS_TILE, values.shape[1])


def split_tiles(rows):
    shaped = rows.reshape(TILE, 3, TILE, rows.shape[1])
    return [shaped[:, c].reshape(TILE * TILE, rows.shape[1]) for c in range(3)]


def join_tiles(tiles):
    return jnp.concatenate(
        [tiles[c][i * TILE : (i + 1) * TILE] for i in range(TILE) for c in range(3)], axis=0
    )


def gelu_parts(e):
    gauss = jnp.exp2((-0.5 * 1.4426950408889634) * (e * e))
    size = jnp.abs(e)
    t = 1.0 / (1.0 + (0.3275911 * 0.7071067811865476) * size)
    poly = t * (
        0.5 * 0.254829592
        + t
        * (
            0.5 * -0.284496736
            + t * (0.5 * 1.421413741 + t * (0.5 * -1.453152027 + t * (0.5 * 1.061405429)))
        )
    )
    tail = poly * gauss
    phi = jnp.where(e >= 0.0, 1.0 - tail, tail)
    return phi, gauss * 0.3989422804014327


def block_kernel(
    flags,
    order,
    x_ref,
    dy_ref,
    ma,
    mb,
    vec,
    la,
    ra,
    lb,
    rb,
    out_ref,
    gin_ref,
    wire,
    wq,
    wk,
    wv,
    wo,
    wup,
    wr,
    wdn,
    wide,
    pick,
    hmask,
    gq,
    gk,
    gv,
    go,
    gup,
    gr,
    gdn,
    gsm,
    gwd,
    mas,
    mbs,
    sems,
    xrow,
    dyrow,
    orow,
    grow,
    codes,
    rows_m,
    flat,
    msk,
    xs,
    n1s,
    r1s,
    h1s,
    hms,
    qs,
    pats,
    kin,
    nks,
    rks,
    ks,
    vs,
    ps,
    ctxs,
    tmp,
    m1s,
    n2s,
    r2s,
    h2s,
    dmt,
    h2t,
    acc,
    u_a,
    d_a,
    hid_a,
    du_a,
    u_b,
    d_b,
    hid_b,
    du_b,
    dms,
    das,
    dcs,
    dqs,
    dks,
    dvs,
    dps,
    *,
    per,
    per_block,
):
    g = pl.program_id(0)
    part = lax.rem(g, per)
    width = x_ref.shape[1]
    hidden = wup.shape[1]
    spans = x_ref.shape[2] // LANES
    base_row = part * SLOTS
    load_a = pltpu.make_async_copy(ma, mas, sems.at[0])
    load_b = pltpu.make_async_copy(mb, mbs, sems.at[1])

    @pl.when(g == 0)
    def _():
        load_a.start()
        load_b.start()
        pick[...] = pick_matrix()
        hmask[...] = head_mask(width)
        ratio = hidden // width
        for k in range(11):
            for q in range(ratio):
                row = 11 + ratio * k + q
                wide[k : k + 1, q * width : (q + 1) * width] = vec[row : row + 1, :]
        for ref in (gq, gk, gv, go, gup, gr, gdn, gsm, acc):
            ref[...] = jnp.zeros(ref.shape, F32)

    @pl.when(part == 0)
    def _():
        for c in range(spans):
            cols = slice(c * LANES, (c + 1) * LANES)
            xrow[cols, :] = jnp.transpose(x_ref[0, :, cols].astype(F32)).astype(BF16)
            dyrow[cols, :] = jnp.transpose(dy_ref[0, :, cols].astype(F32)).astype(BF16)

    row = lax.broadcasted_iota(jnp.int32, (TILE * TILE, width), 0)
    inside = jnp.where((row % TILE < TILE - 1) & (row < TILE * (TILE - 1)), 1.0, 0.0)
    for t in range(TILES):
        msk[t * 64 : (t + 1) * 64, :] = inside * flags[g, t].astype(F32)

    def vrow(number):
        return vec[number : number + 1, :]

    def add_small(number, sums):
        gsm[number : number + 1, :] += jnp.sum(sums, axis=0, keepdims=True)

    zero_rows = jnp.zeros((8, width), F32)

    def first_norm(big, carry):
        base = pl.multiple_of(big * 192, 64)
        tiles = split_tiles(xrow[pl.ds(base_row + base, 192), :].astype(F32))
        grads = split_tiles(dyrow[pl.ds(base_row + base, 192), :].astype(F32))
        for c in range(3):
            rows = pl.ds(base + c * 64, 64)
            normal, inverse = normalize(tiles[c])
            xs[rows, :] = tiles[c]
            n1s[rows, :] = normal
            r1s[rows, :] = inverse
            low = (normal * vrow(0) + vrow(1)).astype(BF16)
            h1s[rows, :] = low
            mask = msk[rows, :]
            hms[rows, :] = (low.astype(F32) * mask).astype(BF16)
            dms[rows, :] = (grads[c] * mask).astype(BF16)
        return carry

    lax.fori_loop(0, 3, first_norm, 0, unroll=3)

    @pl.when(g == 0)
    def _():
        load_a.wait()
        for k, ref in enumerate((wq, wk, wv, wo)):
            ref[...] = mas[:, k * width : (k + 1) * width].astype(BF16)
        wup[...] = mas[:, 4 * width :].astype(BF16)
        load_b.wait()
        wr[...] = mbs[:, :width].astype(BF16)
        wdn[...] = mbs[:, width:].astype(BF16)

    qs[...] = (jnp.dot(h1s[...], wq[...], preferred_element_type=F32) + vrow(2)).astype(BF16)
    for t in range(TILES):
        slots = hms[t * 64 : (t + 1) * 64, :]
        picked = jnp.dot(pick[...], slots, preferred_element_type=F32).astype(BF16)
        for d in range(4):
            spot = d * KEYS + t * KEYS_TILE
            pats[spot : spot + KEYS_TILE, :] = picked[d * KEYS_TILE : (d + 1) * KEYS_TILE]
    reduced = vrow(4)
    for d in range(4):
        reduced = reduced + jnp.dot(
            pats[d * KEYS : (d + 1) * KEYS, :],
            wr[d * width : (d + 1) * width, :],
            preferred_element_type=F32,
        )
    normal, inverse = normalize(reduced)
    nks[...] = normal
    rks[...] = inverse
    kin[...] = (normal * vrow(5) + vrow(6)).astype(BF16)
    ks[...] = jnp.dot(kin[...], wk[...], preferred_element_type=F32).astype(BF16)
    vs[...] = (jnp.dot(kin[...], wv[...], preferred_element_type=F32) + vrow(3)).astype(BF16)
    score_scale = HEAD_DIM ** (-0.5)

    def spread(ref, t):
        part = ref[pl.ds(pl.multiple_of(t * KEYS_TILE, KEYS_TILE), KEYS_TILE), :]
        return jnp.concatenate([part] * HEADS, axis=0) * hmask[...]

    def gather_heads(big):
        big = by_head(big * hmask[...].astype(F32))
        return jnp.sum(big, axis=0)

    def attend_tile(t, carry):
        rows = pl.ds(pl.multiple_of(t * 64, 64), 64)
        scores = by_head(contract(spread(ks, t), qs[rows, :], 1, 1) * score_scale)
        exped = jnp.exp(scores - jnp.max(scores, axis=1, keepdims=True))
        probs = exped * (1.0 / jnp.sum(exped, axis=1, keepdims=True))
        probs = probs.reshape(HEADS * KEYS_TILE, 64)
        ps[pl.ds(pl.multiple_of(t * 80, 16), 80), :] = probs
        ctxs[rows, :] = contract(probs.astype(BF16), spread(vs, t), 0, 0).astype(BF16)
        return carry

    lax.fori_loop(0, TILES, attend_tile, 0, unroll=9)
    tmp[...] = jnp.dot(ctxs[...], wo[...], preferred_element_type=F32)

    def second_norm(t, carry):
        rows = pl.ds(pl.multiple_of(t * 64, 64), 64)
        middle = xs[rows, :] + msk[rows, :] * (tmp[rows, :] + vrow(7))
        m1s[rows, :] = middle
        normal, inverse = normalize(middle)
        n2s[rows, :] = normal
        r2s[rows, :] = inverse
        h2s[rows, :] = (normal * vrow(8) + vrow(9)).astype(BF16)
        return carry

    lax.fori_loop(0, TILES, second_norm, 0, unroll=9)
    for r in range(3):
        rows = slice(r * 192, (r + 1) * 192)
        dmt[r] = jnp.transpose(dms[rows, :])
        h2t[r] = jnp.transpose(h2s[rows, :])
    for ref in (tmp, xs):
        ref[...] = jnp.zeros(ref.shape, F32)
    for ref in (hid_b, du_b):
        ref[...] = jnp.zeros(ref.shape, BF16)

    def spots(step):
        group = lax.div(step, 3)
        big = step - group * 3
        return big, pl.ds(pl.multiple_of(big * 192, 64), 192), pl.ds(
            pl.multiple_of(group * 256, 256), 256
        )

    def feed(step, u_ref, d_ref):
        big, rows, cols = spots(step)

        def up():
            u_ref[...] = jnp.dot(h2s[rows, :], wup[:, cols], preferred_element_type=F32)

        def down():
            d_ref[...] = contract(dms[rows, :], wdn[cols, :], 1, 1)

        return [up, down]

    def drain(step, hid_ref, du_ref):
        big, rows, cols = spots(step)

        def one():
            tmp[rows, :] += jnp.dot(hid_ref[...], wdn[cols, :], preferred_element_type=F32)

        def two():
            xs[rows, :] += contract(du_ref[...], wup[:, cols], 1, 1)

        def three():
            gdn[:, cols] += jnp.dot(dmt[big], hid_ref[...], preferred_element_type=F32)

        def four():
            gup[:, cols] += jnp.dot(h2t[big], du_ref[...], preferred_element_type=F32)

        return [one, two, three, four]

    def mix(step, u_ref, d_ref, hid_ref, du_ref, extras):
        big = lax.rem(step, 3)
        extras = list(extras)
        for lane in range(2):
            local = slice(lane * LANES, (lane + 1) * LANES)
            cols = pl.ds(
                pl.multiple_of(lax.div(step, 3) * 256 + lane * LANES, LANES), LANES
            )
            bias_up = wide[0:1, cols]
            bias_dw = wide[1:2, cols]
            taps = [wide[2 + k : 3 + k, cols] for k in range(9)]
            sums = [jnp.zeros((8, LANES), F32)] * 11
            for c in range(3):
                rows = slice(c * 64, (c + 1) * 64)
                mask = msk[pl.ds(pl.multiple_of(big * 192 + c * 64, 64), 64), 0:LANES]
                sums = mix_unit(
                    u_ref, d_ref, hid_ref, du_ref, rows, local, mask, bias_up, bias_dw, taps, sums
                )
                if extras:
                    extras.pop(0)()
            for k in range(11):
                acc[k * 8 : (k + 1) * 8, cols] += sums[k]
        for extra in extras:
            extra()

    def mix_unit(
        u_ref, d_ref, hid_ref, du_ref, rows, local, mask, bias_up, bias_dw, taps, sums
    ):
        sums = list(sums)
        ups = (u_ref[rows, local] + bias_up) * mask
        mid = [ups[i * 8 : (i + 1) * 8] for i in range(7)]
        shifted = [
            [pltpu.roll(v, 1, 0) for v in mid],
            mid,
            [pltpu.roll(v, 7, 0) for v in mid],
        ]
        grads = d_ref[rows, local]
        hid_rows = []
        de_rows = []
        for i in range(7):
            e = bias_dw
            for a in range(3):
                if 0 <= i + a - 1 < 7:
                    for b in range(3):
                        e = e + taps[3 * a + b] * shifted[b][i + a - 1]
            phi, gauss = gelu_parts(e)
            hid_rows.append(e * phi)
            de = grads[i * 8 : (i + 1) * 8] * (phi + e * gauss)
            de_rows.append(de)
            sums[1] = sums[1] + de
            for a in range(3):
                if 0 <= i + a - 1 < 7:
                    for b in range(3):
                        k = 2 + 3 * a + b
                        sums[k] = sums[k] + de * shifted[b][i + a - 1]
        zero = jnp.zeros((8, LANES), F32)
        hid_ref[rows, local] = jnp.concatenate(hid_rows + [zero], axis=0).astype(BF16)
        back = [
            [pltpu.roll(v, 7, 0) for v in de_rows],
            de_rows,
            [pltpu.roll(v, 1, 0) for v in de_rows],
        ]
        du_rows = []
        for i in range(7):
            du = None
            for a in range(3):
                if 0 <= i - a + 1 < 7:
                    for b in range(3):
                        term = taps[3 * a + b] * back[b][i - a + 1]
                        du = term if du is None else du + term
            du_rows.append(du * mask[i * 8 : (i + 1) * 8])
        du_low = jnp.concatenate(du_rows + [zero], axis=0).astype(BF16)
        du_ref[rows, local] = du_low
        sums[0] = sums[0] + row_sums(du_low.astype(F32))
        return sums

    steps = 3 * hidden // 256
    even = (u_a, d_a, hid_a, du_a)
    odd = (u_b, d_b, hid_b, du_b)
    for piece in feed(0, *even[:2]):
        piece()

    def slot(step, own, other, ahead):
        extras = feed(step + 1, *other[:2]) if ahead else []
        mix(step, *own, extras + drain(jnp.maximum(step - 1, 0), *other[2:]))

    def pair(number, carry):
        slot(2 * number, even, odd, True)
        slot(2 * number + 1, odd, even, True)
        return carry

    lax.fori_loop(0, (steps - 1) // 2, pair, 0)
    slot(steps - 1, even, odd, False)
    for piece in drain(steps - 1, *even[2:]):
        piece()

    def middle_rows(big, sums):
        sums = list(sums)
        base = pl.multiple_of(big * 192, 64)
        grads = split_tiles(dyrow[pl.ds(base_row + base, 192), :].astype(F32))
        outs = []
        for c in range(3):
            rows = pl.ds(base + c * 64, 64)
            mask = msk[rows, :]
            outs.append(m1s[rows, :] + mask * (tmp[rows, :] + vrow(10)))
            dout = xs[rows, :]
            normal = n2s[rows, :]
            dmid = grads[c] + norm_back(dout, normal, r2s[rows, :], vrow(8))
            m1s[rows, :] = dmid
            low = (dmid * mask).astype(BF16)
            das[rows, :] = low
            sums[0] = sums[0] + row_sums(dout * normal)
            sums[1] = sums[1] + row_sums(dout)
            sums[2] = sums[2] + row_sums(low.astype(F32))
            sums[3] = sums[3] + row_sums(dms[rows, :].astype(F32))
        orow[pl.ds(base_row + base, 192), :] = join_tiles(outs).astype(BF16)
        return tuple(sums)

    sums = lax.fori_loop(0, 3, middle_rows, (zero_rows,) * 4, unroll=3)
    add_small(8, sums[0])
    add_small(9, sums[1])
    add_small(7, sums[2])
    add_small(10, sums[3])
    go[...] += contract(ctxs[...], das[...], 0, 0)
    dcs[...] = contract(das[...], wo[...], 1, 1).astype(BF16)

    def attend_back(t, sums):
        rows = pl.ds(pl.multiple_of(t * 64, 64), 64)
        keys = pl.ds(pl.multiple_of(t * KEYS_TILE, KEYS_TILE), KEYS_TILE)
        probs = ps[pl.ds(pl.multiple_of(t * 80, 16), 80), :]
        upper = dcs[rows, :]
        dprobs = contract(spread(vs, t), upper, 1, 1)
        inner = jnp.sum(by_head(dprobs * probs), axis=1, keepdims=True)
        dz = (by_head(probs) * (by_head(dprobs) - inner)).reshape(probs.shape).astype(BF16)
        dq = (contract(dz, spread(ks, t), 0, 0) * score_scale).astype(BF16)
        dqs[rows, :] = dq
        dk = gather_heads(jnp.dot(dz, qs[rows, :], preferred_element_type=F32)) * score_scale
        dks[keys, :] = dk.astype(BF16)
        dv = gather_heads(
            jnp.dot(probs.astype(BF16), upper, preferred_element_type=F32)
        ).astype(BF16)
        dvs[keys, :] = dv
        return (sums[0] + row_sums(dq.astype(F32)), sums[1] + row_sums(dv.astype(F32)))

    sums = lax.fori_loop(0, TILES, attend_back, (zero_rows,) * 2, unroll=9)
    add_small(2, sums[0])
    add_small(3, sums[1])
    gq[...] += contract(h1s[...], dqs[...], 0, 0)
    gk[...] += contract(kin[...], dks[...], 0, 0)
    gv[...] += contract(kin[...], dvs[...], 0, 0)
    dout = contract(dks[...], wk[...], 1, 1) + contract(dvs[...], wv[...], 1, 1)
    normal = nks[...]
    ds = norm_back(dout, normal, rks[...], vrow(5)).astype(BF16)
    add_small(5, row_sums(dout * normal))
    add_small(6, row_sums(dout))
    add_small(4, row_sums(ds.astype(F32)))
    for d in range(4):
        rows = slice(d * KEYS, (d + 1) * KEYS)
        wide_rows = slice(d * width, (d + 1) * width)
        gr[wide_rows, :] += contract(pats[rows, :], ds, 0, 0)
        dps[rows, :] = contract(ds, wr[wide_rows, :], 1, 1).astype(BF16)
    for t in range(TILES):
        spots = [d * KEYS + t * KEYS_TILE for d in range(4)]
        picked = jnp.concatenate([dps[spot : spot + KEYS_TILE, :] for spot in spots], axis=0)
        tmp[t * 64 : (t + 1) * 64, :] = contract(pick[...], picked, 0, 0)
    xs[...] = contract(dqs[...], wq[...], 1, 1)

    def last_rows(big, sums):
        sums = list(sums)
        base = pl.multiple_of(big * 192, 64)
        outs = []
        for c in range(3):
            rows = pl.ds(base + c * 64, 64)
            dout = xs[rows, :] + msk[rows, :] * tmp[rows, :]
            normal = n1s[rows, :]
            outs.append(m1s[rows, :] + norm_back(dout, normal, r1s[rows, :], vrow(0)))
            sums[0] = sums[0] + row_sums(dout * normal)
            sums[1] = sums[1] + row_sums(dout)
        grow[pl.ds(base_row + base, 192), :] = join_tiles(outs)
        return tuple(sums)

    sums = lax.fori_loop(0, 3, last_rows, (zero_rows,) * 2, unroll=3)
    add_small(0, sums[0])
    add_small(1, sums[1])

    @pl.when(part == per - 1)
    def _():
        for c in range(spans):
            cols = slice(c * LANES, (c + 1) * LANES)
            out_ref[0, :, cols] = jnp.transpose(orow[cols, :].astype(F32)).astype(BF16)
            gin_ref[0, :, cols] = jnp.transpose(grow[cols, :])

    @pl.when(g == pl.num_programs(0) - 1)
    def _():
        for k in range(11):
            gwd[k : k + 1, :] = jnp.sum(acc[k * 8 : (k + 1) * 8, :], axis=0, keepdims=True)
        rotate(
            order, gq, gk, gv, go, gup, gr, gdn, gsm, gwd, la, ra, lb, rb, wire,
            codes, rows_m, mas, mbs, flat, per_block,
        )


def rotate(
    order, gq, gk, gv, go, gup, gr, gdn, gsm, gwd, la, ra, lb, rb, wire,
    codes, rows_m, ras, rbs, flat, per_block,
):
    width, hidden = gup.shape
    fill_codes(la, ra, lb, rb, codes, width)

    def dot(left, right):
        return jnp.dot(left, right, preferred_element_type=F32)

    for k, parts in enumerate(((gq,), (gk, gv), (go,), (gup,))):
        first, count = SPANS_A[k]
        right = lane_matrix(codes, 6 + k, count * width)
        total = None
        depth = right.shape[0] // len(parts)
        for p, part in enumerate(parts):
            piece = dot(part[...].astype(BF16), right[p * depth : (p + 1) * depth])
            total = piece if total is None else total + piece
        row_matrix(codes, k, rows_m, width)
        ras[:, first * width : (first + count) * width] = dot(rows_m[0:width, 0:width], total.astype(BF16))
    row_matrix(codes, 4, rows_m, hidden)
    part = dot(rows_m[...], gr[...].astype(BF16)).astype(BF16)
    rbs[:, 0:width] = dot(part, lane_matrix(codes, 10, width))
    row_matrix(codes, 5, rows_m, hidden)
    part = contract(rows_m[...], gdn[...].astype(BF16), 1, 1).astype(BF16)
    rbs[:, width : 2 * width] = dot(part, lane_matrix(codes, 11, width))
    count, tall, _ = wire.shape
    half = count // 2
    depth = 2 * flat.shape[0] // count
    for first, (source, rows) in enumerate(((ras, width), (rbs, hidden))):
        per_row = source.shape[1] // LANES
        for j in range(per_row):
            cols = slice(j * LANES, (j + 1) * LANES)
            flat[pl.ds(j, rows, stride=per_row), :] = source[:, cols]

        def place(t, carry, first=first):
            spot = order[t] - first * half

            @pl.when((spot >= 0) & (spot < half))
            def _():
                wire[t, 0:depth, :] = flat[pl.ds(spot * depth, depth), :].astype(BF16)
                wire[t, depth:tall, :] = jnp.zeros((tall - depth, LANES), BF16)

            return carry

        lax.fori_loop(0, count, place, 0)
    for number, (kind, k, col, size) in enumerate(vector_spots(width, hidden)):
        block, row = number // per_block, depth + number % per_block
        source = (gsm, gwd)[kind]
        wire[block, row : row + 1, 0:size] = source[k : k + 1, col : col + size].astype(BF16)


def pick_matrix():
    spot = lax.broadcasted_iota(jnp.int32, (64, 64), 0)
    lane = lax.broadcasted_iota(jnp.int32, (64, 64), 1)
    part = spot >> 4
    inner = spot & 15
    row = 2 * (inner >> 2) + (part >> 1)
    col = 2 * (inner & 3) + (part & 1)
    return jnp.where(row * TILE + col == lane, 1.0, 0.0).astype(BF16)


def head_mask(width):
    row = lax.broadcasted_iota(jnp.int32, (HEADS * KEYS_TILE, width), 0) >> 4
    col = lax.broadcasted_iota(jnp.int32, (HEADS * KEYS_TILE, width), 1) >> 6
    return jnp.where(row == col, 1.0, 0.0).astype(BF16)


def run_block(
    tokens, grad_output, valid_tiles, master_a, master_b, vector_params, order, la, ra, lb, rb
):
    width = tokens.shape[2]
    hidden = master_b.shape[0]
    rows = tokens.shape[1]
    per = rows // SLOTS
    grids = tokens.shape[0] * per
    flags = valid_tiles.reshape(grids, TILES)
    blocks = order.shape[0]
    per_block = -(-VECTOR_ROWS // blocks)
    total = (master_a.size + master_b.size) // LANES
    tall_block = -(-(total // blocks + per_block) // 32) * 32
    flip = pl.BlockSpec((1, width, rows), lambda g: (g // per, 0, 0))
    tall = (SLOTS, width)
    keys = (KEYS, width)
    scratch = [((width, width), BF16)] * 4 + [
        ((width, hidden), BF16),
        ((hidden, width), BF16),
        ((hidden, width), BF16),
        ((16, hidden), F32),
        ((64, 64), BF16),
        ((HEADS * KEYS_TILE, width), BF16),
    ]
    scratch += [((width, width), F32)] * 4 + [
        ((width, hidden), F32),
        ((hidden, width), F32),
        ((width, hidden), F32),
        ((16, width), F32),
        ((16, hidden), F32),
        (master_a.shape, F32),
        (master_b.shape, F32),
        None,
        ((rows, width), BF16),
        ((rows, width), BF16),
        ((rows, width), BF16),
        ((rows, width), F32),
        ((16, hidden), jnp.int32),
        ((hidden, hidden), BF16),
        ((total // 2, LANES), F32),
    ]
    scratch += [
        (tall, F32),
        (tall, F32),
        (tall, F32),
        ((SLOTS, 1), F32),
        (tall, BF16),
        (tall, BF16),
        (tall, BF16),
        (tall, BF16),
        (keys, BF16),
        (keys, F32),
        ((KEYS, 1), F32),
        (keys, BF16),
        (keys, BF16),
        ((TILES * HEADS * KEYS_TILE, 64), F32),
        (tall, BF16),
        (tall, F32),
        (tall, F32),
        (tall, F32),
        ((SLOTS, 1), F32),
        (tall, BF16),
        ((3, width, 192), BF16),
        ((3, width, 192), BF16),
        ((88, hidden), F32),
        ((192, 256), F32),
        ((192, 256), F32),
        ((192, 256), BF16),
        ((192, 256), BF16),
        ((192, 256), F32),
        ((192, 256), F32),
        ((192, 256), BF16),
        ((192, 256), BF16),
        (tall, BF16),
        (tall, BF16),
        (tall, BF16),
        (tall, BF16),
        (keys, BF16),
        (keys, BF16),
        (tall, BF16),
    ]
    smem = pl.BlockSpec(memory_space=pltpu.SMEM)
    anywhere = pl.BlockSpec(memory_space=pl.ANY)

    def whole(shape):
        return pl.BlockSpec(shape, lambda g: (0,) * len(shape), pipeline_mode=pl.Buffered(1))

    small = (vector_params, la, ra.reshape(-1, LANES), lb, rb.reshape(-1, LANES))
    out, gin, wire = pl.pallas_call(
        functools.partial(block_kernel, per=per, per_block=per_block),
        name="block_step",
        grid=(grids,),
        in_specs=[smem, smem, flip, flip, anywhere, anywhere] + [whole(c.shape) for c in small],
        out_specs=[flip, flip, whole((blocks, tall_block, LANES))],
        out_shape=[
            jax.ShapeDtypeStruct((tokens.shape[0], width, rows), BF16),
            jax.ShapeDtypeStruct((tokens.shape[0], width, rows), F32),
            jax.ShapeDtypeStruct((blocks, tall_block, LANES), BF16),
        ],
        scratch_shapes=[
            pltpu.SemaphoreType.DMA((2,)) if item is None else pltpu.VMEM(*item)
            for item in scratch
        ],
        compiler_params=pltpu.CompilerParams(vmem_limit_bytes=67_000_000),
    )(
        flags,
        order,
        jnp.transpose(tokens, (0, 2, 1)),
        jnp.transpose(grad_output, (0, 2, 1)),
        master_a,
        master_b,
        *small,
    )
    return jnp.transpose(out, (0, 2, 1)), jnp.transpose(gin, (0, 2, 1)), wire

SPANS_A = ((0, 1), (1, 2), (3, 1), (4, 4))
VECTOR_ROWS = 143


def fill_codes(la, ra, lb, rb, codes, width):
    hidden = lb.shape[1]
    codes[...] = jnp.full(codes.shape, -2, jnp.int32)
    right_a = jnp.concatenate([ra[j : j + 1, :] for j in range(ra.shape[0])], axis=1)
    right_b = jnp.concatenate([rb[j : j + 1, :] for j in range(rb.shape[0])], axis=1)
    codes[0:4, 0:width] = la[...]
    codes[4:6, 0:hidden] = lb[...]
    for k, (first, count) in enumerate(SPANS_A):
        start = first * width
        span = count * width
        codes[6 + k : 7 + k, 0:span] = right_a[:, start : start + span] - 2 * start
    for k in range(2):
        codes[10 + k : 11 + k, 0:width] = right_b[:, k * width : (k + 1) * width] - 2 * k * width


def lane_matrix(codes, k, size):
    code = codes[k : k + 1, 0:size]
    sign = (1 - 2 * (code & 1)).astype(F32)
    spot = lax.broadcasted_iota(jnp.int32, (size, size), 0)
    return jnp.where(spot == (code >> 1), sign, 0.0).astype(BF16)


def row_matrix(codes, k, out, size):
    for start in range(0, size, LANES):
        code = codes[k : k + 1, start : start + LANES]
        spot = jnp.transpose(jnp.broadcast_to((code >> 1).astype(F32), (LANES, LANES)))
        sign = jnp.transpose(
            jnp.broadcast_to((1 - 2 * (code & 1)).astype(F32), (LANES, LANES))
        )
        for col in range(0, size, LANES):
            lane = lax.broadcasted_iota(jnp.int32, (LANES, LANES), 1).astype(F32) + col
            part = jnp.where(spot == lane, sign, 0.0).astype(BF16)
            out[start : start + LANES, col : col + LANES] = part


def vector_spots(width, hidden):
    spots = []
    for k in range(11):
        for col in range(0, width, LANES):
            spots.append((0, k, col, min(LANES, width - col)))
    for k in range(11):
        for col in range(0, hidden, LANES):
            spots.append((1, k, col, LANES))
    return spots


def restore_kernel(
    blocks, order, la, ra, lb, rb, steps, ma, mb, vp, vf, vsec, owned, first, second,
    na, nb, ca, cb, vg, vfn, vsn, nv, grad, first_new, second_new,
    codes, rows_m, das, dbs, flat, wide_s, mas, mbs, cas, cbs, sems, per_block,
):
    width = ma.shape[0]
    hidden = mb.shape[0]
    load_a = pltpu.make_async_copy(ma, mas, sems.at[0])
    load_b = pltpu.make_async_copy(mb, mbs, sems.at[1])
    load_a.start()
    load_b.start()
    fill_codes(la, ra, lb, rb, codes, width)
    count = blocks.shape[0]
    depth = flat.shape[0] // count

    def place(t, carry):
        flat[pl.ds(order[t] * depth, depth), :] = blocks[t, 0:depth, :].astype(F32)
        return carry

    lax.fori_loop(0, count, place, 0)
    per_row = ma.shape[1] // LANES
    for j in range(per_row):
        cols = slice(j * LANES, (j + 1) * LANES)
        das[:, cols] = flat[pl.ds(j, width, stride=per_row), :].astype(BF16)
    base = width * per_row
    per_row = mb.shape[1] // LANES
    for j in range(per_row):
        cols = slice(j * LANES, (j + 1) * LANES)
        dbs[:, cols] = flat[pl.ds(base + j, hidden, stride=per_row), :].astype(BF16)

    def dot(left, right):
        return jnp.dot(left, right, preferred_element_type=F32)

    def update(master, step, copy, rows, cols):
        old = master[rows, cols]
        value = old - matrix_rate * (step + weight_decay * old)
        master[rows, cols] = value
        copy[rows, cols] = value.astype(BF16)

    stores = []

    def send(source, target, rows):
        copy = pltpu.make_async_copy(
            source.at[rows, :], target.at[rows, :], sems.at[2 + len(stores)]
        )
        copy.start()
        stores.append(copy)

    load_a.wait()
    for k, (start, span) in enumerate(SPANS_A):
        size = span * width
        cols = slice(start * width, start * width + size)
        part = dot(lane_matrix(codes, k, width), das[:, cols]).astype(BF16)
        row_matrix(codes, 6 + k, rows_m, size)
        update(mas, dot(part, rows_m[0:size, 0:size]), cas, slice(None), cols)
    send(mas, na, slice(0, width))
    send(cas, ca, slice(0, width))
    parts = []
    for k in range(2):
        cols = slice(k * width, (k + 1) * width)
        parts.append(dot(lane_matrix(codes, 4 + k, hidden), dbs[:, cols]).astype(BF16))
        row_matrix(codes, 10 + k, rows_m.at[k * 512 : k * 512 + 512, :], width)
    load_b.wait()
    for c in range(hidden // width):
        rows = slice(c * width, (c + 1) * width)
        for k in range(2):
            right = rows_m[k * 512 : k * 512 + width, 0:width]
            cols = slice(k * width, (k + 1) * width)
            update(mbs, dot(parts[k][rows], right), cbs, rows, cols)
        send(mbs, nb, rows)
        send(cbs, cb, rows)
    total = owned[...]
    grad[...] = total
    first_new[...] = beta_one * first[...] + (1.0 - beta_one) * total
    second_new[...] = beta_two * second[...] + (1.0 - beta_two) * total * total
    for number, (kind, k, col, size) in enumerate(vector_spots(width, hidden)):
        block, row = number // per_block, depth + number % per_block
        value = blocks[block, row : row + 1, 0:size].astype(F32)
        if kind == 0:
            vg[k : k + 1, col : col + size] = value
        else:
            wide_s[k : k + 1, col : col + size] = value
    ratio = hidden // width
    for k in range(11):
        for q in range(ratio):
            row = 11 + ratio * k + q
            vg[row : row + 1, :] = wide_s[k : k + 1, q * width : (q + 1) * width]
    grad = vg[...]
    first_new = beta_one * vf[...] + (1.0 - beta_one) * grad
    second_new = beta_two * vsec[...] + (1.0 - beta_two) * grad * grad
    vfn[...] = first_new
    vsn[...] = second_new
    move = direction_of(first_new, second_new, steps[0])
    old = vp[...]
    nv[...] = old - vector_rate * (move + weight_decay * old)
    for copy in stores:
        copy.wait()


def direction_of(first_new, second_new, steps):
    count = jnp.full((1, LANES), steps, jnp.int32).astype(F32)
    log_one = -0.10536051565782628
    log_two = -0.0010005003335835335
    one = (1.0 / (1.0 - jnp.exp(count * log_one)))[:, 0:1]
    two = (1.0 / (1.0 - jnp.exp(count * log_two)))[:, 0:1]
    return first_new * one / (jnp.sqrt(second_new * two) + adam_epsilon)


def vmem_spec():
    return pl.BlockSpec(memory_space=pltpu.VMEM)


def restore_blocks(
    blocks, order, la, ra, lb, rb, steps, ma, mb, vp, vf, vsec, owned, first, second
):
    width = ma.shape[0]
    hidden = mb.shape[0]
    per_block = -(-VECTOR_ROWS // blocks.shape[0])
    total = (ma.size + mb.size) // LANES
    smem = pl.BlockSpec(memory_space=pltpu.SMEM)
    anywhere = pl.BlockSpec(memory_space=pl.ANY)
    return pl.pallas_call(
        functools.partial(restore_kernel, per_block=per_block),
        name="restore",
        in_specs=[vmem_spec(), smem]
        + [vmem_spec()] * 4
        + [smem]
        + [anywhere] * 2
        + [vmem_spec()] * 6,
        out_specs=[anywhere] * 4 + [vmem_spec()] * 7,
        out_shape=[
            jax.ShapeDtypeStruct(ma.shape, F32),
            jax.ShapeDtypeStruct(mb.shape, F32),
            jax.ShapeDtypeStruct(ma.shape, BF16),
            jax.ShapeDtypeStruct(mb.shape, BF16),
        ]
        + [jax.ShapeDtypeStruct(vp.shape, F32)] * 4
        + [jax.ShapeDtypeStruct(owned.shape, F32)] * 3,
        scratch_shapes=[
            pltpu.VMEM((16, hidden), jnp.int32),
            pltpu.VMEM((hidden, hidden), BF16),
            pltpu.VMEM(ma.shape, BF16),
            pltpu.VMEM(mb.shape, BF16),
            pltpu.VMEM((total, LANES), F32),
            pltpu.VMEM((16, hidden), F32),
            pltpu.VMEM(ma.shape, F32),
            pltpu.VMEM(mb.shape, F32),
            pltpu.VMEM(ma.shape, BF16),
            pltpu.VMEM(mb.shape, BF16),
            pltpu.SemaphoreType.DMA((4 + 2 * (hidden // width),)),
        ],
        compiler_params=pltpu.CompilerParams(vmem_limit_bytes=60 << 20),
    )(
        blocks, order, la, ra.reshape(-1, LANES), lb, rb.reshape(-1, LANES), steps,
        ma, mb, vp, vf, vsec, owned, first, second,
    )


def exchange_kernel(wire, first, second, steps, grad, every, *scratch,
                    plan, bits, depth):
    buffers = []
    spot = 0
    for _, _, order in plan:
        buffers.append(scratch[spot : spot + len(order)])
        spot += len(order)
    rs_send, rs_recv, ag_send, ag_recv = scratch[spot:]
    tok = lax.axis_index("tok")
    side = lax.axis_index("ch")

    def mine(axis):
        return side if axis == "ch" else lax.rem(lax.div(tok, 2**axis), 2)

    def peer(axis):
        if axis == "ch":
            return {"ch": 1 - side}
        return {"tok": tok + 2**axis - 2 ** (axis + 1) * mine(axis)}

    axes = [*reversed(range(bits)), "ch"]
    barrier = pltpu.get_barrier_semaphore()
    for axis in axes:
        pl.semaphore_signal(barrier, inc=1, device_id=peer(axis), device_id_type=pl.DeviceIdType.MESH)
    pl.semaphore_wait(barrier, len(axes))

    chunks = range(len(plan))
    left = [list(axes) for _ in chunks]
    held = [wire for _ in chunks]
    pending = []

    def region(c, choice):
        index = tuple(choice(axis) for axis in left[c])
        start, size, _ = plan[c]
        rows = pl.ds(start, size) if held[c] is wire else slice(None)
        return index + (rows, slice(None))

    def scatter_start(c, s):
        axis = plan[c][2][s]
        index = region(c, lambda a: 1 - mine(a) if a == axis else slice(None))
        copy = pltpu.make_async_remote_copy(
            held[c].at[index], buffers[c][s], rs_send.at[c, s], rs_recv.at[c, s],
            device_id=peer(axis), device_id_type=pl.DeviceIdType.MESH,
        )
        copy.start()
        pending.append(copy)
        return copy

    def scatter_keep(c, s):
        axis = plan[c][2][s]
        return held[c][region(c, lambda a: mine(a) if a == axis else slice(None))]

    def gather_start(c, s):
        start, size, order = plan[c]
        axis = order[len(order) - 1 - s]
        done = order[len(order) - s :]
        index = tuple(slice(None) if a in done else mine(a) for a in axes)
        piece = every.at[index + (pl.ds(start, size), slice(None))]
        copy = pltpu.make_async_remote_copy(
            piece, piece, ag_send.at[c, s], ag_recv.at[c, s],
            device_id=peer(axis), device_id_type=pl.DeviceIdType.MESH,
        )
        copy.start()
        pending.append(copy)
        return copy

    stages = len(axes)
    flying = [scatter_start(c, 0) for c in chunks]
    for s in range(stages):
        for c in chunks:
            start, size, order = plan[c]
            flying[c].wait_recv()
            kept = scatter_keep(c, s)
            buffer = buffers[c][s]
            if s < stages - 1:
                buffer[...] = buffer[...] + kept
                left[c].remove(order[s])
                held[c] = buffer
                flying[c] = scatter_start(c, s + 1)
                continue
            total = buffer[...].astype(F32) + kept.astype(F32)
            count = max(0, min(depth - start, size))
            parts = []
            if count:
                rows = slice(start, start + count)
                owned = total[:count]
                grad[rows, :] = owned
                one = beta_one * first[rows, :] + (1.0 - beta_one) * owned
                two = beta_two * second[rows, :] + (1.0 - beta_two) * owned * owned
                parts.append(direction_of(one, two, steps[0]))
            if count < size:
                parts.append(total[count:])
            ready = parts[0] if len(parts) == 1 else jnp.concatenate(parts, axis=0)
            own = tuple(mine(a) for a in axes)
            every[own + (slice(start, start + size), slice(None))] = ready.astype(BF16)
            flying[c] = gather_start(c, 0)
    for s in range(stages):
        for c in chunks:
            flying[c].wait_recv()
            if s < stages - 1:
                flying[c] = gather_start(c, s + 1)
    for copy in pending:
        copy.wait_send()


def exchange_blocks(wire, first, second, steps, bits):
    units = wire.shape[1] // 16
    each = -(-units // 9)
    rest = list(range(2, bits))
    orders = ([0] + rest + ["ch", 1], [0, "ch", 1] + rest, [0, 1, "ch"] + rest)
    plan = []
    for number, start in enumerate(range(0, units, each)):
        size = min(each, units - start)
        plan.append((start * 16, size * 16, orders[number % 3]))
    return exchange_plan(wire, first, second, steps, bits, plan)


def exchange_plan(wire, first, second, steps, bits, plan):
    count, tall, _ = wire.shape
    depth = first.shape[0]
    scratch = []
    for _, size, order in plan:
        for s in range(len(order)):
            scratch.append(pltpu.VMEM((2,) * (len(order) - 1 - s) + (size, LANES), BF16))
    for _ in range(4):
        scratch.append(pltpu.SemaphoreType.DMA((len(plan), bits + 1)))
    shape = (2,) * (bits + 1) + (tall, LANES)
    block = jax.ShapeDtypeStruct((depth, LANES), F32)
    grad, every = pl.pallas_call(
        functools.partial(exchange_kernel, plan=plan, bits=bits, depth=depth),
        name="exchange",
        in_specs=[vmem_spec()] * 3 + [pl.BlockSpec(memory_space=pltpu.SMEM)],
        out_specs=[vmem_spec()] * 2,
        out_shape=[block, jax.ShapeDtypeStruct(shape, BF16)],
        scratch_shapes=scratch,
        compiler_params=pltpu.CompilerParams(
            vmem_limit_bytes=60 << 20, collective_id=0, has_side_effects=True
        ),
    )(wire.reshape(shape), first, second, steps)
    return grad, every.reshape(wire.shape)


def on_device(
    tokens, grad_output, valid_tiles, master_a, master_b, vector_params, matrix_first,
    matrix_second, vector_first, vector_second, left_a, right_a, left_b, right_b,
    owner_list, step_count, bits,
):
    out, grad_in, wire = run_block(
        tokens, grad_output, valid_tiles, master_a, master_b, vector_params, owner_list,
        left_a, right_a, left_b, right_b,
    )
    shape = matrix_first.shape
    first = matrix_first.reshape(-1, LANES)
    second = matrix_second.reshape(-1, LANES)
    owned, every = exchange_blocks(wire, first, second, step_count, bits)
    *restored, grad, first_new, second_new = restore_blocks(
        every, owner_list, left_a, right_a, left_b, right_b, step_count, master_a, master_b,
        vector_params, vector_first, vector_second, owned, first, second,
    )
    return (
        out,
        grad_in,
        grad.reshape(shape),
        first_new.reshape(shape),
        second_new.reshape(shape),
        *restored,
    )


def solution(mesh):
    bits = mesh.shape["tok"].bit_length() - 1
    part = P(None, ("tok", "ch"), None)
    owned = P(("tok", "ch"), None)
    in_specs = (part,) * 3 + (P(),) * 3 + (owned,) * 2 + (P(),) * 8
    out_specs = (part,) * 2 + (owned,) * 3 + (P(),) * 8
    return jax.shard_map(
        functools.partial(on_device, bits=bits), mesh=mesh, in_specs=in_specs, out_specs=out_specs, check_vma=False
    )
```

```python
import functools

import jax
import jax.numpy as jnp
from jax import lax
from jax.experimental import pallas as pl
from jax.experimental.pallas import tpu as pltpu
from jax.sharding import PartitionSpec as P

HEADS = 5
HEAD_DIM = 64
SIDE = 24
TILE = 8
TILES = 9
SLOTS = 576
KEYS = 144
LANES = 128
KEYS_TILE = 16

beta_one = 0.9
beta_two = 0.999
adam_epsilon = 1e-08
norm_epsilon = 1e-05
matrix_rate = 0.05
vector_rate = 0.2
weight_decay = 0.01

F32 = jnp.float32
BF16 = jnp.bfloat16


def contract(left, right, left_dim, right_dim):
    return lax.dot_general(
        left, right, (((left_dim,), (right_dim,)), ((), ())), preferred_element_type=F32
    )


def normalize(values):
    scale = 1.0 / values.shape[-1]
    center = values - jnp.sum(values, axis=-1, keepdims=True) * scale
    inverse = lax.rsqrt(jnp.sum(center * center, axis=-1, keepdims=True) * scale + norm_epsilon)
    return center * inverse, inverse


def norm_back(upstream, normal, inverse, gain):
    scale = 1.0 / upstream.shape[-1]
    scaled = upstream * gain
    inner = jnp.sum(scaled * normal, axis=-1, keepdims=True) * scale
    mean = jnp.sum(scaled, axis=-1, keepdims=True) * scale
    return inverse * (scaled - mean - normal * inner)


def row_sums(values):
    rows, cols = values.shape
    return jnp.sum(values.reshape(rows // 8, 8, cols), axis=0)


def by_head(values):
    return values.reshape(HEADS, KEYS_TILE, values.shape[1])


def split_tiles(rows):
    shaped = rows.reshape(TILE, 3, TILE, rows.shape[1])
    return [shaped[:, c].reshape(TILE * TILE, rows.shape[1]) for c in range(3)]


def join_tiles(tiles):
    return jnp.concatenate(
        [tiles[c][i * TILE : (i + 1) * TILE] for i in range(TILE) for c in range(3)], axis=0
    )


def gelu_parts(e):
    gauss = jnp.exp2((-0.5 * 1.4426950408889634) * (e * e))
    size = jnp.abs(e)
    t = 1.0 / (1.0 + (0.3275911 * 0.7071067811865476) * size)
    poly = t * (
        0.5 * 0.254829592
        + t
        * (
            0.5 * -0.284496736
            + t * (0.5 * 1.421413741 + t * (0.5 * -1.453152027 + t * (0.5 * 1.061405429)))
        )
    )
    tail = poly * gauss
    phi = jnp.where(e >= 0.0, 1.0 - tail, tail)
    return phi, gauss * 0.3989422804014327


def block_kernel(
    flags,
    order,
    x_ref,
    dy_ref,
    ma,
    mb,
    vec,
    la,
    ra,
    lb,
    rb,
    out_ref,
    gin_ref,
    wire,
    wq,
    wk,
    wv,
    wo,
    wup,
    wr,
    wdn,
    wide,
    pick,
    hmask,
    gq,
    gk,
    gv,
    go,
    gup,
    gr,
    gdn,
    gsm,
    gwd,
    mas,
    mbs,
    sems,
    xrow,
    dyrow,
    orow,
    grow,
    codes,
    rows_m,
    rbt,
    flat,
    msk,
    xs,
    n1s,
    r1s,
    h1s,
    hms,
    qs,
    pats,
    kin,
    nks,
    rks,
    ks,
    vs,
    ps,
    ctxs,
    tmp,
    m1s,
    n2s,
    r2s,
    h2s,
    dmt,
    h2t,
    acc,
    u_a,
    d_a,
    hid_a,
    du_a,
    u_b,
    d_b,
    hid_b,
    du_b,
    u_c,
    d_c,
    hid_c,
    du_c,
    dms,
    das,
    dcs,
    dqs,
    dks,
    dvs,
    dps,
    *,
    per,
    per_block,
):
    g = pl.program_id(0)
    part = lax.rem(g, per)
    width = x_ref.shape[1]
    hidden = wup.shape[1]
    wider = wup.shape[0]
    spans = x_ref.shape[2] // LANES
    base_row = part * SLOTS
    load_a = pltpu.make_async_copy(ma, mas, sems.at[0])
    load_b = pltpu.make_async_copy(mb, mbs, sems.at[1])

    @pl.when(g == 0)
    def _():
        load_a.start()
        load_b.start()
        pick[...] = pick_matrix()
        hmask[...] = head_mask(width)
        ratio = hidden // width
        for k in range(11):
            for q in range(ratio):
                row = 11 + ratio * k + q
                wide[k : k + 1, q * width : (q + 1) * width] = vec[row : row + 1, :]
        for ref in (gq, gk, gv, go, gup, gr, gdn, gsm, acc):
            ref[...] = jnp.zeros(ref.shape, F32)

    @pl.when(part == 0)
    def _():
        for c in range(spans):
            cols = slice(c * LANES, (c + 1) * LANES)
            xrow[cols, :] = jnp.transpose(x_ref[0, :, cols].astype(F32)).astype(BF16)
            dyrow[cols, :] = jnp.transpose(dy_ref[0, :, cols].astype(F32)).astype(BF16)

    row = lax.broadcasted_iota(jnp.int32, (TILE * TILE, width), 0)
    inside = jnp.where((row % TILE < TILE - 1) & (row < TILE * (TILE - 1)), 1.0, 0.0)
    for t in range(TILES):
        msk[t * 64 : (t + 1) * 64, :] = inside * flags[g, t].astype(F32)

    def vrow(number):
        return vec[number : number + 1, :]

    def add_small(number, sums):
        gsm[number : number + 1, :] += jnp.sum(sums, axis=0, keepdims=True)

    zero_rows = jnp.zeros((8, width), F32)

    def first_norm(big, carry):
        base = pl.multiple_of(big * 192, 64)
        tiles = split_tiles(xrow[pl.ds(base_row + base, 192), :].astype(F32))
        grads = split_tiles(dyrow[pl.ds(base_row + base, 192), :].astype(F32))
        for c in range(3):
            rows = pl.ds(base + c * 64, 64)
            normal, inverse = normalize(tiles[c])
            xs[rows, :] = tiles[c]
            n1s[rows, :] = normal
            r1s[rows, :] = inverse
            low = (normal * vrow(0) + vrow(1)).astype(BF16)
            h1s[rows, :] = low
            mask = msk[rows, :]
            hms[rows, :] = (low.astype(F32) * mask).astype(BF16)
            dms[rows, :] = (grads[c] * mask).astype(BF16)
        return carry

    lax.fori_loop(0, 3, first_norm, 0, unroll=3)

    @pl.when(g == 0)
    def _():
        load_a.wait()
        for k, ref in enumerate((wq, wk, wv, wo)):
            ref[...] = mas[:, k * width : (k + 1) * width].astype(BF16)
        wup[0:width, :] = mas[:, 4 * width :].astype(BF16)
        bias = wide[0:1, :]
        high = bias.astype(BF16).astype(F32)
        empty = jnp.zeros((wider - width - 2, hidden), F32)
        wup[width:wider, :] = jnp.concatenate([high, bias - high, empty], axis=0).astype(BF16)
        load_b.wait()
        wr[...] = mbs[:, :width].astype(BF16)
        wdn[...] = mbs[:, width:].astype(BF16)

    qs[...] = (jnp.dot(h1s[...], wq[...], preferred_element_type=F32) + vrow(2)).astype(BF16)
    for t in range(TILES):
        slots = hms[t * 64 : (t + 1) * 64, :]
        picked = jnp.dot(pick[...], slots, preferred_element_type=F32).astype(BF16)
        pats[t * KEYS_TILE : (t + 1) * KEYS_TILE, :] = jnp.concatenate(
            [picked[d * KEYS_TILE : (d + 1) * KEYS_TILE] for d in range(4)], axis=1
        )
    reduced = jnp.dot(pats[...], wr[...], preferred_element_type=F32) + vrow(4)
    normal, inverse = normalize(reduced)
    nks[...] = normal
    rks[...] = inverse
    kin[...] = (normal * vrow(5) + vrow(6)).astype(BF16)
    ks[...] = jnp.dot(kin[...], wk[...], preferred_element_type=F32).astype(BF16)
    vs[...] = (jnp.dot(kin[...], wv[...], preferred_element_type=F32) + vrow(3)).astype(BF16)
    score_scale = HEAD_DIM ** (-0.5)

    def spread(ref, t):
        part = ref[pl.ds(pl.multiple_of(t * KEYS_TILE, KEYS_TILE), KEYS_TILE), :]
        return jnp.concatenate([part] * HEADS, axis=0) * hmask[...]

    def gather_heads(big):
        big = by_head(big * hmask[...].astype(F32))
        return jnp.sum(big, axis=0)

    def attend_tile(t, carry):
        rows = pl.ds(pl.multiple_of(t * 64, 64), 64)
        scores = by_head(contract(spread(ks, t), qs[rows, :], 1, 1) * score_scale)
        exped = jnp.exp(scores - jnp.max(scores, axis=1, keepdims=True))
        probs = exped * (1.0 / jnp.sum(exped, axis=1, keepdims=True))
        probs = probs.reshape(HEADS * KEYS_TILE, 64)
        ps[pl.ds(pl.multiple_of(t * 80, 16), 80), :] = probs
        ctxs[rows, :] = contract(probs.astype(BF16), spread(vs, t), 0, 0).astype(BF16)
        return carry

    lax.fori_loop(0, TILES, attend_tile, 0, unroll=9)
    tmp[...] = jnp.dot(ctxs[...], wo[...], preferred_element_type=F32)

    def second_norm(t, carry):
        rows = pl.ds(pl.multiple_of(t * 64, 64), 64)
        middle = xs[rows, :] + msk[rows, :] * (tmp[rows, :] + vrow(7))
        m1s[rows, :] = middle
        normal, inverse = normalize(middle)
        n2s[rows, :] = normal
        r2s[rows, :] = inverse
        mask = msk[rows, :]
        h2s[rows, 0:width] = ((normal * vrow(8) + vrow(9)) * mask).astype(BF16)
        lane = lax.broadcasted_iota(jnp.int32, (64, wider - width), 1)
        flag = jnp.where(lane < 2, mask[:, 0 : wider - width], 0.0)
        h2s[rows, width:wider] = flag.astype(BF16)
        return carry

    lax.fori_loop(0, TILES, second_norm, 0, unroll=9)
    for r in range(3):
        rows = slice(r * 192, (r + 1) * 192)
        dmt[r] = jnp.transpose(dms[rows, :])
        h2t[r] = jnp.transpose(h2s[rows, :])
    for ref in (tmp, xs):
        ref[...] = jnp.zeros(ref.shape, F32)
    for ref in (hid_c, du_c):
        ref[...] = jnp.zeros(ref.shape, BF16)

    def columns(group):
        return pl.ds(pl.multiple_of(group * 256, 256), 256)

    def feed(group, big, u_ref, d_ref):
        rows = slice(big * 192, (big + 1) * 192)
        cols = columns(group)

        def up():
            u_ref[...] = jnp.dot(h2s[rows, :], wup[:, cols], preferred_element_type=F32)

        def down():
            d_ref[...] = contract(dms[rows, :], wdn[cols, :], 1, 1)

        return [up, down]

    def drain(group, big, hid_ref, du_ref):
        rows = slice(big * 192, (big + 1) * 192)
        cols = columns(group)

        def one():
            tmp[rows, :] += jnp.dot(hid_ref[...], wdn[cols, :], preferred_element_type=F32)

        def two():
            xs[rows, :] += contract(du_ref[...], wup[0:width, cols], 1, 1)

        def three():
            gdn[:, cols] += jnp.dot(dmt[big], hid_ref[...], preferred_element_type=F32)

        def four():
            gup[:, cols] += jnp.dot(h2t[big], du_ref[...], preferred_element_type=F32)

        return [one, two, three, four]

    def mix(group, u_ref, d_ref, hid_ref, du_ref, extras):
        extras = list(extras)
        for lane in range(2):
            local = slice(lane * LANES, (lane + 1) * LANES)
            cols = pl.ds(
                pl.multiple_of(group * 256 + lane * LANES, LANES), LANES
            )
            bias_dw = wide[1:2, cols]
            taps = [wide[2 + k : 3 + k, cols] for k in range(9)]
            sums = [None] + [jnp.zeros((8, LANES), F32)] * 10
            for c in range(3):
                rows = slice(c * 64, (c + 1) * 64)
                sums = mix_unit(
                    u_ref, d_ref, hid_ref, du_ref, rows, local, bias_dw, taps, sums
                )
                if extras:
                    extras.pop(0)()
            for k in range(1, 11):
                acc[k * 8 : (k + 1) * 8, cols] += sums[k]
        for extra in extras:
            extra()

    def mix_unit(
        u_ref, d_ref, hid_ref, du_ref, rows, local, bias_dw, taps, sums
    ):
        sums = list(sums)
        ups = u_ref[rows, local]
        mid = [ups[i * 8 : (i + 1) * 8] for i in range(7)]
        shifted = [
            [pltpu.roll(v, 1, 0) for v in mid],
            mid,
            [pltpu.roll(v, 7, 0) for v in mid],
        ]
        grads = d_ref[rows, local]
        hid_rows = []
        de_rows = []
        for i in range(7):
            e = bias_dw
            for a in range(3):
                if 0 <= i + a - 1 < 7:
                    for b in range(3):
                        e = e + taps[3 * a + b] * shifted[b][i + a - 1]
            phi, gauss = gelu_parts(e)
            hid_rows.append(e * phi)
            de = grads[i * 8 : (i + 1) * 8] * (phi + e * gauss)
            de_rows.append(de)
            sums[1] = sums[1] + de
            for a in range(3):
                if 0 <= i + a - 1 < 7:
                    for b in range(3):
                        k = 2 + 3 * a + b
                        sums[k] = sums[k] + de * shifted[b][i + a - 1]
        zero = jnp.zeros((8, LANES), F32)
        hid_ref[rows, local] = jnp.concatenate(hid_rows + [zero], axis=0).astype(BF16)
        back = [
            [pltpu.roll(v, 7, 0) for v in de_rows],
            de_rows,
            [pltpu.roll(v, 1, 0) for v in de_rows],
        ]
        du_rows = []
        for i in range(7):
            du = None
            for a in range(3):
                if 0 <= i - a + 1 < 7:
                    for b in range(3):
                        term = taps[3 * a + b] * back[b][i - a + 1]
                        du = term if du is None else du + term
            du_rows.append(du)
        du_low = jnp.concatenate(du_rows + [zero], axis=0).astype(BF16)
        du_ref[rows, local] = du_low
        return sums

    sets = (
        (u_a, d_a, hid_a, du_a),
        (u_b, d_b, hid_b, du_b),
        (u_c, d_c, hid_c, du_c),
    )
    groups = hidden // 256
    for big in range(2):
        for piece in feed(0, big, *sets[big][:2]):
            piece()

    def group_step(group, carry):
        after = jnp.minimum(group + 1, groups - 1)
        before = jnp.maximum(group - 1, 0)
        plans = ((group, 2, before, 2), (after, 0, group, 0), (after, 1, group, 1))
        for big, (feed_group, feed_big, drain_group, drain_big) in enumerate(plans):
            extras = drain(drain_group, drain_big, *sets[drain_big][2:])
            later = feed(feed_group, feed_big, *sets[feed_big][:2])
            mix(group, *sets[big], extras + later)
        return carry

    lax.fori_loop(0, groups, group_step, 0)
    for piece in drain(groups - 1, 2, *sets[2][2:]):
        piece()

    def middle_rows(big, sums):
        sums = list(sums)
        base = pl.multiple_of(big * 192, 64)
        grads = split_tiles(dyrow[pl.ds(base_row + base, 192), :].astype(F32))
        outs = []
        for c in range(3):
            rows = pl.ds(base + c * 64, 64)
            mask = msk[rows, :]
            outs.append(m1s[rows, :] + mask * (tmp[rows, :] + vrow(10)))
            dout = xs[rows, :] * mask
            normal = n2s[rows, :]
            dmid = grads[c] + norm_back(dout, normal, r2s[rows, :], vrow(8))
            m1s[rows, :] = dmid
            low = (dmid * mask).astype(BF16)
            das[rows, :] = low
            sums[0] = sums[0] + row_sums(dout * normal)
            sums[1] = sums[1] + row_sums(dout)
            sums[2] = sums[2] + row_sums(low.astype(F32))
            sums[3] = sums[3] + row_sums(dms[rows, :].astype(F32))
        orow[pl.ds(base_row + base, 192), :] = join_tiles(outs).astype(BF16)
        return tuple(sums)

    sums = lax.fori_loop(0, 3, middle_rows, (zero_rows,) * 4, unroll=3)
    add_small(8, sums[0])
    add_small(9, sums[1])
    add_small(7, sums[2])
    add_small(10, sums[3])
    go[...] += contract(ctxs[...], das[...], 0, 0)
    dcs[...] = contract(das[...], wo[...], 1, 1).astype(BF16)

    def attend_back(t, sums):
        rows = pl.ds(pl.multiple_of(t * 64, 64), 64)
        keys = pl.ds(pl.multiple_of(t * KEYS_TILE, KEYS_TILE), KEYS_TILE)
        probs = ps[pl.ds(pl.multiple_of(t * 80, 16), 80), :]
        upper = dcs[rows, :]
        dprobs = contract(spread(vs, t), upper, 1, 1)
        inner = jnp.sum(by_head(dprobs * probs), axis=1, keepdims=True)
        dz = (by_head(probs) * (by_head(dprobs) - inner)).reshape(probs.shape).astype(BF16)
        dq = (contract(dz, spread(ks, t), 0, 0) * score_scale).astype(BF16)
        dqs[rows, :] = dq
        dk = gather_heads(jnp.dot(dz, qs[rows, :], preferred_element_type=F32)) * score_scale
        dks[keys, :] = dk.astype(BF16)
        dv = gather_heads(
            jnp.dot(probs.astype(BF16), upper, preferred_element_type=F32)
        ).astype(BF16)
        dvs[keys, :] = dv
        return (sums[0] + row_sums(dq.astype(F32)), sums[1] + row_sums(dv.astype(F32)))

    sums = lax.fori_loop(0, TILES, attend_back, (zero_rows,) * 2, unroll=9)
    add_small(2, sums[0])
    add_small(3, sums[1])
    gq[...] += contract(h1s[...], dqs[...], 0, 0)
    gk[...] += contract(kin[...], dks[...], 0, 0)
    gv[...] += contract(kin[...], dvs[...], 0, 0)
    dout = contract(dks[...], wk[...], 1, 1) + contract(dvs[...], wv[...], 1, 1)
    normal = nks[...]
    ds = norm_back(dout, normal, rks[...], vrow(5)).astype(BF16)
    add_small(5, row_sums(dout * normal))
    add_small(6, row_sums(dout))
    add_small(4, row_sums(ds.astype(F32)))
    gr[...] += contract(ds, pats[...], 0, 0)
    dps[...] = contract(ds, wr[...], 1, 1).astype(BF16)
    for t in range(TILES):
        back_rows = dps[t * KEYS_TILE : (t + 1) * KEYS_TILE, :]
        picked = jnp.concatenate(
            [back_rows[:, d * width : (d + 1) * width] for d in range(4)], axis=0
        )
        tmp[t * 64 : (t + 1) * 64, :] = contract(pick[...], picked, 0, 0)
    xs[...] = contract(dqs[...], wq[...], 1, 1)

    def last_rows(big, sums):
        sums = list(sums)
        base = pl.multiple_of(big * 192, 64)
        outs = []
        for c in range(3):
            rows = pl.ds(base + c * 64, 64)
            dout = xs[rows, :] + msk[rows, :] * tmp[rows, :]
            normal = n1s[rows, :]
            outs.append(m1s[rows, :] + norm_back(dout, normal, r1s[rows, :], vrow(0)))
            sums[0] = sums[0] + row_sums(dout * normal)
            sums[1] = sums[1] + row_sums(dout)
        grow[pl.ds(base_row + base, 192), :] = join_tiles(outs)
        return tuple(sums)

    sums = lax.fori_loop(0, 3, last_rows, (zero_rows,) * 2, unroll=3)
    add_small(0, sums[0])
    add_small(1, sums[1])

    @pl.when(part == per - 1)
    def _():
        for c in range(spans):
            cols = slice(c * LANES, (c + 1) * LANES)
            out_ref[0, :, cols] = jnp.transpose(orow[cols, :].astype(F32)).astype(BF16)
            gin_ref[0, :, cols] = jnp.transpose(grow[cols, :])

    @pl.when(g == pl.num_programs(0) - 1)
    def _():
        gwd[0:1, :] = gup[width : width + 1, :]
        for k in range(1, 11):
            gwd[k : k + 1, :] = jnp.sum(acc[k * 8 : (k + 1) * 8, :], axis=0, keepdims=True)
        rotate(
            order, gq, gk, gv, go, gup, gr, gdn, gsm, gwd, la, ra, lb, rb, wire,
            codes, rows_m, mas, rbt, flat, per_block,
        )


def rotate(
    order, gq, gk, gv, go, gup, gr, gdn, gsm, gwd, la, ra, lb, rb, wire,
    codes, rows_m, ras, rbt, flat, per_block,
):
    width, hidden = gq.shape[0], gup.shape[1]
    fill_codes(la, ra, lb, rb, codes, width)

    def dot(left, right):
        return jnp.dot(left, right, preferred_element_type=F32)

    for k, parts in enumerate(((gq,), (gk, gv), (go,), (gup.at[0:width],))):
        first, count = SPANS_A[k]
        right = lane_matrix(codes, 6 + k, count * width)
        total = None
        depth = right.shape[0] // len(parts)
        for p, part in enumerate(parts):
            piece = dot(part[...].astype(BF16), right[p * depth : (p + 1) * depth])
            total = piece if total is None else total + piece
        row_matrix(codes, k, rows_m, width)
        ras[:, first * width : (first + count) * width] = dot(rows_m[0:width, 0:width], total.astype(BF16))
    for k, grad in enumerate((gr, gdn)):
        row_matrix(codes, 10 + k, rows_m, width)
        right = rows_m[0:width, 0:width]
        part = dot(right, grad[...].astype(BF16)).astype(BF16)
        rbt[k * width : (k + 1) * width, :] = dot(part, lane_matrix(codes, 4 + k, hidden))
    count, tall, _ = wire.shape
    half = count // 2
    depth = 2 * flat.shape[0] // count
    for first in range(2):
        if first == 0:
            per_row = ras.shape[1] // LANES
            for j in range(per_row):
                cols = slice(j * LANES, (j + 1) * LANES)
                flat[pl.ds(j, width, stride=per_row), :] = ras[:, cols]
        else:
            per_row = rbt.shape[0] // LANES
            for j in range(per_row):
                rows = slice(j * LANES, (j + 1) * LANES)
                flat[pl.ds(j, hidden, stride=per_row), :] = jnp.transpose(rbt[rows, :])

        def place(t, carry, first=first):
            spot = order[t] - first * half

            @pl.when((spot >= 0) & (spot < half))
            def _():
                wire[t, 0:depth, :] = flat[pl.ds(spot * depth, depth), :].astype(BF16)
                wire[t, depth:tall, :] = jnp.zeros((tall - depth, LANES), BF16)

            return carry

        lax.fori_loop(0, count, place, 0)
    for number, (kind, k, col, size) in enumerate(vector_spots(width, hidden)):
        block, row = number // per_block, depth + number % per_block
        source = (gsm, gwd)[kind]
        wire[block, row : row + 1, 0:size] = source[k : k + 1, col : col + size].astype(BF16)


def pick_matrix():
    spot = lax.broadcasted_iota(jnp.int32, (64, 64), 0)
    lane = lax.broadcasted_iota(jnp.int32, (64, 64), 1)
    part = spot >> 4
    inner = spot & 15
    row = 2 * (inner >> 2) + (part >> 1)
    col = 2 * (inner & 3) + (part & 1)
    return jnp.where(row * TILE + col == lane, 1.0, 0.0).astype(BF16)


def head_mask(width):
    row = lax.broadcasted_iota(jnp.int32, (HEADS * KEYS_TILE, width), 0) >> 4
    col = lax.broadcasted_iota(jnp.int32, (HEADS * KEYS_TILE, width), 1) >> 6
    return jnp.where(row == col, 1.0, 0.0).astype(BF16)


def run_block(
    tokens, grad_output, valid_tiles, master_a, master_b, vector_params, order, la, ra, lb, rb
):
    width = tokens.shape[2]
    hidden = master_b.shape[0]
    rows = tokens.shape[1]
    per = rows // SLOTS
    grids = tokens.shape[0] * per
    flags = valid_tiles.reshape(grids, TILES)
    blocks = order.shape[0]
    per_block = -(-VECTOR_ROWS // blocks)
    total = (master_a.size + master_b.size) // LANES
    tall_block = -(-(total // blocks + per_block) // 32) * 32
    flip = pl.BlockSpec((1, width, rows), lambda g: (g // per, 0, 0))
    tall = (SLOTS, width)
    keys = (KEYS, width)
    scratch = [((width, width), BF16)] * 4 + [
        ((width + 16, hidden), BF16),
        ((hidden, width), BF16),
        ((hidden, width), BF16),
        ((16, hidden), F32),
        ((64, 64), BF16),
        ((HEADS * KEYS_TILE, width), BF16),
    ]
    scratch += [((width, width), F32)] * 4 + [
        ((width + 16, hidden), F32),
        ((width, hidden), F32),
        ((width, hidden), F32),
        ((16, width), F32),
        ((16, hidden), F32),
        (master_a.shape, F32),
        (master_b.shape, F32),
        None,
        ((rows, width), BF16),
        ((rows, width), BF16),
        ((rows, width), BF16),
        ((rows, width), F32),
        ((16, hidden), jnp.int32),
        ((hidden, hidden), BF16),
        ((2 * width, hidden), F32),
        ((total // 2, LANES), F32),
    ]
    scratch += [
        (tall, F32),
        (tall, F32),
        (tall, F32),
        ((SLOTS, 1), F32),
        (tall, BF16),
        (tall, BF16),
        (tall, BF16),
        ((KEYS, hidden), BF16),
        (keys, BF16),
        (keys, F32),
        ((KEYS, 1), F32),
        (keys, BF16),
        (keys, BF16),
        ((TILES * HEADS * KEYS_TILE, 64), F32),
        (tall, BF16),
        (tall, F32),
        (tall, F32),
        (tall, F32),
        ((SLOTS, 1), F32),
        ((SLOTS, width + 16), BF16),
        ((3, width, 192), BF16),
        ((3, width + 16, 192), BF16),
        ((88, hidden), F32),
        ((192, 256), F32),
        ((192, 256), F32),
        ((192, 256), BF16),
        ((192, 256), BF16),
        ((192, 256), F32),
        ((192, 256), F32),
        ((192, 256), BF16),
        ((192, 256), BF16),
        ((192, 256), F32),
        ((192, 256), F32),
        ((192, 256), BF16),
        ((192, 256), BF16),
        (tall, BF16),
        (tall, BF16),
        (tall, BF16),
        (tall, BF16),
        (keys, BF16),
        (keys, BF16),
        ((KEYS, hidden), BF16),
    ]
    smem = pl.BlockSpec(memory_space=pltpu.SMEM)
    anywhere = pl.BlockSpec(memory_space=pl.ANY)

    def whole(shape):
        return pl.BlockSpec(shape, lambda g: (0,) * len(shape), pipeline_mode=pl.Buffered(1))

    small = (vector_params, la, ra.reshape(-1, LANES), lb, rb.reshape(-1, LANES))
    out, gin, wire = pl.pallas_call(
        functools.partial(block_kernel, per=per, per_block=per_block),
        name="block_step",
        grid=(grids,),
        in_specs=[smem, smem, flip, flip, anywhere, anywhere] + [whole(c.shape) for c in small],
        out_specs=[flip, flip, whole((blocks, tall_block, LANES))],
        out_shape=[
            jax.ShapeDtypeStruct((tokens.shape[0], width, rows), BF16),
            jax.ShapeDtypeStruct((tokens.shape[0], width, rows), F32),
            jax.ShapeDtypeStruct((blocks, tall_block, LANES), BF16),
        ],
        scratch_shapes=[
            pltpu.SemaphoreType.DMA((2,)) if item is None else pltpu.VMEM(*item)
            for item in scratch
        ],
        compiler_params=pltpu.CompilerParams(vmem_limit_bytes=67_000_000),
    )(
        flags,
        order,
        jnp.transpose(tokens, (0, 2, 1)),
        jnp.transpose(grad_output, (0, 2, 1)),
        master_a,
        master_b,
        *small,
    )
    return jnp.transpose(out, (0, 2, 1)), jnp.transpose(gin, (0, 2, 1)), wire

SPANS_A = ((0, 1), (1, 2), (3, 1), (4, 4))
VECTOR_ROWS = 143


def fill_codes(la, ra, lb, rb, codes, width):
    hidden = lb.shape[1]
    codes[...] = jnp.full(codes.shape, -2, jnp.int32)
    right_a = jnp.concatenate([ra[j : j + 1, :] for j in range(ra.shape[0])], axis=1)
    right_b = jnp.concatenate([rb[j : j + 1, :] for j in range(rb.shape[0])], axis=1)
    codes[0:4, 0:width] = la[...]
    codes[4:6, 0:hidden] = lb[...]
    for k, (first, count) in enumerate(SPANS_A):
        start = first * width
        span = count * width
        codes[6 + k : 7 + k, 0:span] = right_a[:, start : start + span] - 2 * start
    for k in range(2):
        codes[10 + k : 11 + k, 0:width] = right_b[:, k * width : (k + 1) * width] - 2 * k * width


def lane_matrix(codes, k, size):
    code = codes[k : k + 1, 0:size]
    sign = (1 - 2 * (code & 1)).astype(F32)
    spot = lax.broadcasted_iota(jnp.int32, (size, size), 0)
    return jnp.where(spot == (code >> 1), sign, 0.0).astype(BF16)


def row_matrix(codes, k, out, size):
    for start in range(0, size, LANES):
        code = codes[k : k + 1, start : start + LANES]
        spot = jnp.transpose(jnp.broadcast_to((code >> 1).astype(F32), (LANES, LANES)))
        sign = jnp.transpose(
            jnp.broadcast_to((1 - 2 * (code & 1)).astype(F32), (LANES, LANES))
        )
        for col in range(0, size, LANES):
            lane = lax.broadcasted_iota(jnp.int32, (LANES, LANES), 1).astype(F32) + col
            part = jnp.where(spot == lane, sign, 0.0).astype(BF16)
            out[start : start + LANES, col : col + LANES] = part


def vector_spots(width, hidden):
    spots = []
    for k in range(11):
        for col in range(0, width, LANES):
            spots.append((0, k, col, min(LANES, width - col)))
    for k in range(11):
        for col in range(0, hidden, LANES):
            spots.append((1, k, col, LANES))
    return spots


def restore_kernel(
    blocks, order, la, ra, lb, rb, steps, ma, mb, vp, vf, vsec, owned, first, second,
    na, nb, ca, cb, vg, vfn, vsn, nv, grad, first_new, second_new,
    codes, rows_m, das, dbs, flat, wide_s, mas, mbs, cas, cbs, sbt, sems, per_block,
):
    width = ma.shape[0]
    hidden = mb.shape[0]
    load_a = pltpu.make_async_copy(ma, mas, sems.at[0])
    load_b = pltpu.make_async_copy(mb, mbs, sems.at[1])
    load_a.start()
    load_b.start()
    fill_codes(la, ra, lb, rb, codes, width)
    count = blocks.shape[0]
    depth = flat.shape[0] // count

    def place(t, carry):
        flat[pl.ds(order[t] * depth, depth), :] = blocks[t, 0:depth, :].astype(F32)
        return carry

    lax.fori_loop(0, count, place, 0)
    per_row = ma.shape[1] // LANES
    for j in range(per_row):
        cols = slice(j * LANES, (j + 1) * LANES)
        das[:, cols] = flat[pl.ds(j, width, stride=per_row), :].astype(BF16)
    base = width * per_row
    per_row = mb.shape[1] // LANES
    for j in range(per_row):
        rows = slice(j * LANES, (j + 1) * LANES)
        dbs[rows, :] = jnp.transpose(flat[pl.ds(base + j, hidden, stride=per_row), :]).astype(BF16)

    def dot(left, right):
        return jnp.dot(left, right, preferred_element_type=F32)

    def update(master, step, copy, rows, cols):
        old = master[rows, cols]
        value = old - matrix_rate * (step + weight_decay * old)
        master[rows, cols] = value
        copy[rows, cols] = value.astype(BF16)

    stores = []

    def send(source, target, rows):
        copy = pltpu.make_async_copy(
            source.at[rows, :], target.at[rows, :], sems.at[2 + len(stores)]
        )
        copy.start()
        stores.append(copy)

    load_a.wait()
    for k, (start, span) in enumerate(SPANS_A):
        size = span * width
        cols = slice(start * width, start * width + size)
        part = dot(lane_matrix(codes, k, width), das[:, cols]).astype(BF16)
        row_matrix(codes, 6 + k, rows_m, size)
        update(mas, dot(part, rows_m[0:size, 0:size]), cas, slice(None), cols)
    send(mas, na, slice(0, width))
    send(cas, ca, slice(0, width))
    for k in range(2):
        rows = slice(k * width, (k + 1) * width)
        part = dot(lane_matrix(codes, 10 + k, width), dbs[rows, :]).astype(BF16)
        row_matrix(codes, 4 + k, rows_m, hidden)
        sbt[rows, :] = dot(part, rows_m[...])
    load_b.wait()
    for c in range(hidden // 256):
        rows = slice(c * 256, (c + 1) * 256)
        for j in range(per_row):
            cols = slice(j * LANES, (j + 1) * LANES)
            update(mbs, jnp.transpose(sbt[cols, rows]), cbs, rows, cols)
        send(mbs, nb, rows)
        send(cbs, cb, rows)
    total = owned[...]
    grad[...] = total
    first_new[...] = beta_one * first[...] + (1.0 - beta_one) * total
    second_new[...] = beta_two * second[...] + (1.0 - beta_two) * total * total
    for number, (kind, k, col, size) in enumerate(vector_spots(width, hidden)):
        block, row = number // per_block, depth + number % per_block
        value = blocks[block, row : row + 1, 0:size].astype(F32)
        if kind == 0:
            vg[k : k + 1, col : col + size] = value
        else:
            wide_s[k : k + 1, col : col + size] = value
    ratio = hidden // width
    for k in range(11):
        for q in range(ratio):
            row = 11 + ratio * k + q
            vg[row : row + 1, :] = wide_s[k : k + 1, q * width : (q + 1) * width]
    grad = vg[...]
    first_new = beta_one * vf[...] + (1.0 - beta_one) * grad
    second_new = beta_two * vsec[...] + (1.0 - beta_two) * grad * grad
    vfn[...] = first_new
    vsn[...] = second_new
    move = direction_of(first_new, second_new, steps[0])
    old = vp[...]
    nv[...] = old - vector_rate * (move + weight_decay * old)
    for copy in stores:
        copy.wait()


def direction_of(first_new, second_new, steps):
    count = jnp.full((1, LANES), steps, jnp.int32).astype(F32)
    log_one = -0.10536051565782628
    log_two = -0.0010005003335835335
    one = (1.0 / (1.0 - jnp.exp(count * log_one)))[:, 0:1]
    two = (1.0 / (1.0 - jnp.exp(count * log_two)))[:, 0:1]
    return first_new * one / (jnp.sqrt(second_new * two) + adam_epsilon)


def vmem_spec():
    return pl.BlockSpec(memory_space=pltpu.VMEM)


def restore_blocks(
    blocks, order, la, ra, lb, rb, steps, ma, mb, vp, vf, vsec, owned, first, second
):
    width = ma.shape[0]
    hidden = mb.shape[0]
    per_block = -(-VECTOR_ROWS // blocks.shape[0])
    total = (ma.size + mb.size) // LANES
    smem = pl.BlockSpec(memory_space=pltpu.SMEM)
    anywhere = pl.BlockSpec(memory_space=pl.ANY)
    return pl.pallas_call(
        functools.partial(restore_kernel, per_block=per_block),
        name="restore",
        in_specs=[vmem_spec(), smem]
        + [vmem_spec()] * 4
        + [smem]
        + [anywhere] * 2
        + [vmem_spec()] * 6,
        out_specs=[anywhere] * 4 + [vmem_spec()] * 7,
        out_shape=[
            jax.ShapeDtypeStruct(ma.shape, F32),
            jax.ShapeDtypeStruct(mb.shape, F32),
            jax.ShapeDtypeStruct(ma.shape, BF16),
            jax.ShapeDtypeStruct(mb.shape, BF16),
        ]
        + [jax.ShapeDtypeStruct(vp.shape, F32)] * 4
        + [jax.ShapeDtypeStruct(owned.shape, F32)] * 3,
        scratch_shapes=[
            pltpu.VMEM((16, hidden), jnp.int32),
            pltpu.VMEM((hidden, hidden), BF16),
            pltpu.VMEM(ma.shape, BF16),
            pltpu.VMEM((2 * width, hidden), BF16),
            pltpu.VMEM((total, LANES), F32),
            pltpu.VMEM((16, hidden), F32),
            pltpu.VMEM(ma.shape, F32),
            pltpu.VMEM(mb.shape, F32),
            pltpu.VMEM(ma.shape, BF16),
            pltpu.VMEM(mb.shape, BF16),
            pltpu.VMEM((2 * width, hidden), F32),
            pltpu.SemaphoreType.DMA((4 + 2 * (hidden // 256),)),
        ],
        compiler_params=pltpu.CompilerParams(vmem_limit_bytes=60 << 20),
    )(
        blocks, order, la, ra.reshape(-1, LANES), lb, rb.reshape(-1, LANES), steps,
        ma, mb, vp, vf, vsec, owned, first, second,
    )


def exchange_kernel(wire, first, second, steps, grad, every, *scratch,
                    plan, bits, depth):
    buffers = []
    spot = 0
    for _, _, order in plan:
        buffers.append(scratch[spot : spot + len(order)])
        spot += len(order)
    keeps = scratch[spot : spot + len(plan)]
    rs_send, rs_recv, ag_send, ag_recv, local_sem = scratch[spot + len(plan) :]
    tok = lax.axis_index("tok")
    side = lax.axis_index("ch")

    def mine(axis):
        return side if axis == "ch" else lax.rem(lax.div(tok, 2**axis), 2)

    def peer(axis):
        if axis == "ch":
            return {"ch": 1 - side}
        return {"tok": tok + 2**axis - 2 ** (axis + 1) * mine(axis)}

    axes = [*reversed(range(bits)), "ch"]
    loads = []
    for c, (start, size, order) in enumerate(plan):
        index = tuple(mine(a) if a == order[0] else slice(None) for a in axes)
        copy = pltpu.make_async_copy(
            wire.at[index + (pl.ds(start, size), slice(None))], keeps[c], local_sem.at[c]
        )
        copy.start()
        loads.append(copy)
    barrier = pltpu.get_barrier_semaphore()
    for axis in axes:
        pl.semaphore_signal(barrier, inc=1, device_id=peer(axis), device_id_type=pl.DeviceIdType.MESH)
    pl.semaphore_wait(barrier, len(axes))

    chunks = range(len(plan))
    left = [list(axes) for _ in chunks]
    held = [wire for _ in chunks]
    pending = []

    def region(c, choice):
        index = tuple(choice(axis) for axis in left[c])
        start, size, _ = plan[c]
        rows = pl.ds(start, size) if held[c] is wire else slice(None)
        return index + (rows, slice(None))

    def scatter_start(c, s):
        axis = plan[c][2][s]
        index = region(c, lambda a: 1 - mine(a) if a == axis else slice(None))
        copy = pltpu.make_async_remote_copy(
            held[c].at[index], buffers[c][s], rs_send.at[c, s], rs_recv.at[c, s],
            device_id=peer(axis), device_id_type=pl.DeviceIdType.MESH,
        )
        copy.start()
        pending.append(copy)
        return copy

    def scatter_keep(c, s):
        if s == 0:
            loads[c].wait()
            return keeps[c][...]
        axis = plan[c][2][s]
        return held[c][region(c, lambda a: mine(a) if a == axis else slice(None))]

    def gather_start(c, s):
        start, size, order = plan[c]
        axis = order[len(order) - 1 - s]
        done = order[len(order) - s :]
        index = tuple(slice(None) if a in done else mine(a) for a in axes)
        piece = every.at[index + (pl.ds(start, size), slice(None))]
        copy = pltpu.make_async_remote_copy(
            piece, piece, ag_send.at[c, s], ag_recv.at[c, s],
            device_id=peer(axis), device_id_type=pl.DeviceIdType.MESH,
        )
        copy.start()
        pending.append(copy)
        return copy

    stages = len(axes)
    flying = [scatter_start(c, 0) for c in chunks]
    for s in range(stages):
        for c in chunks:
            start, size, order = plan[c]
            flying[c].wait_recv()
            kept = scatter_keep(c, s)
            buffer = buffers[c][s]
            if s < stages - 1:
                buffer[...] = buffer[...] + kept
                left[c].remove(order[s])
                held[c] = buffer
                flying[c] = scatter_start(c, s + 1)
                continue
            total = buffer[...].astype(F32) + kept.astype(F32)
            count = max(0, min(depth - start, size))
            parts = []
            if count:
                rows = slice(start, start + count)
                owned = total[:count]
                grad[rows, :] = owned
                one = beta_one * first[rows, :] + (1.0 - beta_one) * owned
                two = beta_two * second[rows, :] + (1.0 - beta_two) * owned * owned
                parts.append(direction_of(one, two, steps[0]))
            if count < size:
                parts.append(total[count:])
            ready = parts[0] if len(parts) == 1 else jnp.concatenate(parts, axis=0)
            own = tuple(mine(a) for a in axes)
            every[own + (slice(start, start + size), slice(None))] = ready.astype(BF16)
            flying[c] = gather_start(c, 0)
    for s in range(stages):
        for c in chunks:
            flying[c].wait_recv()
            if s < stages - 1:
                flying[c] = gather_start(c, s + 1)
    for copy in pending:
        copy.wait_send()


def exchange_blocks(wire, first, second, steps, bits):
    units = wire.shape[1] // 16
    each = -(-units // 9)
    rest = list(range(2, bits))
    orders = ([0] + rest + ["ch", 1], [0, "ch", 1] + rest, [0, 1, "ch"] + rest)
    plan = []
    for number, start in enumerate(range(0, units, each)):
        size = min(each, units - start)
        plan.append((start * 16, size * 16, orders[number % 3]))
    return exchange_plan(wire, first, second, steps, bits, plan)


def exchange_plan(wire, first, second, steps, bits, plan):
    count, tall, _ = wire.shape
    depth = first.shape[0]
    scratch = []
    for _, size, order in plan:
        for s in range(len(order)):
            scratch.append(pltpu.VMEM((2,) * (len(order) - 1 - s) + (size, LANES), BF16))
    for _, size, order in plan:
        scratch.append(pltpu.VMEM((2,) * (len(order) - 1) + (size, LANES), BF16))
    for _ in range(4):
        scratch.append(pltpu.SemaphoreType.DMA((len(plan), bits + 1)))
    scratch.append(pltpu.SemaphoreType.DMA((len(plan),)))
    shape = (2,) * (bits + 1) + (tall, LANES)
    block = jax.ShapeDtypeStruct((depth, LANES), F32)
    grad, every = pl.pallas_call(
        functools.partial(exchange_kernel, plan=plan, bits=bits, depth=depth),
        name="exchange",
        in_specs=[pl.BlockSpec(memory_space=pl.ANY)]
        + [vmem_spec()] * 2
        + [pl.BlockSpec(memory_space=pltpu.SMEM)],
        out_specs=[vmem_spec()] * 2,
        out_shape=[block, jax.ShapeDtypeStruct(shape, BF16)],
        scratch_shapes=scratch,
        compiler_params=pltpu.CompilerParams(
            vmem_limit_bytes=60 << 20, collective_id=0, has_side_effects=True
        ),
    )(wire.reshape(shape), first, second, steps)
    return grad, every.reshape(wire.shape)


def on_device(
    tokens, grad_output, valid_tiles, master_a, master_b, vector_params, matrix_first,
    matrix_second, vector_first, vector_second, left_a, right_a, left_b, right_b,
    owner_list, step_count, bits,
):
    out, grad_in, wire = run_block(
        tokens, grad_output, valid_tiles, master_a, master_b, vector_params, owner_list,
        left_a, right_a, left_b, right_b,
    )
    shape = matrix_first.shape
    first = matrix_first.reshape(-1, LANES)
    second = matrix_second.reshape(-1, LANES)
    owned, every = exchange_blocks(wire, first, second, step_count, bits)
    *restored, grad, first_new, second_new = restore_blocks(
        every, owner_list, left_a, right_a, left_b, right_b, step_count, master_a, master_b,
        vector_params, vector_first, vector_second, owned, first, second,
    )
    return (
        out,
        grad_in,
        grad.reshape(shape),
        first_new.reshape(shape),
        second_new.reshape(shape),
        *restored,
    )


def solution(mesh):
    bits = mesh.shape["tok"].bit_length() - 1
    part = P(None, ("tok", "ch"), None)
    owned = P(("tok", "ch"), None)
    in_specs = (part,) * 3 + (P(),) * 3 + (owned,) * 2 + (P(),) * 8
    out_specs = (part,) * 2 + (owned,) * 3 + (P(),) * 8
    return jax.shard_map(
        functools.partial(on_device, bits=bits), mesh=mesh, in_specs=in_specs, out_specs=out_specs, check_vma=False
    )
```

```python
import functools

import jax
import jax.numpy as jnp
from jax import lax
from jax.experimental import pallas as pl
from jax.experimental.pallas import tpu as pltpu
from jax.sharding import PartitionSpec as P

HEADS = 5
HEAD_DIM = 64
SIDE = 24
TILE = 8
TILES = 9
SLOTS = 576
KEYS = 144
LANES = 128
KEYS_TILE = 16

beta_one = 0.9
beta_two = 0.999
adam_epsilon = 1e-08
norm_epsilon = 1e-05
matrix_rate = 0.05
vector_rate = 0.2
weight_decay = 0.01

F32 = jnp.float32
BF16 = jnp.bfloat16


def contract(left, right, left_dim, right_dim):
    return lax.dot_general(
        left, right, (((left_dim,), (right_dim,)), ((), ())), preferred_element_type=F32
    )


def normalize(values):
    scale = 1.0 / values.shape[-1]
    center = values - jnp.sum(values, axis=-1, keepdims=True) * scale
    inverse = lax.rsqrt(jnp.sum(center * center, axis=-1, keepdims=True) * scale + norm_epsilon)
    return center * inverse, inverse


def norm_back(upstream, normal, inverse, gain):
    scale = 1.0 / upstream.shape[-1]
    scaled = upstream * gain
    inner = jnp.sum(scaled * normal, axis=-1, keepdims=True) * scale
    mean = jnp.sum(scaled, axis=-1, keepdims=True) * scale
    return inverse * (scaled - mean - normal * inner)


def row_sums(values):
    rows, cols = values.shape
    return jnp.sum(values.reshape(rows // 8, 8, cols), axis=0)


def by_head(values):
    return values.reshape(HEADS, KEYS_TILE, values.shape[1])


def split_tiles(rows):
    shaped = rows.reshape(TILE, 3, TILE, rows.shape[1])
    return [shaped[:, c].reshape(TILE * TILE, rows.shape[1]) for c in range(3)]


def join_tiles(tiles):
    return jnp.concatenate(
        [tiles[c][i * TILE : (i + 1) * TILE] for i in range(TILE) for c in range(3)], axis=0
    )


def gelu_parts(e):
    gauss = jnp.exp2((-0.5 * 1.4426950408889634) * (e * e))
    size = jnp.abs(e)
    t = 1.0 / (1.0 + (0.3275911 * 0.7071067811865476) * size)
    poly = t * (
        0.5 * 0.254829592
        + t
        * (
            0.5 * -0.284496736
            + t * (0.5 * 1.421413741 + t * (0.5 * -1.453152027 + t * (0.5 * 1.061405429)))
        )
    )
    tail = poly * gauss
    phi = jnp.where(e >= 0.0, 1.0 - tail, tail)
    return phi, gauss * 0.3989422804014327


def block_kernel(
    flags,
    order,
    x_ref,
    dy_ref,
    ma,
    mb,
    vec,
    la,
    ra,
    lb,
    rb,
    out_ref,
    gin_ref,
    wire,
    wq,
    wk,
    wv,
    wo,
    wup,
    wr,
    wdn,
    wide,
    pick,
    hmask,
    gq,
    gk,
    gv,
    go,
    gup,
    gr,
    gdn,
    gsm,
    gwd,
    mas,
    mbs,
    sems,
    xrow,
    dyrow,
    orow,
    grow,
    codes,
    rows_m,
    rbt,
    flat,
    msk,
    xs,
    n1s,
    r1s,
    h1s,
    hms,
    qs,
    pats,
    kin,
    nks,
    rks,
    ks,
    vs,
    ps,
    ctxs,
    tmp,
    m1s,
    n2s,
    r2s,
    h2s,
    dmt,
    h2t,
    acc,
    u_a,
    d_a,
    hid_a,
    du_a,
    u_b,
    d_b,
    hid_b,
    du_b,
    u_c,
    d_c,
    hid_c,
    du_c,
    dms,
    das,
    dcs,
    dqs,
    dks,
    dvs,
    dps,
    *,
    per,
    per_block,
):
    g = pl.program_id(0)
    part = lax.rem(g, per)
    width = x_ref.shape[1]
    hidden = wup.shape[1]
    wider = wup.shape[0]
    spans = x_ref.shape[2] // LANES
    base_row = part * SLOTS
    load_a = pltpu.make_async_copy(ma, mas, sems.at[0])
    load_b = pltpu.make_async_copy(mb, mbs, sems.at[1])

    @pl.when(g == 0)
    def _():
        load_a.start()
        load_b.start()
        pick[...] = pick_matrix()
        hmask[...] = head_mask(width)
        ratio = hidden // width
        for k in range(11):
            for q in range(ratio):
                row = 11 + ratio * k + q
                wide[k : k + 1, q * width : (q + 1) * width] = vec[row : row + 1, :]
        for ref in (gq, gk, gv, go, gup, gr, gdn, gsm, acc):
            ref[...] = jnp.zeros(ref.shape, F32)

    @pl.when(part == 0)
    def _():
        for c in range(spans):
            cols = slice(c * LANES, (c + 1) * LANES)
            xrow[cols, :] = jnp.transpose(x_ref[0, :, cols].astype(F32)).astype(BF16)
            dyrow[cols, :] = jnp.transpose(dy_ref[0, :, cols].astype(F32)).astype(BF16)

    row = lax.broadcasted_iota(jnp.int32, (TILE * TILE, width), 0)
    inside = jnp.where((row % TILE < TILE - 1) & (row < TILE * (TILE - 1)), 1.0, 0.0)
    for t in range(TILES):
        msk[t * 64 : (t + 1) * 64, :] = inside * flags[g, t].astype(F32)

    def vrow(number):
        return vec[number : number + 1, :]

    def add_small(number, sums):
        gsm[number : number + 1, :] += jnp.sum(sums, axis=0, keepdims=True)

    zero_rows = jnp.zeros((8, width), F32)

    def first_norm(big, carry):
        base = pl.multiple_of(big * 192, 64)
        tiles = split_tiles(xrow[pl.ds(base_row + base, 192), :].astype(F32))
        grads = split_tiles(dyrow[pl.ds(base_row + base, 192), :].astype(F32))
        for c in range(3):
            rows = pl.ds(base + c * 64, 64)
            normal, inverse = normalize(tiles[c])
            xs[rows, :] = tiles[c]
            n1s[rows, :] = normal
            r1s[rows, :] = inverse
            low = (normal * vrow(0) + vrow(1)).astype(BF16)
            h1s[rows, :] = low
            mask = msk[rows, :]
            hms[rows, :] = (low.astype(F32) * mask).astype(BF16)
            dms[rows, :] = (grads[c] * mask).astype(BF16)
        return carry

    lax.fori_loop(0, 3, first_norm, 0, unroll=3)

    @pl.when(g == 0)
    def _():
        load_a.wait()
        for k, ref in enumerate((wq, wk, wv, wo)):
            ref[...] = mas[:, k * width : (k + 1) * width].astype(BF16)
        wup[0:width, :] = mas[:, 4 * width :].astype(BF16)
        bias = wide[0:1, :]
        high = bias.astype(BF16).astype(F32)
        empty = jnp.zeros((wider - width - 2, hidden), F32)
        wup[width:wider, :] = jnp.concatenate([high, bias - high, empty], axis=0).astype(BF16)
        load_b.wait()
        wr[...] = mbs[:, :width].astype(BF16)
        wdn[...] = mbs[:, width:].astype(BF16)

    qs[...] = (jnp.dot(h1s[...], wq[...], preferred_element_type=F32) + vrow(2)).astype(BF16)
    for t in range(TILES):
        slots = hms[t * 64 : (t + 1) * 64, :]
        picked = jnp.dot(pick[...], slots, preferred_element_type=F32).astype(BF16)
        pats[t * KEYS_TILE : (t + 1) * KEYS_TILE, :] = jnp.concatenate(
            [picked[d * KEYS_TILE : (d + 1) * KEYS_TILE] for d in range(4)], axis=1
        )
    reduced = jnp.dot(pats[...], wr[...], preferred_element_type=F32) + vrow(4)
    normal, inverse = normalize(reduced)
    nks[...] = normal
    rks[...] = inverse
    kin[...] = (normal * vrow(5) + vrow(6)).astype(BF16)
    ks[...] = jnp.dot(kin[...], wk[...], preferred_element_type=F32).astype(BF16)
    vs[...] = (jnp.dot(kin[...], wv[...], preferred_element_type=F32) + vrow(3)).astype(BF16)
    score_scale = HEAD_DIM ** (-0.5)

    def spread(ref, t):
        part = ref[pl.ds(pl.multiple_of(t * KEYS_TILE, KEYS_TILE), KEYS_TILE), :]
        return jnp.concatenate([part] * HEADS, axis=0) * hmask[...]

    def gather_heads(big):
        big = by_head(big * hmask[...].astype(F32))
        return jnp.sum(big, axis=0)

    def attend_tile(t, carry):
        rows = pl.ds(pl.multiple_of(t * 64, 64), 64)
        scores = by_head(contract(spread(ks, t), qs[rows, :], 1, 1) * score_scale)
        exped = jnp.exp(scores - jnp.max(scores, axis=1, keepdims=True))
        probs = exped * (1.0 / jnp.sum(exped, axis=1, keepdims=True))
        probs = probs.reshape(HEADS * KEYS_TILE, 64)
        ps[pl.ds(pl.multiple_of(t * 80, 16), 80), :] = probs
        ctxs[rows, :] = contract(probs.astype(BF16), spread(vs, t), 0, 0).astype(BF16)
        return carry

    lax.fori_loop(0, TILES, attend_tile, 0, unroll=9)
    tmp[...] = jnp.dot(ctxs[...], wo[...], preferred_element_type=F32)

    def second_norm(t, carry):
        rows = pl.ds(pl.multiple_of(t * 64, 64), 64)
        middle = xs[rows, :] + msk[rows, :] * (tmp[rows, :] + vrow(7))
        m1s[rows, :] = middle
        normal, inverse = normalize(middle)
        n2s[rows, :] = normal
        r2s[rows, :] = inverse
        mask = msk[rows, :]
        h2s[rows, 0:width] = ((normal * vrow(8) + vrow(9)) * mask).astype(BF16)
        lane = lax.broadcasted_iota(jnp.int32, (64, wider - width), 1)
        flag = jnp.where(lane < 2, mask[:, 0 : wider - width], 0.0)
        h2s[rows, width:wider] = flag.astype(BF16)
        return carry

    lax.fori_loop(0, TILES, second_norm, 0, unroll=9)
    for r in range(3):
        rows = slice(r * 192, (r + 1) * 192)
        dmt[r] = jnp.transpose(dms[rows, :])
        h2t[r] = jnp.transpose(h2s[rows, :])
    for ref in (tmp, xs):
        ref[...] = jnp.zeros(ref.shape, F32)
    def columns(group):
        return pl.ds(pl.multiple_of(group * 256, 256), 256)

    def feed(group, big, u_ref, d_ref):
        rows = slice(big * 192, (big + 1) * 192)
        cols = columns(group)

        def up():
            u_ref[...] = jnp.dot(h2s[rows, :], wup[:, cols], preferred_element_type=F32)

        def down():
            d_ref[...] = contract(dms[rows, :], wdn[cols, :], 1, 1)

        return [up, down]

    def drain(group, big, hid_ref, du_ref):
        rows = slice(big * 192, (big + 1) * 192)
        cols = columns(group)

        def one():
            tmp[rows, :] += jnp.dot(hid_ref[...], wdn[cols, :], preferred_element_type=F32)

        def two():
            xs[rows, :] += contract(du_ref[...], wup[0:width, cols], 1, 1)

        def three():
            gdn[:, cols] += jnp.dot(dmt[big], hid_ref[...], preferred_element_type=F32)

        def four():
            gup[:, cols] += jnp.dot(h2t[big], du_ref[...], preferred_element_type=F32)

        return [one, two, three, four]

    def mix(group, u_ref, d_ref, hid_ref, du_ref, extras):
        extras = list(extras)
        for lane in range(2):
            local = slice(lane * LANES, (lane + 1) * LANES)
            cols = pl.ds(
                pl.multiple_of(group * 256 + lane * LANES, LANES), LANES
            )
            bias_dw = wide[1:2, cols]
            taps = [wide[2 + k : 3 + k, cols] for k in range(9)]
            sums = [None] + [jnp.zeros((8, LANES), F32)] * 10
            for c in range(3):
                rows = slice(c * 64, (c + 1) * 64)
                sums = mix_unit(
                    u_ref, d_ref, hid_ref, du_ref, rows, local, bias_dw, taps, sums
                )
                if extras:
                    extras.pop(0)()
            for k in range(1, 11):
                acc[k * 8 : (k + 1) * 8, cols] += sums[k]
        for extra in extras:
            extra()

    def mix_unit(
        u_ref, d_ref, hid_ref, du_ref, rows, local, bias_dw, taps, sums
    ):
        sums = list(sums)
        ups = u_ref[rows, local]
        mid = [ups[i * 8 : (i + 1) * 8] for i in range(7)]
        shifted = [
            [pltpu.roll(v, 1, 0) for v in mid],
            mid,
            [pltpu.roll(v, 7, 0) for v in mid],
        ]
        grads = d_ref[rows, local]
        hid_rows = []
        de_rows = []
        for i in range(7):
            e = bias_dw
            for a in range(3):
                if 0 <= i + a - 1 < 7:
                    for b in range(3):
                        e = e + taps[3 * a + b] * shifted[b][i + a - 1]
            phi, gauss = gelu_parts(e)
            hid_rows.append(e * phi)
            de = grads[i * 8 : (i + 1) * 8] * (phi + e * gauss)
            de_rows.append(de)
            sums[1] = sums[1] + de
            for a in range(3):
                if 0 <= i + a - 1 < 7:
                    for b in range(3):
                        k = 2 + 3 * a + b
                        sums[k] = sums[k] + de * shifted[b][i + a - 1]
        zero = jnp.zeros((8, LANES), F32)
        hid_ref[rows, local] = jnp.concatenate(hid_rows + [zero], axis=0).astype(BF16)
        back = [
            [pltpu.roll(v, 7, 0) for v in de_rows],
            de_rows,
            [pltpu.roll(v, 1, 0) for v in de_rows],
        ]
        du_rows = []
        for i in range(7):
            du = None
            for a in range(3):
                if 0 <= i - a + 1 < 7:
                    for b in range(3):
                        term = taps[3 * a + b] * back[b][i - a + 1]
                        du = term if du is None else du + term
            du_rows.append(du)
        du_low = jnp.concatenate(du_rows + [zero], axis=0).astype(BF16)
        du_ref[rows, local] = du_low
        return sums

    sets = (
        (u_a, d_a, hid_a, du_a),
        (u_b, d_b, hid_b, du_b),
        (u_c, d_c, hid_c, du_c),
    )
    groups = hidden // 256
    for big in range(2):
        for piece in feed(0, big, *sets[big][:2]):
            piece()

    def group_step(group, first, last):
        after = group + 1 if first else jnp.minimum(group + 1, groups - 1)
        plans = ((group, 2, group - 1, 2), (after, 0, group, 0), (after, 1, group, 1))
        for big, (feed_group, feed_big, drain_group, drain_big) in enumerate(plans):
            extras = []
            if big or not first:
                extras += drain(drain_group, drain_big, *sets[drain_big][2:])
            if not (big and last):
                extras += feed(feed_group, feed_big, *sets[feed_big][:2])
            mix(group, *sets[big], extras)

    def group_pair(number, carry):
        for k in range(2):
            group_step(2 * number + k + 1, False, False)
        return carry

    group_step(0, True, False)
    lax.fori_loop(0, (groups - 1) // 2, group_pair, 0)
    for piece in drain(groups - 1, 2, *sets[2][2:]):
        piece()

    def middle_rows(big, sums):
        sums = list(sums)
        base = pl.multiple_of(big * 192, 64)
        grads = split_tiles(dyrow[pl.ds(base_row + base, 192), :].astype(F32))
        outs = []
        for c in range(3):
            rows = pl.ds(base + c * 64, 64)
            mask = msk[rows, :]
            outs.append(m1s[rows, :] + mask * (tmp[rows, :] + vrow(10)))
            dout = xs[rows, :] * mask
            normal = n2s[rows, :]
            dmid = grads[c] + norm_back(dout, normal, r2s[rows, :], vrow(8))
            m1s[rows, :] = dmid
            low = (dmid * mask).astype(BF16)
            das[rows, :] = low
            sums[0] = sums[0] + row_sums(dout * normal)
            sums[1] = sums[1] + row_sums(dout)
            sums[2] = sums[2] + row_sums(low.astype(F32))
            sums[3] = sums[3] + row_sums(dms[rows, :].astype(F32))
        orow[pl.ds(base_row + base, 192), :] = join_tiles(outs).astype(BF16)
        return tuple(sums)

    sums = lax.fori_loop(0, 3, middle_rows, (zero_rows,) * 4, unroll=3)
    add_small(8, sums[0])
    add_small(9, sums[1])
    add_small(7, sums[2])
    add_small(10, sums[3])
    go[...] += contract(ctxs[...], das[...], 0, 0)
    dcs[...] = contract(das[...], wo[...], 1, 1).astype(BF16)

    def attend_back(t, sums):
        rows = pl.ds(pl.multiple_of(t * 64, 64), 64)
        keys = pl.ds(pl.multiple_of(t * KEYS_TILE, KEYS_TILE), KEYS_TILE)
        probs = ps[pl.ds(pl.multiple_of(t * 80, 16), 80), :]
        upper = dcs[rows, :]
        dprobs = contract(spread(vs, t), upper, 1, 1)
        inner = jnp.sum(by_head(dprobs * probs), axis=1, keepdims=True)
        dz = (by_head(probs) * (by_head(dprobs) - inner)).reshape(probs.shape).astype(BF16)
        dq = (contract(dz, spread(ks, t), 0, 0) * score_scale).astype(BF16)
        dqs[rows, :] = dq
        dk = gather_heads(jnp.dot(dz, qs[rows, :], preferred_element_type=F32)) * score_scale
        dks[keys, :] = dk.astype(BF16)
        dv = gather_heads(
            jnp.dot(probs.astype(BF16), upper, preferred_element_type=F32)
        ).astype(BF16)
        dvs[keys, :] = dv
        return (sums[0] + row_sums(dq.astype(F32)), sums[1] + row_sums(dv.astype(F32)))

    sums = lax.fori_loop(0, TILES, attend_back, (zero_rows,) * 2, unroll=9)
    add_small(2, sums[0])
    add_small(3, sums[1])
    gq[...] += contract(h1s[...], dqs[...], 0, 0)
    gk[...] += contract(kin[...], dks[...], 0, 0)
    gv[...] += contract(kin[...], dvs[...], 0, 0)
    dout = contract(dks[...], wk[...], 1, 1) + contract(dvs[...], wv[...], 1, 1)
    normal = nks[...]
    ds = norm_back(dout, normal, rks[...], vrow(5)).astype(BF16)
    add_small(5, row_sums(dout * normal))
    add_small(6, row_sums(dout))
    add_small(4, row_sums(ds.astype(F32)))
    gr[...] += contract(ds, pats[...], 0, 0)
    dps[...] = contract(ds, wr[...], 1, 1).astype(BF16)
    for t in range(TILES):
        back_rows = dps[t * KEYS_TILE : (t + 1) * KEYS_TILE, :]
        picked = jnp.concatenate(
            [back_rows[:, d * width : (d + 1) * width] for d in range(4)], axis=0
        )
        tmp[t * 64 : (t + 1) * 64, :] = contract(pick[...], picked, 0, 0)
    xs[...] = contract(dqs[...], wq[...], 1, 1)

    def last_rows(big, sums):
        sums = list(sums)
        base = pl.multiple_of(big * 192, 64)
        outs = []
        for c in range(3):
            rows = pl.ds(base + c * 64, 64)
            dout = xs[rows, :] + msk[rows, :] * tmp[rows, :]
            normal = n1s[rows, :]
            outs.append(m1s[rows, :] + norm_back(dout, normal, r1s[rows, :], vrow(0)))
            sums[0] = sums[0] + row_sums(dout * normal)
            sums[1] = sums[1] + row_sums(dout)
        grow[pl.ds(base_row + base, 192), :] = join_tiles(outs)
        return tuple(sums)

    sums = lax.fori_loop(0, 3, last_rows, (zero_rows,) * 2, unroll=3)
    add_small(0, sums[0])
    add_small(1, sums[1])

    @pl.when(part == per - 1)
    def _():
        for c in range(spans):
            cols = slice(c * LANES, (c + 1) * LANES)
            out_ref[0, :, cols] = jnp.transpose(orow[cols, :].astype(F32)).astype(BF16)
            gin_ref[0, :, cols] = jnp.transpose(grow[cols, :])

    @pl.when(g == pl.num_programs(0) - 1)
    def _():
        gwd[0:1, :] = gup[width : width + 1, :]
        for k in range(1, 11):
            gwd[k : k + 1, :] = jnp.sum(acc[k * 8 : (k + 1) * 8, :], axis=0, keepdims=True)
        rotate(
            order, gq, gk, gv, go, gup, gr, gdn, gsm, gwd, la, ra, lb, rb, wire,
            codes, rows_m, mas, rbt, flat, per_block,
        )


def rotate(
    order, gq, gk, gv, go, gup, gr, gdn, gsm, gwd, la, ra, lb, rb, wire,
    codes, rows_m, ras, rbt, flat, per_block,
):
    width, hidden = gq.shape[0], gup.shape[1]
    fill_codes(la, ra, lb, rb, codes, width)

    def dot(left, right):
        return jnp.dot(left, right, preferred_element_type=F32)

    for k, parts in enumerate(((gq,), (gk, gv), (go,), (gup.at[0:width],))):
        first, count = SPANS_A[k]
        right = lane_matrix(codes, 6 + k, count * width)
        total = None
        depth = right.shape[0] // len(parts)
        for p, part in enumerate(parts):
            piece = dot(part[...].astype(BF16), right[p * depth : (p + 1) * depth])
            total = piece if total is None else total + piece
        row_matrix(codes, k, rows_m, width)
        ras[:, first * width : (first + count) * width] = dot(rows_m[0:width, 0:width], total.astype(BF16))
    for k, grad in enumerate((gr, gdn)):
        row_matrix(codes, 10 + k, rows_m, width)
        right = rows_m[0:width, 0:width]
        part = dot(right, grad[...].astype(BF16)).astype(BF16)
        rbt[k * width : (k + 1) * width, :] = dot(part, lane_matrix(codes, 4 + k, hidden))
    count, tall, _ = wire.shape
    half = count // 2
    depth = 2 * flat.shape[0] // count
    for first in range(2):
        if first == 0:
            per_row = ras.shape[1] // LANES
            for j in range(per_row):
                cols = slice(j * LANES, (j + 1) * LANES)
                flat[pl.ds(j, width, stride=per_row), :] = ras[:, cols]
        else:
            per_row = rbt.shape[0] // LANES
            for j in range(per_row):
                rows = slice(j * LANES, (j + 1) * LANES)
                flat[pl.ds(j, hidden, stride=per_row), :] = jnp.transpose(rbt[rows, :])

        def place(t, carry, first=first):
            spot = order[t] - first * half

            @pl.when((spot >= 0) & (spot < half))
            def _():
                wire[t, 0:depth, :] = flat[pl.ds(spot * depth, depth), :].astype(BF16)
                wire[t, depth:tall, :] = jnp.zeros((tall - depth, LANES), BF16)

            return carry

        lax.fori_loop(0, count, place, 0)
    for number, (kind, k, col, size) in enumerate(vector_spots(width, hidden)):
        block, row = number // per_block, depth + number % per_block
        source = (gsm, gwd)[kind]
        wire[block, row : row + 1, 0:size] = source[k : k + 1, col : col + size].astype(BF16)


def pick_matrix():
    spot = lax.broadcasted_iota(jnp.int32, (64, 64), 0)
    lane = lax.broadcasted_iota(jnp.int32, (64, 64), 1)
    part = spot >> 4
    inner = spot & 15
    row = 2 * (inner >> 2) + (part >> 1)
    col = 2 * (inner & 3) + (part & 1)
    return jnp.where(row * TILE + col == lane, 1.0, 0.0).astype(BF16)


def head_mask(width):
    row = lax.broadcasted_iota(jnp.int32, (HEADS * KEYS_TILE, width), 0) >> 4
    col = lax.broadcasted_iota(jnp.int32, (HEADS * KEYS_TILE, width), 1) >> 6
    return jnp.where(row == col, 1.0, 0.0).astype(BF16)


def run_block(
    tokens, grad_output, valid_tiles, master_a, master_b, vector_params, order, la, ra, lb, rb
):
    width = tokens.shape[2]
    hidden = master_b.shape[0]
    rows = tokens.shape[1]
    per = rows // SLOTS
    grids = tokens.shape[0] * per
    flags = valid_tiles.reshape(grids, TILES)
    blocks = order.shape[0]
    per_block = -(-VECTOR_ROWS // blocks)
    total = (master_a.size + master_b.size) // LANES
    tall_block = -(-(total // blocks + per_block) // 32) * 32
    flip = pl.BlockSpec((1, width, rows), lambda g: (g // per, 0, 0))
    tall = (SLOTS, width)
    keys = (KEYS, width)
    scratch = [((width, width), BF16)] * 4 + [
        ((width + 16, hidden), BF16),
        ((hidden, width), BF16),
        ((hidden, width), BF16),
        ((16, hidden), F32),
        ((64, 64), BF16),
        ((HEADS * KEYS_TILE, width), BF16),
    ]
    scratch += [((width, width), F32)] * 4 + [
        ((width + 16, hidden), F32),
        ((width, hidden), F32),
        ((width, hidden), F32),
        ((16, width), F32),
        ((16, hidden), F32),
        (master_a.shape, F32),
        (master_b.shape, F32),
        None,
        ((rows, width), BF16),
        ((rows, width), BF16),
        ((rows, width), BF16),
        ((rows, width), F32),
        ((16, hidden), jnp.int32),
        ((hidden, hidden), BF16),
        ((2 * width, hidden), F32),
        ((total // 2, LANES), F32),
    ]
    scratch += [
        (tall, F32),
        (tall, F32),
        (tall, F32),
        ((SLOTS, 1), F32),
        (tall, BF16),
        (tall, BF16),
        (tall, BF16),
        ((KEYS, hidden), BF16),
        (keys, BF16),
        (keys, F32),
        ((KEYS, 1), F32),
        (keys, BF16),
        (keys, BF16),
        ((TILES * HEADS * KEYS_TILE, 64), F32),
        (tall, BF16),
        (tall, F32),
        (tall, F32),
        (tall, F32),
        ((SLOTS, 1), F32),
        ((SLOTS, width + 16), BF16),
        ((3, width, 192), BF16),
        ((3, width + 16, 192), BF16),
        ((88, hidden), F32),
        ((192, 256), F32),
        ((192, 256), F32),
        ((192, 256), BF16),
        ((192, 256), BF16),
        ((192, 256), F32),
        ((192, 256), F32),
        ((192, 256), BF16),
        ((192, 256), BF16),
        ((192, 256), F32),
        ((192, 256), F32),
        ((192, 256), BF16),
        ((192, 256), BF16),
        (tall, BF16),
        (tall, BF16),
        (tall, BF16),
        (tall, BF16),
        (keys, BF16),
        (keys, BF16),
        ((KEYS, hidden), BF16),
    ]
    smem = pl.BlockSpec(memory_space=pltpu.SMEM)
    anywhere = pl.BlockSpec(memory_space=pl.ANY)

    def whole(shape):
        return pl.BlockSpec(shape, lambda g: (0,) * len(shape), pipeline_mode=pl.Buffered(1))

    small = (vector_params, la, ra.reshape(-1, LANES), lb, rb.reshape(-1, LANES))
    out, gin, wire = pl.pallas_call(
        functools.partial(block_kernel, per=per, per_block=per_block),
        name="block_step",
        grid=(grids,),
        in_specs=[smem, smem, flip, flip, anywhere, anywhere] + [whole(c.shape) for c in small],
        out_specs=[flip, flip, whole((blocks, tall_block, LANES))],
        out_shape=[
            jax.ShapeDtypeStruct((tokens.shape[0], width, rows), BF16),
            jax.ShapeDtypeStruct((tokens.shape[0], width, rows), F32),
            jax.ShapeDtypeStruct((blocks, tall_block, LANES), BF16),
        ],
        scratch_shapes=[
            pltpu.SemaphoreType.DMA((2,)) if item is None else pltpu.VMEM(*item)
            for item in scratch
        ],
        compiler_params=pltpu.CompilerParams(vmem_limit_bytes=67_000_000),
    )(
        flags,
        order,
        jnp.transpose(tokens, (0, 2, 1)),
        jnp.transpose(grad_output, (0, 2, 1)),
        master_a,
        master_b,
        *small,
    )
    return jnp.transpose(out, (0, 2, 1)), jnp.transpose(gin, (0, 2, 1)), wire

SPANS_A = ((0, 1), (1, 2), (3, 1), (4, 4))
VECTOR_ROWS = 143


def fill_codes(la, ra, lb, rb, codes, width):
    hidden = lb.shape[1]
    codes[...] = jnp.full(codes.shape, -2, jnp.int32)
    right_a = jnp.concatenate([ra[j : j + 1, :] for j in range(ra.shape[0])], axis=1)
    right_b = jnp.concatenate([rb[j : j + 1, :] for j in range(rb.shape[0])], axis=1)
    codes[0:4, 0:width] = la[...]
    codes[4:6, 0:hidden] = lb[...]
    for k, (first, count) in enumerate(SPANS_A):
        start = first * width
        span = count * width
        codes[6 + k : 7 + k, 0:span] = right_a[:, start : start + span] - 2 * start
    for k in range(2):
        codes[10 + k : 11 + k, 0:width] = right_b[:, k * width : (k + 1) * width] - 2 * k * width


def lane_matrix(codes, k, size):
    code = codes[k : k + 1, 0:size]
    sign = (1 - 2 * (code & 1)).astype(F32)
    spot = lax.broadcasted_iota(jnp.int32, (size, size), 0)
    return jnp.where(spot == (code >> 1), sign, 0.0).astype(BF16)


def row_matrix(codes, k, out, size):
    for start in range(0, size, LANES):
        code = codes[k : k + 1, start : start + LANES]
        spot = jnp.transpose(jnp.broadcast_to((code >> 1).astype(F32), (LANES, LANES)))
        sign = jnp.transpose(
            jnp.broadcast_to((1 - 2 * (code & 1)).astype(F32), (LANES, LANES))
        )
        for col in range(0, size, LANES):
            lane = lax.broadcasted_iota(jnp.int32, (LANES, LANES), 1).astype(F32) + col
            part = jnp.where(spot == lane, sign, 0.0).astype(BF16)
            out[start : start + LANES, col : col + LANES] = part


def vector_spots(width, hidden):
    spots = []
    for k in range(11):
        for col in range(0, width, LANES):
            spots.append((0, k, col, min(LANES, width - col)))
    for k in range(11):
        for col in range(0, hidden, LANES):
            spots.append((1, k, col, LANES))
    return spots


def restore_kernel(
    blocks, order, la, ra, lb, rb, steps, ma, mb, vp, vf, vsec, owned, first, second,
    na, nb, ca, cb, vg, vfn, vsn, nv, grad, first_new, second_new,
    codes, rows_m, das, dbs, flat, wide_s, mas, mbs, cas, cbs, sbt, sems, per_block,
):
    width = ma.shape[0]
    hidden = mb.shape[0]
    load_a = pltpu.make_async_copy(ma, mas, sems.at[0])
    load_b = pltpu.make_async_copy(mb, mbs, sems.at[1])
    load_a.start()
    load_b.start()
    fill_codes(la, ra, lb, rb, codes, width)
    count = blocks.shape[0]
    depth = flat.shape[0] // count

    def place(t, carry):
        flat[pl.ds(order[t] * depth, depth), :] = blocks[t, 0:depth, :].astype(F32)
        return carry

    lax.fori_loop(0, count, place, 0)
    per_row = ma.shape[1] // LANES
    for j in range(per_row):
        cols = slice(j * LANES, (j + 1) * LANES)
        das[:, cols] = flat[pl.ds(j, width, stride=per_row), :].astype(BF16)
    base = width * per_row
    per_row = mb.shape[1] // LANES
    for j in range(per_row):
        rows = slice(j * LANES, (j + 1) * LANES)
        dbs[rows, :] = jnp.transpose(flat[pl.ds(base + j, hidden, stride=per_row), :]).astype(BF16)

    def dot(left, right):
        return jnp.dot(left, right, preferred_element_type=F32)

    def update(master, step, copy, rows, cols):
        old = master[rows, cols]
        value = old - matrix_rate * (step + weight_decay * old)
        master[rows, cols] = value
        copy[rows, cols] = value.astype(BF16)

    stores = []

    def send(source, target, rows):
        copy = pltpu.make_async_copy(
            source.at[rows, :], target.at[rows, :], sems.at[2 + len(stores)]
        )
        copy.start()
        stores.append(copy)

    load_a.wait()
    for k, (start, span) in enumerate(SPANS_A):
        size = span * width
        cols = slice(start * width, start * width + size)
        part = dot(lane_matrix(codes, k, width), das[:, cols]).astype(BF16)
        row_matrix(codes, 6 + k, rows_m, size)
        update(mas, dot(part, rows_m[0:size, 0:size]), cas, slice(None), cols)
    send(mas, na, slice(0, width))
    send(cas, ca, slice(0, width))
    for k in range(2):
        rows = slice(k * width, (k + 1) * width)
        part = dot(lane_matrix(codes, 10 + k, width), dbs[rows, :]).astype(BF16)
        row_matrix(codes, 4 + k, rows_m, hidden)
        sbt[rows, :] = dot(part, rows_m[...])
    load_b.wait()
    for c in range(hidden // 256):
        rows = slice(c * 256, (c + 1) * 256)
        for j in range(per_row):
            cols = slice(j * LANES, (j + 1) * LANES)
            update(mbs, jnp.transpose(sbt[cols, rows]), cbs, rows, cols)
        send(mbs, nb, rows)
        send(cbs, cb, rows)
    total = owned[...]
    grad[...] = total
    first_new[...] = beta_one * first[...] + (1.0 - beta_one) * total
    second_new[...] = beta_two * second[...] + (1.0 - beta_two) * total * total
    for number, (kind, k, col, size) in enumerate(vector_spots(width, hidden)):
        block, row = number // per_block, depth + number % per_block
        value = blocks[block, row : row + 1, 0:size].astype(F32)
        if kind == 0:
            vg[k : k + 1, col : col + size] = value
        else:
            wide_s[k : k + 1, col : col + size] = value
    ratio = hidden // width
    for k in range(11):
        for q in range(ratio):
            row = 11 + ratio * k + q
            vg[row : row + 1, :] = wide_s[k : k + 1, q * width : (q + 1) * width]
    grad = vg[...]
    first_new = beta_one * vf[...] + (1.0 - beta_one) * grad
    second_new = beta_two * vsec[...] + (1.0 - beta_two) * grad * grad
    vfn[...] = first_new
    vsn[...] = second_new
    move = direction_of(first_new, second_new, steps[0])
    old = vp[...]
    nv[...] = old - vector_rate * (move + weight_decay * old)
    for copy in stores:
        copy.wait()


def direction_of(first_new, second_new, steps):
    count = jnp.full((1, LANES), steps, jnp.int32).astype(F32)
    log_one = -0.10536051565782628
    log_two = -0.0010005003335835335
    one = (1.0 / (1.0 - jnp.exp(count * log_one)))[:, 0:1]
    two = (1.0 / (1.0 - jnp.exp(count * log_two)))[:, 0:1]
    return first_new * one / (jnp.sqrt(second_new * two) + adam_epsilon)


def vmem_spec():
    return pl.BlockSpec(memory_space=pltpu.VMEM)


def restore_blocks(
    blocks, order, la, ra, lb, rb, steps, ma, mb, vp, vf, vsec, owned, first, second
):
    width = ma.shape[0]
    hidden = mb.shape[0]
    per_block = -(-VECTOR_ROWS // blocks.shape[0])
    total = (ma.size + mb.size) // LANES
    smem = pl.BlockSpec(memory_space=pltpu.SMEM)
    anywhere = pl.BlockSpec(memory_space=pl.ANY)
    return pl.pallas_call(
        functools.partial(restore_kernel, per_block=per_block),
        name="restore",
        in_specs=[vmem_spec(), smem]
        + [vmem_spec()] * 4
        + [smem]
        + [anywhere] * 2
        + [vmem_spec()] * 6,
        out_specs=[anywhere] * 4 + [vmem_spec()] * 7,
        out_shape=[
            jax.ShapeDtypeStruct(ma.shape, F32),
            jax.ShapeDtypeStruct(mb.shape, F32),
            jax.ShapeDtypeStruct(ma.shape, BF16),
            jax.ShapeDtypeStruct(mb.shape, BF16),
        ]
        + [jax.ShapeDtypeStruct(vp.shape, F32)] * 4
        + [jax.ShapeDtypeStruct(owned.shape, F32)] * 3,
        scratch_shapes=[
            pltpu.VMEM((16, hidden), jnp.int32),
            pltpu.VMEM((hidden, hidden), BF16),
            pltpu.VMEM(ma.shape, BF16),
            pltpu.VMEM((2 * width, hidden), BF16),
            pltpu.VMEM((total, LANES), F32),
            pltpu.VMEM((16, hidden), F32),
            pltpu.VMEM(ma.shape, F32),
            pltpu.VMEM(mb.shape, F32),
            pltpu.VMEM(ma.shape, BF16),
            pltpu.VMEM(mb.shape, BF16),
            pltpu.VMEM((2 * width, hidden), F32),
            pltpu.SemaphoreType.DMA((4 + 2 * (hidden // 256),)),
        ],
        compiler_params=pltpu.CompilerParams(vmem_limit_bytes=60 << 20),
    )(
        blocks, order, la, ra.reshape(-1, LANES), lb, rb.reshape(-1, LANES), steps,
        ma, mb, vp, vf, vsec, owned, first, second,
    )


def exchange_kernel(wire, first, second, steps, grad, every, *scratch,
                    plan, bits, depth):
    buffers = []
    spot = 0
    for _, _, order in plan:
        buffers.append(scratch[spot : spot + len(order)])
        spot += len(order)
    keeps = scratch[spot : spot + len(plan)]
    rs_send, rs_recv, ag_send, ag_recv, local_sem = scratch[spot + len(plan) :]
    tok = lax.axis_index("tok")
    side = lax.axis_index("ch")

    def mine(axis):
        return side if axis == "ch" else lax.rem(lax.div(tok, 2**axis), 2)

    def peer(axis):
        if axis == "ch":
            return {"ch": 1 - side}
        return {"tok": tok + 2**axis - 2 ** (axis + 1) * mine(axis)}

    axes = [*reversed(range(bits)), "ch"]
    loads = []
    for c, (start, size, order) in enumerate(plan):
        index = tuple(mine(a) if a == order[0] else slice(None) for a in axes)
        copy = pltpu.make_async_copy(
            wire.at[index + (pl.ds(start, size), slice(None))], keeps[c], local_sem.at[c]
        )
        copy.start()
        loads.append(copy)
    barrier = pltpu.get_barrier_semaphore()
    for axis in axes:
        pl.semaphore_signal(barrier, inc=1, device_id=peer(axis), device_id_type=pl.DeviceIdType.MESH)
    pl.semaphore_wait(barrier, len(axes))

    chunks = range(len(plan))
    left = [list(axes) for _ in chunks]
    held = [wire for _ in chunks]
    pending = []

    def region(c, choice):
        index = tuple(choice(axis) for axis in left[c])
        start, size, _ = plan[c]
        rows = pl.ds(start, size) if held[c] is wire else slice(None)
        return index + (rows, slice(None))

    def scatter_start(c, s):
        axis = plan[c][2][s]
        index = region(c, lambda a: 1 - mine(a) if a == axis else slice(None))
        copy = pltpu.make_async_remote_copy(
            held[c].at[index], buffers[c][s], rs_send.at[c, s], rs_recv.at[c, s],
            device_id=peer(axis), device_id_type=pl.DeviceIdType.MESH,
        )
        copy.start()
        pending.append(copy)
        return copy

    def scatter_keep(c, s):
        if s == 0:
            loads[c].wait()
            return keeps[c][...]
        axis = plan[c][2][s]
        return held[c][region(c, lambda a: mine(a) if a == axis else slice(None))]

    def gather_start(c, s):
        start, size, order = plan[c]
        axis = order[len(order) - 1 - s]
        done = order[len(order) - s :]
        index = tuple(slice(None) if a in done else mine(a) for a in axes)
        piece = every.at[index + (pl.ds(start, size), slice(None))]
        copy = pltpu.make_async_remote_copy(
            piece, piece, ag_send.at[c, s], ag_recv.at[c, s],
            device_id=peer(axis), device_id_type=pl.DeviceIdType.MESH,
        )
        copy.start()
        pending.append(copy)
        return copy

    stages = len(axes)
    flying = [scatter_start(c, 0) for c in chunks]
    for s in range(stages):
        for c in chunks:
            start, size, order = plan[c]
            flying[c].wait_recv()
            kept = scatter_keep(c, s)
            buffer = buffers[c][s]
            if s < stages - 1:
                buffer[...] = buffer[...] + kept
                left[c].remove(order[s])
                held[c] = buffer
                flying[c] = scatter_start(c, s + 1)
                continue
            total = buffer[...].astype(F32) + kept.astype(F32)
            count = max(0, min(depth - start, size))
            parts = []
            if count:
                rows = slice(start, start + count)
                owned = total[:count]
                grad[rows, :] = owned
                one = beta_one * first[rows, :] + (1.0 - beta_one) * owned
                two = beta_two * second[rows, :] + (1.0 - beta_two) * owned * owned
                parts.append(direction_of(one, two, steps[0]))
            if count < size:
                parts.append(total[count:])
            ready = parts[0] if len(parts) == 1 else jnp.concatenate(parts, axis=0)
            own = tuple(mine(a) for a in axes)
            every[own + (slice(start, start + size), slice(None))] = ready.astype(BF16)
            flying[c] = gather_start(c, 0)
    for s in range(stages):
        for c in chunks:
            flying[c].wait_recv()
            if s < stages - 1:
                flying[c] = gather_start(c, s + 1)
    for copy in pending:
        copy.wait_send()


def exchange_blocks(wire, first, second, steps, bits):
    units = wire.shape[1] // 16
    each = -(-units // 9)
    rest = list(range(2, bits))
    orders = ([0] + rest + ["ch", 1], [0, "ch", 1] + rest, [0, 1, "ch"] + rest)
    plan = []
    for number, start in enumerate(range(0, units, each)):
        size = min(each, units - start)
        plan.append((start * 16, size * 16, orders[number % 3]))
    return exchange_plan(wire, first, second, steps, bits, plan)


def exchange_plan(wire, first, second, steps, bits, plan):
    count, tall, _ = wire.shape
    depth = first.shape[0]
    scratch = []
    for _, size, order in plan:
        for s in range(len(order)):
            scratch.append(pltpu.VMEM((2,) * (len(order) - 1 - s) + (size, LANES), BF16))
    for _, size, order in plan:
        scratch.append(pltpu.VMEM((2,) * (len(order) - 1) + (size, LANES), BF16))
    for _ in range(4):
        scratch.append(pltpu.SemaphoreType.DMA((len(plan), bits + 1)))
    scratch.append(pltpu.SemaphoreType.DMA((len(plan),)))
    shape = (2,) * (bits + 1) + (tall, LANES)
    block = jax.ShapeDtypeStruct((depth, LANES), F32)
    grad, every = pl.pallas_call(
        functools.partial(exchange_kernel, plan=plan, bits=bits, depth=depth),
        name="exchange",
        in_specs=[pl.BlockSpec(memory_space=pl.ANY)]
        + [vmem_spec()] * 2
        + [pl.BlockSpec(memory_space=pltpu.SMEM)],
        out_specs=[vmem_spec()] * 2,
        out_shape=[block, jax.ShapeDtypeStruct(shape, BF16)],
        scratch_shapes=scratch,
        compiler_params=pltpu.CompilerParams(
            vmem_limit_bytes=60 << 20, collective_id=0, has_side_effects=True
        ),
    )(wire.reshape(shape), first, second, steps)
    return grad, every.reshape(wire.shape)


def on_device(
    tokens, grad_output, valid_tiles, master_a, master_b, vector_params, matrix_first,
    matrix_second, vector_first, vector_second, left_a, right_a, left_b, right_b,
    owner_list, step_count, bits,
):
    out, grad_in, wire = run_block(
        tokens, grad_output, valid_tiles, master_a, master_b, vector_params, owner_list,
        left_a, right_a, left_b, right_b,
    )
    shape = matrix_first.shape
    first = matrix_first.reshape(-1, LANES)
    second = matrix_second.reshape(-1, LANES)
    owned, every = exchange_blocks(wire, first, second, step_count, bits)
    *restored, grad, first_new, second_new = restore_blocks(
        every, owner_list, left_a, right_a, left_b, right_b, step_count, master_a, master_b,
        vector_params, vector_first, vector_second, owned, first, second,
    )
    return (
        out,
        grad_in,
        grad.reshape(shape),
        first_new.reshape(shape),
        second_new.reshape(shape),
        *restored,
    )


def solution(mesh):
    bits = mesh.shape["tok"].bit_length() - 1
    part = P(None, ("tok", "ch"), None)
    owned = P(("tok", "ch"), None)
    in_specs = (part,) * 3 + (P(),) * 3 + (owned,) * 2 + (P(),) * 8
    out_specs = (part,) * 2 + (owned,) * 3 + (P(),) * 8
    return jax.shard_map(
        functools.partial(on_device, bits=bits), mesh=mesh, in_specs=in_specs, out_specs=out_specs, check_vma=False
    )
```
